32 devices in a mesh: blk: 16 (over z, y, core), tp: 2 (over x).
Axes of the slice: x: 2, y: 2, z: 4, core: 2. Of those that a mesh axis runs over, the one named last changes fastest.
Arguments:
- layer_input: bfloat16 [25088, 768], P('blk', 'tp'), may hold values from -6 to 6
- first_gain: float32 [768], replicated, may hold values from 0.5 to 1.5
- first_shift: float32 [768], replicated, may hold values from -0.5 to 0.5
- project_weight: bfloat16 [768, 3, 768], P(None, None, 'tp'), may hold values from -0.21875 to 0.21875
- project_bias: float32 [3, 768], P(None, 'tp'), may hold values from -0.5 to 0.5
- pool_taps: float32 [3, 27, 768], P(None, None, 'tp'), may hold values from -0.35 to 0.35
- memory_taps: float32 [2, 4, 768], P(None, None, 'tp'), may hold values from -0.85 to 0.85
- position_bias: float32 [8, 45], P('tp'), may hold values from -0.85 to 0.85
- output_weight: bfloat16 [768, 768], P('tp'), may hold values from -0.21875 to 0.21875
- output_bias: float32 [768], P('tp'), may hold values from -0.5 to 0.5
- second_gain: float32 [768], replicated, may hold values from 0.5 to 1.5
- second_shift: float32 [768], replicated, may hold values from -0.5 to 0.5
- expand_weight: bfloat16 [768, 3072], P(None, 'tp'), may hold values from -0.21875 to 0.21875
- expand_bias: float32 [3072], P('tp'), may hold values from -0.5 to 0.5
- reduce_weight: bfloat16 [3072, 768], P('tp'), may hold values from -0.109375 to 0.109375
- reduce_bias: float32 [768], P('tp'), may hold values from -0.5 to 0.5
- cotangent: bfloat16 [25088, 768], P('blk', 'tp'), may hold values from -6 to 6
- clip_place: int32 [64], P('blk'), may hold values from 0 to 11, as said below
Outputs:
- layer_output: bfloat16 [25088, 768], P('blk', 'tp')
- input_grad: float32 [25088, 768], P('blk', 'tp')
- first_gain_grad: float32 [768], replicated
- first_shift_grad: float32 [768], replicated
- project_weight_grad: float32 [768, 3, 768], P(None, None, 'tp')
- project_bias_grad: float32 [3, 768], P(None, 'tp')
- pool_taps_grad: float32 [3, 27, 768], P(None, None, 'tp')
- memory_taps_grad: float32 [2, 4, 768], P(None, None, 'tp')
- position_bias_grad: float32 [8, 45], P('tp')
- output_weight_grad: float32 [768, 768], P('tp')
- output_bias_grad: float32 [768], P('tp')
- second_gain_grad: float32 [768], replicated
- second_shift_grad: float32 [768], replicated
- expand_weight_grad: float32 [768, 3072], P(None, 'tp')
- expand_bias_grad: float32 [3072], P('tp')
- reduce_weight_grad: float32 [3072, 768], P('tp')
- reduce_bias_grad: float32 [768], P('tp')
The draws below stay inside these ranges and needn't reach their ends.
Inputs may be any that keep to these rules, and one draw needn't show every extreme that they name: clip_place[c] is clip c's place in its video counted from 0; videos of 1 to 12 clips follow one another, the first at clip 0, so clip_place[c] = clip_place[c - 1] + 1 wherever clip_place[c] > 0.
All inputs are finite; a program needn't handle non-finite values.
Results may differ from the reference program's by a relative error of at most 0.012.
Values may be sent and summed in bfloat16 or wider, within the bound.
A program may use at most 512 MiB of HBM per device.

```python
import jax
import jax.numpy as jnp
from jax import lax

D = 768
HEADS = 8
HEAD_DIM = 96
FF = 3072
CT = 8
CS = 7
MEMT = 2
DEPTH = 2
KC = 4
KT = 12
NT = 19
NHW = 13
NREL = 45
CLIP_TOK = 392
KEYS = 588
CLIPS = 64
TOKENS = 25088


def draw_clip_place(key, part):
    key_length = jax.random.fold_in(key, 11)
    key_choose = jax.random.fold_in(key, 12)
    lengths = jax.random.randint(key_length, (CLIPS,), 1, 13)
    chosen = jax.random.randint(key_choose, (), 0, 2)
    lengths = jnp.where(jnp.arange(CLIPS) == chosen, 12, lengths)
    ending = jnp.cumsum(lengths)
    starting = ending - lengths
    position = jnp.arange(CLIPS)
    began = jnp.where(starting[None, :] <= position[:, None], starting[None, :], 0)
    return (position - jnp.max(began, axis=1)).astype(jnp.int32)


def shard_levels(stream_key, shape, split, low, high):
    def one(dim, shards_of):
        steps = jax.random.uniform(jax.random.fold_in(jax.random.fold_in(stream_key, 6), dim), (shards_of,), jnp.float32, low / len(split), high / len(split))
        return jnp.repeat(jnp.exp(steps), shape[dim] // shards_of).reshape((-1,) + (1,) * (len(shape) - dim - 1))

    loudness = one(*split[0])
    for cut in split[1:]:
        loudness = loudness * one(*cut)
    return loudness


def noise(rng, shape, deviation, limit, split=(), kind=jnp.bfloat16):
    array = deviation * jax.random.normal(rng, shape, jnp.float32)
    if split:
        array = array * shard_levels(rng, shape, split, -0.22, 0.18)
    return jnp.clip(array, -limit, limit).astype(kind)


def setup_inputs(seed: int = 0) -> dict:
    key_list = jax.random.split(jax.random.key(seed), 19)
    layer_input = noise(key_list[0], (TOKENS, D), 1.0, 6.0, ((0, 16), (1, 2)))
    first_gain = jnp.clip(1.0 + 0.1 * jax.random.normal(key_list[1], (D,), jnp.float32), 0.5, 1.5)
    first_shift = jnp.clip(jax.random.uniform(key_list[2], (D,), jnp.float32, -0.5, 0.5), -0.5, 0.5)
    project_weight = noise(key_list[3], (D, 3, D), D ** -0.5, 0.21875, ((2, 2),))
    project_bias = jnp.clip(jax.random.uniform(key_list[4], (3, D), jnp.float32, -0.5, 0.5) * shard_levels(key_list[4], (3, D), ((1, 2),), -0.4, 0.0), -0.5, 0.5)
    pool_taps = jnp.clip(jax.random.uniform(key_list[5], (3, 27, D), jnp.float32, -0.35, 0.35) * shard_levels(key_list[5], (3, 27, D), ((2, 2),), -0.4, 0.0), -0.35, 0.35)
    memory_taps = jnp.clip(jax.random.uniform(key_list[6], (2, KC, D), jnp.float32, -0.85, 0.85) * shard_levels(key_list[6], (2, KC, D), ((2, 2),), -0.4, 0.0), -0.85, 0.85)
    position_bias = jnp.clip(jax.random.uniform(key_list[7], (HEADS, NREL), jnp.float32, -0.85, 0.85) * shard_levels(key_list[7], (HEADS, NREL), ((0, 2),), -0.4, 0.0), -0.85, 0.85)
    output_weight = noise(key_list[8], (D, D), D ** -0.5, 0.21875, ((0, 2),))
    output_bias = jnp.clip(jax.random.uniform(key_list[9], (D,), jnp.float32, -0.5, 0.5) * shard_levels(key_list[9], (D,), ((0, 2),), -0.4, 0.0), -0.5, 0.5)
    second_gain = jnp.clip(1.0 + 0.1 * jax.random.normal(key_list[10], (D,), jnp.float32), 0.5, 1.5)
    second_shift = jnp.clip(jax.random.uniform(key_list[11], (D,), jnp.float32, -0.5, 0.5), -0.5, 0.5)
    expand_weight = noise(key_list[12], (D, FF), D ** -0.5, 0.21875, ((1, 2),))
    expand_bias = jnp.clip(jax.random.uniform(key_list[13], (FF,), jnp.float32, -0.5, 0.5) * shard_levels(key_list[13], (FF,), ((0, 2),), -0.4, 0.0), -0.5, 0.5)
    reduce_weight = noise(key_list[14], (FF, D), FF ** -0.5, 0.109375, ((0, 2),))
    reduce_bias = jnp.clip(jax.random.uniform(key_list[15], (D,), jnp.float32, -0.5, 0.5) * shard_levels(key_list[15], (D,), ((0, 2),), -0.4, 0.0), -0.5, 0.5)
    cotangent = noise(key_list[16], (TOKENS, D), 1.0, 6.0, ((0, 16), (1, 2)))
    clip_place = draw_clip_place(jax.random.fold_in(key_list[18], 71), 0)
    return {"layer_input": layer_input, "first_gain": first_gain, "first_shift": first_shift, "project_weight": project_weight, "project_bias": project_bias, "pool_taps": pool_taps, "memory_taps": memory_taps, "position_bias": position_bias, "output_weight": output_weight, "output_bias": output_bias, "second_gain": second_gain, "second_shift": second_shift, "expand_weight": expand_weight, "expand_bias": expand_bias, "reduce_weight": reduce_weight, "reduce_bias": reduce_bias, "cotangent": cotangent, "clip_place": clip_place}


EPS = 1e-06
HIGH = lax.Precision.HIGHEST

@jax.custom_vjp
def low(v):
    return lax.optimization_barrier(v.astype(jnp.bfloat16)).astype(jnp.float32)

@jax.custom_vjp
def low_back(v):
    return v

def low_keep(v):
    return (low(v), None)

def low_pass(kept, grad):
    return (grad,)

def back_keep(v):
    return (v, None)

def back_low(kept, grad):
    return (low(grad),)
low.defvjp(low_keep, low_pass)
low_back.defvjp(back_keep, back_low)

def layer_norm(values, norm_gain, norm_shift):
    row_mean = lax.optimization_barrier(jnp.mean(values, axis=-1, keepdims=True))
    centred = values - row_mean
    spread = lax.optimization_barrier(jnp.mean(centred * centred, axis=-1, keepdims=True))
    return centred * lax.rsqrt(spread + EPS) * norm_gain + norm_shift

def exact_gelu(values):
    return jax.nn.gelu(values, approximate=False)

def pool_grid(grid_in, tap_weights):
    frames = grid_in.shape[1]
    extent = grid_in.shape[2]
    padded = jnp.pad(grid_in, ((0, 0), (1, 1), (1, 1), (1, 1), (0, 0), (0, 0)))
    summed = jnp.zeros(grid_in.shape, grid_in.dtype)
    for tap_index in range(27):
        along_time = tap_index // 9
        along_height = tap_index // 3 % 3
        along_width = tap_index % 3
        summed = summed + padded[:, along_time:along_time + frames, along_height:along_height + extent, along_width:along_width + extent] * tap_weights[tap_index]
    return summed

def compress(keyval, memory_taps):
    grouped = keyval.reshape(keyval.shape[0], MEMT, KC, CS, CS, 2, keyval.shape[-1])
    weights = jnp.transpose(memory_taps, (1, 0, 2))
    return lax.optimization_barrier(jnp.sum(grouped * weights[None, None, :, None, None, :, :], axis=2))

def bias_table(position_bias):
    head_total = position_bias.shape[0]
    query_time = jnp.arange(CT)[:, None]
    key_time = jnp.arange(KT)[None, :]
    time_index = jnp.where(key_time < CT, query_time - key_time + CT - 1, key_time + CT - 1)
    time_onehot = (time_index[:, :, None] == jnp.arange(NT)[None, None, :]).astype(position_bias.dtype)
    space_index = jnp.arange(CS)[:, None] - jnp.arange(CS)[None, :] + CS - 1
    space_onehot = (space_index[:, :, None] == jnp.arange(NHW)[None, None, :]).astype(position_bias.dtype)
    time_part = jnp.einsum('abr,hr->hab', time_onehot, position_bias[:, :NT], precision=HIGH)
    height_part = jnp.einsum('abr,hr->hab', space_onehot, position_bias[:, NT:NT + NHW], precision=HIGH)
    width_part = jnp.einsum('abr,hr->hab', space_onehot, position_bias[:, NT + NHW:], precision=HIGH)
    summed = time_part[:, :, None, None, :, None, None] + height_part[:, None, :, None, None, :, None] + width_part[:, None, None, :, None, None, :]
    return summed.reshape(head_total, CLIP_TOK, KEYS)

def key_usable(clip_place):
    key_time = jnp.arange(KEYS) // (CS * CS)
    needed = jnp.where(key_time < CT, 0, (key_time - CT) // MEMT + 1)
    return clip_place[:, None] >= needed[None, :]

def forward(inputs, first_gain, first_shift, project_weight, project_bias, pool_taps, memory_taps, position_bias, output_weight, output_bias, second_gain, second_shift, expand_weight, expand_bias, reduce_weight, reduce_bias, clip_place):
    score_scale = HEAD_DIM ** (-0.5)
    normed = low(layer_norm(inputs, first_gain, first_shift))
    project = jnp.einsum('rd,dif->rif', normed, project_weight, precision=HIGH) + project_bias
    project = low_back(project)
    head_grid = project.reshape(CLIPS, CT, CS, CS, 3, D)
    pooled = pool_grid(head_grid, jnp.transpose(pool_taps, (1, 0, 2)))
    queries = low(pooled[..., 0, :])
    keyval = low(pooled[..., 1:, :])
    memory = low(compress(pooled[..., 1:, :], memory_taps))
    key_parts = [keyval]
    for step_back in range(1, DEPTH + 1):
        key_parts.append(jnp.concatenate([jnp.zeros_like(memory[:step_back]), memory[:CLIPS - step_back]], axis=0))
    keys_all = jnp.concatenate(key_parts, axis=1).reshape(CLIPS, KEYS, 2, HEADS, HEAD_DIM)
    bias_full = bias_table(position_bias)
    usable = key_usable(clip_place)

    def attend(pieces):
        query_clip, keys_clip, usable_clip = pieces
        products = jnp.einsum('nhe,mhe->hnm', query_clip, keys_clip[:, 0], precision=HIGH) * score_scale + bias_full
        scores = low_back(jnp.where(usable_clip[None, None, :], products, -1e+30))
        largest = lax.optimization_barrier(jnp.max(scores, axis=-1, keepdims=True))
        exponent = jnp.exp(scores - largest)
        soft = exponent / lax.optimization_barrier(jnp.sum(exponent, axis=-1, keepdims=True))
        mixture = jnp.einsum('hnm,mhe->nhe', low(soft), keys_clip[:, 1], precision=HIGH)
        return low(low_back(mixture) + query_clip)
    heads_out = lax.map(jax.checkpoint(attend), (queries.reshape(CLIPS, CLIP_TOK, HEADS, HEAD_DIM), keys_all, usable))
    merged = heads_out.reshape(CLIPS * CLIP_TOK, D)
    update = low_back(jnp.dot(merged, output_weight, precision=HIGH) + output_bias)
    hidden = inputs + update
    normed_two = low(layer_norm(hidden, second_gain, second_shift))
    expand = low_back(jnp.dot(normed_two, expand_weight, precision=HIGH) + expand_bias)
    activated = low(exact_gelu(expand))
    branch = low_back(jnp.dot(activated, reduce_weight, precision=HIGH) + reduce_bias)
    return hidden + branch

def reference(layer_input, first_gain, first_shift, project_weight, project_bias, pool_taps, memory_taps, position_bias, output_weight, output_bias, second_gain, second_shift, expand_weight, expand_bias, reduce_weight, reduce_bias, cotangent, clip_place):

    def wrapped(*params):
        return forward(*params, clip_place)
    floats = (layer_input.astype(jnp.float32), first_gain, first_shift, project_weight.astype(jnp.float32), project_bias, pool_taps, memory_taps, position_bias, output_weight.astype(jnp.float32), output_bias, second_gain, second_shift, expand_weight.astype(jnp.float32), expand_bias, reduce_weight.astype(jnp.float32), reduce_bias)
    result, pullback = jax.vjp(wrapped, *floats)
    grads = pullback(cotangent.astype(jnp.float32))
    return (result.astype(jnp.bfloat16), grads[0], grads[1], grads[2], grads[3], grads[4], grads[5], grads[6], grads[7], grads[8], grads[9], grads[10], grads[11], grads[12], grads[13], grads[14], grads[15])
```

```python
import functools

import jax
import jax.numpy as jnp
import numpy as np
from jax import lax
from jax.experimental import pallas as pl
from jax.experimental.pallas import tpu as pltpu
from jax.sharding import PartitionSpec as P

HEAD_DIM = 96
CT = 8
CS = 7
KC = 4
KT = 12
NT = 19
NHW = 13
TOK = 392
PAD = 448
MROW = 112
KROWS = 672
EPS = 1e-06
SCALE = HEAD_DIM ** (-0.5)
LOG2E = 1.4426950408889634
EXP_SCALE = SCALE * LOG2E
NEG = -1e30
VMEM = 60 << 20
F32 = jnp.float32
BF16 = jnp.bfloat16

NT_DIMS = (((1,), (1,)), ((), ()))
TN_DIMS = (((0,), (0,)), ((), ()))


def mm(a, b):
    return jnp.dot(a, b, preferred_element_type=F32)


def mm_nt(a, b):
    return lax.dot_general(a, b, NT_DIMS, preferred_element_type=F32)


def mm_tn(a, b):
    return lax.dot_general(a, b, TN_DIMS, preferred_element_type=F32)


def iota(shape, dim):
    return lax.broadcasted_iota(jnp.int32, shape, dim)


def pad_matrix():
    row = iota((PAD, TOK), 0)
    col = iota((PAD, TOK), 1)
    x = lax.bitwise_and(row, 7)
    line = lax.shift_right_logical(row, 3)
    return jnp.where((x < CS) & (col == line * CS + x), 1.0, 0.0).astype(BF16)


def query_onehot():
    row = iota((PAD, 128), 0)
    col = iota((PAD, 128), 1)
    x = lax.bitwise_and(row, 7)
    line = lax.shift_right_logical(row, 3)
    t = lax.div(line, CS)
    y = line - t * CS
    c = lax.bitwise_and(col, 31)
    hit = (c == t) | (c == 8 + y) | ((c == 15 + x) & (x < CS))
    return jnp.where(hit & (col < 64), 1.0, 0.0).astype(BF16)


def key_onehot(dtype=BF16):
    row = iota((KROWS, 32), 0)
    col = iota((KROWS, 32), 1)
    x = lax.bitwise_and(row, 7)
    line = lax.shift_right_logical(row, 3)
    t = lax.div(line, CS)
    y = line - t * CS
    hit = (col == t) | (col == 12 + y) | ((col == 19 + x) & (x < CS))
    return jnp.where(hit, 1.0, 0.0).astype(dtype)


def key_mask(place):
    row = iota((KROWS, 32), 0)
    col = iota((KROWS, 32), 1)
    x = lax.bitwise_and(row, 7)
    need = jnp.where(row < PAD, 0, jnp.where(row < PAD + MROW, 1, 2))
    bad = (x == CS) | (place < need)
    return jnp.where(bad & (col == 0), NEG, 0.0).astype(BF16)


def one_column():
    return jnp.where(iota((PAD, 32), 1) == 0, 1.0, 0.0).astype(BF16)


def table_onehot():
    out = np.zeros((NT + 2 * NHW, 32, 32), np.float32)
    for t2 in range(KT):
        for t in range(CT):
            out[t - t2 + CT - 1 if t2 < CT else t2 + CT - 1, t2, t] = 1
    for a2 in range(CS):
        for a in range(CS):
            out[NT + a - a2 + CS - 1, 12 + a2, 8 + a] = 1
            out[NT + NHW + a - a2 + CS - 1, 19 + a2, 15 + a] = 1
    return out


def row_stats(x):
    mean = jnp.mean(x, axis=-1, keepdims=True)
    cen = x - mean
    var = jnp.mean(cen * cen, axis=-1, keepdims=True)
    return cen, lax.rsqrt(var + EPS)


def join_halves(dst, own, peer):
    me = lax.axis_index("tp")
    half = own.shape[-1]
    dst[:, pl.ds(pl.multiple_of(me * half, 128), half)] = own
    dst[:, pl.ds(pl.multiple_of((1 - me) * half, 128), half)] = peer


def col_sum(x):
    return jnp.sum(x, axis=0, keepdims=True)


def shifts_to(sh, grid4, by_left, by_right):
    flat = grid4.reshape(CT * CS, 8, 128)
    sh[0] = pltpu.roll(flat, by_left, 1).reshape(CT, CS, 8, 128)
    sh[1] = grid4
    sh[2] = pltpu.roll(flat, by_right, 1).reshape(CT, CS, 8, 128)


def pool_kernel(xo, xp, gain, shift, w, b, taps, mtaps, pool_o, proj_o, mem_o, x_o, xs, pr, sh, ps):
    join_halves(xs, xo[0], xp[0])
    xb = xs[...]
    x_o[0] = xb
    cen, r = row_stats(xb.astype(F32))
    normed = (cen * r * gain[...] + shift[...]).astype(BF16)
    npad = mm(pad_matrix(), normed).astype(BF16)
    valid = lax.bitwise_and(iota((PAD, 384), 0), 7) < CS
    for i in range(3):
        cols = slice(i * 384, i * 384 + 384)
        pr[:, cols] = jnp.where(valid, mm(npad, w[:, cols]) + b[:, cols], 0.0)
    proj_o[0] = pr[...].astype(BF16)
    keep = iota((CT, 8, 128), 1) < CS

    def group(gi, with_memory):
        lanes = pl.ds(pl.multiple_of(gi * 128, 128), 128)
        shifts_to(sh, pr[:, lanes].reshape(CT, CS, 8, 128), 1, 7)
        for y in range(CS):
            a0 = a1 = a2 = 0.0
            for bb in range(3):
                yy = y + bb - 1
                if not 0 <= yy < CS:
                    continue
                for e in range(3):
                    v = sh[e, :, yy]
                    k = 3 * bb + e
                    a0 = a0 + v[: CT - 1] * taps[k : k + 1, lanes]
                    a1 = a1 + v * taps[k + 9 : k + 10, lanes]
                    a2 = a2 + v[1:] * taps[k + 18 : k + 19, lanes]
            zero = jnp.zeros((1, 8, 128), F32)
            total = a1 + jnp.concatenate([zero, a0], 0) + jnp.concatenate([a2, zero], 0)
            ps[:, y] = jnp.where(keep, total, 0.0)
        pool_o[0, :, lanes] = ps[...].reshape(PAD, 128).astype(BF16)
        if with_memory:
            mlanes = pl.ds(pl.multiple_of((gi - 3) * 128, 128), 128)
            for s in range(2):
                m = 0.0
                for u in range(KC):
                    m = m + ps[s * KC + u] * mtaps[u : u + 1, mlanes]
                mem_o[0, s * 56 : s * 56 + 56, mlanes] = m.reshape(56, 128).astype(BF16)

    @pl.loop(0, 3)
    def _(gi):
        group(gi, False)

    @pl.loop(3, 9)
    def _(gi):
        group(gi, True)


def whole(shape):
    zeros = (0,) * len(shape)
    return pl.BlockSpec(shape, lambda c: zeros, pipeline_mode=pl.Buffered(1))


def per_clip(*shape):
    rest = (0,) * len(shape)
    return pl.BlockSpec((1,) + shape, lambda c: (c,) + rest)


def params(**kw):
    return pltpu.CompilerParams(vmem_limit_bytes=VMEM, **kw)


def cost(gflops, mbytes):
    return pl.CostEstimate(
        flops=int(gflops * 1e9), bytes_accessed=int(mbytes * 1e6), transcendentals=0
    )


def pool_call(xo, xp, gain, shift, w, b, taps, mtaps):
    clips = xo.shape[0]
    return pl.pallas_call(
        pool_kernel,
        grid=(clips,),
        in_specs=[
            per_clip(TOK, 384),
            per_clip(TOK, 384),
            whole((1, 768)),
            whole((1, 768)),
            whole((768, 1152)),
            whole((1, 1152)),
            whole((27, 1152)),
            whole((KC, 768)),
        ],
        out_specs=[
            per_clip(PAD, 1152),
            per_clip(PAD, 1152),
            per_clip(MROW, 768),
            per_clip(TOK, 768),
        ],
        out_shape=[
            jax.ShapeDtypeStruct((clips, PAD, 1152), BF16),
            jax.ShapeDtypeStruct((clips, PAD, 1152), BF16),
            jax.ShapeDtypeStruct((clips, MROW, 768), BF16),
            jax.ShapeDtypeStruct((clips, TOK, 768), BF16),
        ],
        scratch_shapes=[
            pltpu.VMEM((TOK, 768), BF16),
            pltpu.VMEM((PAD, 1152), F32),
            pltpu.VMEM((3, CT, CS, 8, 128), F32),
            pltpu.VMEM((CT, CS, 8, 128), F32),
        ],
        compiler_params=params(),
        cost_estimate=cost(4.5, 15),
        name="pool",
    )(xo, xp, gain, shift, w, b, taps, mtaps)


def gather_keys(kv, pool, m1, m2):
    kv[:PAD] = pool[0, :, 384:]
    kv[PAD : PAD + MROW] = m1[0]
    kv[PAD + MROW :] = m2[0]


def head_keys(kv, mask, tab, h):
    k = kv[:, h * HEAD_DIM : (h + 1) * HEAD_DIM]
    bias = mm(key_onehot(), tab[h]).astype(BF16)
    return jnp.concatenate([k, mask, bias], axis=1)


def head_queries(q, ones, onehot):
    return jnp.concatenate([q, ones, onehot], axis=1)


CHUNK = 48


def chunks():
    return [slice(j * CHUNK, j * CHUNK + CHUNK) for j in range(KROWS // CHUNK)]


def fold(x, op):
    return op(x.reshape(x.shape[0] // 8, 8, x.shape[1]), axis=0)


def attend_kernel(place, pool, m1, m2, tab, out_o, lse_o, kv, s_scr, p_scr, mix_t):
    gather_keys(kv, pool, m1, m2)
    mask = key_mask(place[pl.program_id(0)])
    ones = one_column()
    onehot = query_onehot()
    mix_t[:, PAD:] = jnp.zeros((384, 512 - PAD), F32)
    for h in range(4):
        feats = slice(h * HEAD_DIM, (h + 1) * HEAD_DIM)
        ka = head_keys(kv, mask, tab, h)
        qa = head_queries(pool[0, :, feats], ones, onehot)
        s_scr[...] = mm_nt(ka, qa)
        top = jnp.max(fold(s_scr[...], jnp.max), axis=0, keepdims=True) * EXP_SCALE
        total = 0.0
        for rows in chunks():
            p = jnp.exp2(s_scr[rows] * EXP_SCALE - top)
            total = total + fold(p, jnp.sum)
            p_scr[rows] = p.astype(BF16)
        total = jnp.sum(total, axis=0, keepdims=True)
        v = kv[:, 384 + h * HEAD_DIM : 384 + (h + 1) * HEAD_DIM]
        mix_t[feats, :PAD] = mm_tn(v, p_scr[...]) * (1.0 / total)
        lse_o[0, h : h + 1] = top + jnp.log2(total)
    mix = jnp.transpose(mix_t[...])[:PAD]
    merged = (mix + pool[0, :, :384].astype(F32)).astype(BF16)
    out_o[0] = mm_tn(pad_matrix(), merged).astype(BF16)


def attend_specs():
    return [
        pl.BlockSpec(memory_space=pltpu.SMEM),
        per_clip(PAD, 1152),
        pl.BlockSpec((1, MROW, 768), lambda c: (c + 1, 0, 0)),
        pl.BlockSpec((1, MROW, 768), lambda c: (c, 0, 0)),
        whole((4, 32, 128)),
    ]


def attend_call(place, pool, ext, tab):
    clips = pool.shape[0]
    return pl.pallas_call(
        attend_kernel,
        grid=(clips,),
        in_specs=attend_specs(),
        out_specs=[per_clip(TOK, 384), per_clip(4, PAD)],
        out_shape=[
            jax.ShapeDtypeStruct((clips, TOK, 384), BF16),
            jax.ShapeDtypeStruct((clips, 4, PAD), F32),
        ],
        scratch_shapes=[
            pltpu.VMEM((KROWS, 768), BF16),
            pltpu.VMEM((KROWS, PAD), F32),
            pltpu.VMEM((KROWS, PAD), BF16),
            pltpu.VMEM((384, 512), F32),
        ],
        compiler_params=params(),
        cost_estimate=cost(6, 10),
        name="attend",
    )(place, pool, ext, ext, tab)


FFC = 512


def phi_pair(x):
    ax = jnp.abs(x) * 0.7071067811865476
    t = 1.0 / (1.0 + 0.3275911 * ax)
    e = jnp.exp(-ax * ax)
    poly = 1.061405429 * t - 1.453152027
    poly = poly * t + 1.421413741
    poly = poly * t - 0.284496736
    poly = poly * t + 0.254829592
    tail = 0.5 * poly * t * e
    return jnp.where(x >= 0, 1.0 - tail, tail), e * 0.3989422804014327


def ff_kernel(
    mo, mp, x, co, cp, wo, wop, bo, g2, s2, we, be, wr, br,
    hid_o, res_o, bpeer_o, gn_o, cot_o, gwr_o, gwe_o, gbe_o,
    cs, nt_s, br_s, gn_s, gwr, gwe,
):
    c = pl.program_id(0)
    me = lax.axis_index("tp")
    half = mo.shape[-1]
    join_halves(cs, co[0], cp[0])
    cot_o[0] = cs[...]
    hid = x[0].astype(F32) + mm(mo[0], wo[...]) + mm(mp[0], wop[...]) + bo[...]
    hid_o[0] = hid
    cen, r = row_stats(hid)
    nt_s[...] = (cen * r * g2[...] + s2[...]).astype(BF16)

    @pl.when(c == 0)
    def _():
        gwr[...] = jnp.zeros_like(gwr)
        gwe[...] = jnp.zeros_like(gwe)
        gbe_o[...] = jnp.zeros_like(gbe_o)

    br_s[...] = jnp.zeros_like(br_s)
    gn_s[...] = jnp.zeros_like(gn_s)

    @pl.loop(0, we.shape[1] // FFC)
    def _(j):
        cols = pl.ds(pl.multiple_of(j * FFC, FFC), FFC)
        ex = mm(nt_s[...], we[:, cols]) + be[:, cols]
        cdf, pdf = phi_pair(ex)
        act = (ex * cdf).astype(BF16)
        br_s[...] += mm(act, wr[cols, :])
        ga = mm_nt(cs[...], wr[cols, :])
        ge32 = ga * (cdf + ex * pdf)
        ge = ge32.astype(BF16)
        gbe_o[:, cols] += col_sum(ge.astype(F32))
        gn_s[...] += mm_nt(ge, we[:, cols])
        gwr[cols, :] += mm_tn(act, cs[...])
        gwe[:, cols] += mm_tn(nt_s[...], ge)

    gn_o[0] = gn_s[...].astype(BF16)
    own = pl.ds(pl.multiple_of(me * half, 128), half)
    other = pl.ds(pl.multiple_of((1 - me) * half, 128), half)
    res_o[0] = hid_o[0, :, own] + br_s[:, own] + br[...]
    bpeer_o[0] = br_s[:, other].astype(BF16)

    @pl.when(c == pl.num_programs(0) - 1)
    def _():
        gwr_o[...] = gwr[...].astype(BF16)
        gwe_o[...] = gwe[...].astype(BF16)


def ff_call(mo, mp, x, co, cp, wo, wop, bo, g2, s2, we, be, wr, br):
    clips = mo.shape[0]
    ff = we.shape[1]
    return pl.pallas_call(
        ff_kernel,
        grid=(clips,),
        in_specs=[
            per_clip(TOK, 384),
            per_clip(TOK, 384),
            per_clip(TOK, 768),
            per_clip(TOK, 384),
            per_clip(TOK, 384),
            whole((384, 768)),
            whole((384, 768)),
            whole((1, 768)),
            whole((1, 768)),
            whole((1, 768)),
            whole((768, ff)),
            whole((1, ff)),
            whole((ff, 768)),
            whole((1, 384)),
        ],
        out_specs=[
            per_clip(TOK, 768),
            per_clip(TOK, 384),
            per_clip(TOK, 384),
            per_clip(TOK, 768),
            per_clip(TOK, 768),
            whole((ff, 768)),
            whole((768, ff)),
            whole((1, ff)),
        ],
        out_shape=[
            jax.ShapeDtypeStruct((clips, TOK, 768), F32),
            jax.ShapeDtypeStruct((clips, TOK, 384), F32),
            jax.ShapeDtypeStruct((clips, TOK, 384), BF16),
            jax.ShapeDtypeStruct((clips, TOK, 768), BF16),
            jax.ShapeDtypeStruct((clips, TOK, 768), BF16),
            jax.ShapeDtypeStruct((ff, 768), BF16),
            jax.ShapeDtypeStruct((768, ff), BF16),
            jax.ShapeDtypeStruct((1, ff), F32),
        ],
        scratch_shapes=[
            pltpu.VMEM((TOK, 768), BF16),
            pltpu.VMEM((TOK, 768), BF16),
            pltpu.VMEM((TOK, 768), F32),
            pltpu.VMEM((TOK, 768), F32),
            pltpu.VMEM((ff, 768), F32),
            pltpu.VMEM((768, ff), F32),
        ],
        compiler_params=params(),
        cost_estimate=cost(24, 40),
        name="feed",
    )(mo, mp, x, co, cp, wo, wop, bo, g2, s2, we, be, wr, br)


def unattend_kernel(
    place, pool, m1, m2, tab, lse, gno, gnp, hid, cot, mo, wo, g2,
    gp_o, gm_o, gh_o, dtab_o, gwo_o, gbo_o, gg_o, gs_o,
    kv, s_scr, d_scr, p_scr, ds_scr, dq_t, dkv, dl, gh_s,
):
    c = pl.program_id(0)
    me = lax.axis_index("tp")

    @pl.when(c == 0)
    def _():
        dl[...] = jnp.zeros_like(dl)
        gwo_o[...] = jnp.zeros_like(gwo_o)
        gbo_o[...] = jnp.zeros_like(gbo_o)
        gg_o[...] = jnp.zeros_like(gg_o)
        gs_o[...] = jnp.zeros_like(gs_o)

    gn = gno[0].astype(F32) + gnp[0].astype(F32)
    cen, r = row_stats(hid[0])
    xhat = cen * r
    gg_o[...] += col_sum(gn * xhat)
    gs_o[...] += col_sum(gn)
    g = gn * g2[...]
    mean_g = jnp.mean(g, axis=-1, keepdims=True)
    mean_gx = jnp.mean(g * xhat, axis=-1, keepdims=True)
    gh_s[...] = cot[0].astype(F32) + r * (g - mean_g - xhat * mean_gx)
    gh_o[0] = gh_s[:, pl.ds(pl.multiple_of(me * 384, 128), 384)]
    gu = gh_s[...].astype(BF16)
    gbo_o[...] += col_sum(gu.astype(F32))
    gwo_o[...] += mm_tn(mo[0], gu)
    gmerged = mm_nt(mm(pad_matrix(), gu).astype(BF16), wo[...])
    gmix = gmerged.astype(BF16)

    gather_keys(kv, pool, m1, m2)
    mask = key_mask(place[c])
    ones = one_column()
    onehot = query_onehot()
    dq_t[:, PAD:] = jnp.zeros((384, 512 - PAD), F32)
    for h in range(4):
        feats = slice(h * HEAD_DIM, (h + 1) * HEAD_DIM)
        vfeats = slice(384 + h * HEAD_DIM, 384 + (h + 1) * HEAD_DIM)
        ka = head_keys(kv, mask, tab, h)
        qa = head_queries(pool[0, :, feats], ones, onehot)
        gm = gmix[:, feats]
        s_scr[...] = mm_nt(ka, qa)
        d_scr[...] = mm_nt(kv[:, vfeats], gm)
        low = lse[0, h : h + 1]
        inner = 0.0
        for rows in chunks():
            p = jnp.exp2(s_scr[rows] * EXP_SCALE - low)
            s_scr[rows] = p
            p_scr[rows] = p.astype(BF16)
            inner = inner + fold(p * d_scr[rows], jnp.sum)
        inner = jnp.sum(inner, axis=0, keepdims=True)
        for rows in chunks():
            ds_scr[rows] = (s_scr[rows] * (d_scr[rows] - inner)).astype(BF16)
        ds = ds_scr[...]
        dkv[:, vfeats] = mm(p_scr[...], gm)
        dka = mm(ds, qa)
        dkv[:, feats] = dka[:, :HEAD_DIM] * SCALE
        dl[h] += dka[:, 128:]
        dq_t[feats, :PAD] = mm_tn(kv[:, feats], ds) * SCALE
    gp_o[0, :, :384] = (jnp.transpose(dq_t[...])[:PAD] + gmerged).astype(BF16)
    gp_o[0, :, 384:] = dkv[:PAD].astype(BF16)
    gm_o[0, 0] = dkv[PAD : PAD + MROW].astype(BF16)
    gm_o[0, 1] = dkv[PAD + MROW :].astype(BF16)

    @pl.when(c == pl.num_programs(0) - 1)
    def _():
        for h in range(4):
            dtab_o[h] = lax.dot_general(
                key_onehot(F32), dl[h], TN_DIMS,
                precision=lax.Precision.HIGHEST, preferred_element_type=F32,
            )


def unattend_call(place, pool, ext, tab, lse, gno, gnp, hid, cot, mo, wo, g2):
    clips = pool.shape[0]
    return pl.pallas_call(
        unattend_kernel,
        grid=(clips,),
        in_specs=attend_specs()
        + [
            per_clip(4, PAD),
            per_clip(TOK, 768),
            per_clip(TOK, 768),
            per_clip(TOK, 768),
            per_clip(TOK, 768),
            per_clip(TOK, 384),
            whole((384, 768)),
            whole((1, 768)),
        ],
        out_specs=[
            per_clip(PAD, 1152),
            per_clip(2, MROW, 768),
            per_clip(TOK, 384),
            whole((4, 32, 128)),
            whole((384, 768)),
            whole((1, 768)),
            whole((1, 768)),
            whole((1, 768)),
        ],
        out_shape=[
            jax.ShapeDtypeStruct((clips, PAD, 1152), BF16),
            jax.ShapeDtypeStruct((clips, 2, MROW, 768), BF16),
            jax.ShapeDtypeStruct((clips, TOK, 384), F32),
            jax.ShapeDtypeStruct((4, 32, 128), F32),
            jax.ShapeDtypeStruct((384, 768), F32),
            jax.ShapeDtypeStruct((1, 768), F32),
            jax.ShapeDtypeStruct((1, 768), F32),
            jax.ShapeDtypeStruct((1, 768), F32),
        ],
        scratch_shapes=[
            pltpu.VMEM((KROWS, 768), BF16),
            pltpu.VMEM((KROWS, PAD), F32),
            pltpu.VMEM((KROWS, PAD), F32),
            pltpu.VMEM((KROWS, PAD), BF16),
            pltpu.VMEM((KROWS, PAD), BF16),
            pltpu.VMEM((384, 512), F32),
            pltpu.VMEM((KROWS, 768), F32),
            pltpu.VMEM((4, KROWS, 128), F32),
            pltpu.VMEM((TOK, 768), F32),
        ],
        compiler_params=params(),
        cost_estimate=cost(18, 30),
        name="unattend",
    )(place, pool, ext, ext, tab, lse, gno, gnp, hid, cot, mo, wo, g2)


def unpool_kernel(
    gp, gmem, proj, pool, x, w, taps, mtaps, gain, shift,
    own_o, peer_o, sum_o, gw_o, gb_o, gt_o, gmt_o,
    gr, sh, ps, tg, gw,
):
    c = pl.program_id(0)
    me = lax.axis_index("tp")

    @pl.when(c == 0)
    def _():
        gw[...] = jnp.zeros_like(gw)
        gb_o[...] = jnp.zeros_like(gb_o)
        gt_o[...] = jnp.zeros_like(gt_o)
        gmt_o[...] = jnp.zeros_like(gmt_o)

    def group(gi, with_memory):
        lanes = pl.ds(pl.multiple_of(gi * 128, 128), 128)
        grad = gp[0, :, lanes].astype(F32).reshape(CT, CS, 8, 128)
        if with_memory:
            mlanes = pl.ds(pl.multiple_of((gi - 3) * 128, 128), 128)
            gm = gmem[0, :, mlanes].astype(F32).reshape(2, CS, 8, 128)
            pooled = pool[0, :, lanes].astype(F32).reshape(CT, CS, 8, 128)
            parts = []
            for u in range(KC):
                hit = gm[0] * pooled[u] + gm[1] * pooled[KC + u]
                gmt_o[u : u + 1, mlanes] += col_sum(jnp.sum(hit, axis=0))
            for t in range(CT):
                u = t % KC
                parts.append(grad[t] + gm[t // KC] * mtaps[u : u + 1, mlanes])
            grad = jnp.stack(parts, 0)
        shifts_to(sh, grad, 7, 1)
        ps[...] = proj[0, :, lanes].astype(F32).reshape(CT, CS, 8, 128)
        tg[...] = jnp.zeros_like(tg)
        for y in range(CS):
            a0 = a1 = a2 = 0.0
            pr = ps[:, y]
            for bb in range(3):
                yy = y + 1 - bb
                if not 0 <= yy < CS:
                    continue
                for e in range(3):
                    v = sh[e, :, yy]
                    k = 3 * bb + e
                    a0 = a0 + v[1:] * taps[k : k + 1, lanes]
                    a1 = a1 + v * taps[k + 9 : k + 10, lanes]
                    a2 = a2 + v[: CT - 1] * taps[k + 18 : k + 19, lanes]
                    tg[k] += jnp.sum(v[1:] * pr[: CT - 1], axis=0)
                    tg[k + 9] += jnp.sum(v * pr, axis=0)
                    tg[k + 18] += jnp.sum(v[: CT - 1] * pr[1:], axis=0)
            zero = jnp.zeros((1, 8, 128), F32)
            total = a1 + jnp.concatenate([a0, zero], 0) + jnp.concatenate([zero, a2], 0)
            sh[3, :, y] = total
        gr[:, lanes] = sh[3].reshape(PAD, 128).astype(BF16)
        gt_o[:, lanes] += jnp.sum(tg[...], axis=1)

    @pl.loop(0, 3)
    def _(gi):
        group(gi, False)

    @pl.loop(3, 9)
    def _(gi):
        group(gi, True)

    dense = mm_tn(pad_matrix(), gr[...]).astype(BF16)
    gb_o[...] += col_sum(dense.astype(F32))
    cen, r = row_stats(x[0].astype(F32))
    xhat = cen * r
    normed = (xhat * gain[...] + shift[...]).astype(BF16)
    gw[...] += mm_tn(normed, dense)
    gn = mm_nt(dense, w[...])
    g = gn * gain[...]
    first = jnp.sum(g, axis=-1, keepdims=True)
    second = jnp.sum(g * xhat, axis=-1, keepdims=True)
    lane = iota((TOK, 128), 1)
    sum_o[0] = jnp.where(lane == 0, first, jnp.where(lane == 1, second, 0.0))
    ps_own = pl.ds(pl.multiple_of(me * 384, 128), 384)
    ps_other = pl.ds(pl.multiple_of((1 - me) * 384, 128), 384)
    gn_s = sh_as_rows(gn)
    own_o[0], peer_o[0] = gn_s(ps_own, ps_other, me)

    @pl.when(c == pl.num_programs(0) - 1)
    def _():
        gw_o[...] = gw[...].astype(BF16)


def sh_as_rows(gn):
    def pick(own, other, me):
        left, right = gn[:, :384], gn[:, 384:]
        mine = jnp.where(me == 0, left, right)
        theirs = jnp.where(me == 0, right, left)
        return mine, theirs.astype(BF16)

    return pick


def unpool_call(gp, gmem, proj, pool, x, w, taps, mtaps, gain, shift):
    clips = gp.shape[0]
    return pl.pallas_call(
        unpool_kernel,
        grid=(clips,),
        in_specs=[
            per_clip(PAD, 1152),
            per_clip(MROW, 768),
            per_clip(PAD, 1152),
            per_clip(PAD, 1152),
            per_clip(TOK, 768),
            whole((768, 1152)),
            whole((27, 1152)),
            whole((KC, 768)),
            whole((1, 768)),
            whole((1, 768)),
        ],
        out_specs=[
            per_clip(TOK, 384),
            per_clip(TOK, 384),
            per_clip(TOK, 128),
            whole((768, 1152)),
            whole((1, 1152)),
            whole((27, 1152)),
            whole((KC, 768)),
        ],
        out_shape=[
            jax.ShapeDtypeStruct((clips, TOK, 384), F32),
            jax.ShapeDtypeStruct((clips, TOK, 384), BF16),
            jax.ShapeDtypeStruct((clips, TOK, 128), F32),
            jax.ShapeDtypeStruct((768, 1152), BF16),
            jax.ShapeDtypeStruct((1, 1152), F32),
            jax.ShapeDtypeStruct((27, 1152), F32),
            jax.ShapeDtypeStruct((KC, 768), F32),
        ],
        scratch_shapes=[
            pltpu.VMEM((PAD, 1152), BF16),
            pltpu.VMEM((4, CT, CS, 8, 128), F32),
            pltpu.VMEM((CT, CS, 8, 128), F32),
            pltpu.VMEM((27, 8, 128), F32),
            pltpu.VMEM((768, 1152), F32),
        ],
        compiler_params=params(),
        cost_estimate=cost(12, 25),
        name="unpool",
    )(gp, gmem, proj, pool, x, w, taps, mtaps, gain, shift)


def unnorm_kernel(own, recv, sums, sums_p, x, gh, gain, gin_o, gg_o, gs_o, xs):
    c = pl.program_id(0)
    me = lax.axis_index("tp")

    @pl.when(c == 0)
    def _():
        gg_o[...] = jnp.zeros_like(gg_o)
        gs_o[...] = jnp.zeros_like(gs_o)

    cen, r = row_stats(x[0].astype(F32))
    xs[...] = cen * r
    xhat = xs[:, pl.ds(pl.multiple_of(me * 384, 128), 384)]
    gn = own[0] + recv[0].astype(F32)
    total = (sums[0] + sums_p[0]) * (1.0 / 768)
    gain_own = gain[:, pl.ds(pl.multiple_of(me * 384, 128), 384)]
    gg_o[...] += col_sum(gn * xhat)
    gs_o[...] += col_sum(gn)
    gin_o[0] = gh[0] + r * (gn * gain_own - total[:, 0:1] - xhat * total[:, 1:2])


def unnorm_call(own, recv, sums, sums_p, x, gh, gain):
    clips = own.shape[0]
    return pl.pallas_call(
        unnorm_kernel,
        grid=(clips,),
        in_specs=[
            per_clip(TOK, 384),
            per_clip(TOK, 384),
            per_clip(TOK, 128),
            per_clip(TOK, 128),
            per_clip(TOK, 768),
            per_clip(TOK, 384),
            whole((1, 768)),
        ],
        out_specs=[per_clip(TOK, 384), whole((1, 384)), whole((1, 384))],
        out_shape=[
            jax.ShapeDtypeStruct((clips, TOK, 384), F32),
            jax.ShapeDtypeStruct((1, 384), F32),
            jax.ShapeDtypeStruct((1, 384), F32),
        ],
        scratch_shapes=[pltpu.VMEM((TOK, 768), F32)],
        compiler_params=params(),
        cost_estimate=cost(0.1, 15),
        name="unnorm",
    )(own, recv, sums, sums_p, x, gh, gain)


def swap(x):
    return lax.ppermute(x, "tp", [(0, 1), (1, 0)])


def move(x, by):
    peers = lax.axis_size("blk")
    return lax.ppermute(
        x, "blk", [(i, i + by) for i in range(peers) if 0 <= i + by < peers]
    )


def local(
    layer_input,
    first_gain,
    first_shift,
    project_weight,
    project_bias,
    pool_taps,
    memory_taps,
    position_bias,
    output_weight,
    output_bias,
    second_gain,
    second_shift,
    expand_weight,
    expand_bias,
    reduce_weight,
    reduce_bias,
    cotangent,
    clip_place,
):
    me = lax.axis_index("tp")
    clips = layer_input.shape[0] // TOK
    half = layer_input.shape[1]
    depth = 2

    def clipwise(a):
        return a.reshape(clips, TOK, a.shape[-1])

    def line(a):
        return a.reshape(1, -1)

    def in_order(own, peer):
        return jnp.where(
            me == 0, jnp.concatenate([own, peer], -1), jnp.concatenate([peer, own], -1)
        )

    xo = clipwise(layer_input)
    xp = swap(xo)
    co = clipwise(cotangent)
    w = project_weight.reshape(2 * half, 3 * half)
    taps = jnp.transpose(pool_taps, (1, 0, 2)).reshape(27, 3 * half)
    mtaps = jnp.transpose(memory_taps, (1, 0, 2)).reshape(KC, 2 * half)
    hot = jnp.asarray(table_onehot())
    table = jnp.einsum("he,ekc->hkc", position_bias, hot, precision=lax.Precision.HIGHEST)
    table = table * (HEAD_DIM**0.5)
    high = table.astype(BF16)
    low = (table - high.astype(F32)).astype(BF16)
    tab = jnp.concatenate([high, low, jnp.zeros_like(high), jnp.zeros_like(high)], axis=-1)
    gain1, shift1 = line(first_gain), line(first_shift)
    gain2, shift2 = line(second_gain), line(second_shift)

    pool, proj, mem, x = pool_call(
        xo, xp, gain1, shift1, w, line(project_bias), taps, mtaps
    )
    earlier = move(mem[clips - depth :], 1)
    cp = swap(co)
    wop = swap(output_weight)
    bo = in_order(output_bias, swap(output_bias))
    ext = jnp.concatenate([earlier, mem], axis=0)
    mo, lse = attend_call(clip_place, pool, ext, tab)
    mp = swap(mo)
    hid, res, bpeer, gno, cot, gwr, gwe, gbe = ff_call(
        mo, mp, x, co, cp, output_weight, wop, line(bo), gain2, shift2,
        expand_weight, line(expand_bias), reduce_weight, line(reduce_bias),
    )
    gnp = swap(gno)
    gwr, gwe = lax.psum((gwr, gwe), "blk")
    gp, gm, gh, dtab, gwo, gbo, gg2, gs2 = unattend_call(
        clip_place, pool, ext, tab, lse, gno, gnp, hid, cot, mo, output_weight, gain2
    )
    gm = gm.astype(F32)
    zero = jnp.zeros((1,) + gm.shape[2:], F32)
    one = jnp.concatenate([zero, gm[:, 0], zero[:0]], 0)
    two = jnp.concatenate([gm[:, 1], zero], 0)
    ext_grad = one + two
    ext_grad = jnp.concatenate([ext_grad, zero], 0)
    back = move(ext_grad[:depth].astype(BF16), -1).astype(F32)
    gmem = ext_grad[depth:] + jnp.concatenate(
        [jnp.zeros((clips - depth,) + back.shape[1:], F32), back], 0
    )
    own, peer, sums, gw, gb, gt, gmt = unpool_call(
        gp, gmem.astype(BF16), proj, pool, x, w, taps, mtaps, gain1, shift1
    )
    recv = swap(peer)
    bother = swap(bpeer)
    sums2 = jnp.transpose(sums[:, :, :2], (2, 0, 1)).reshape(2, clips * TOK)
    sums_p = jnp.transpose(swap(sums2).reshape(2, clips, TOK), (1, 2, 0))
    sums_p = jnp.pad(sums_p, ((0, 0), (0, 0), (0, 126)))
    gin, gg1, gs1 = unnorm_call(own, recv, sums, sums_p, x, gh, gain1)
    result = (res + bother.astype(F32)).astype(BF16).reshape(clips * TOK, half)

    gw, gwo = lax.psum((gw, gwo.astype(BF16)), "blk")
    grad_pos = jnp.einsum(
        "hkc,ekc->he", dtab[:, :, :32], hot, precision=lax.Precision.HIGHEST
    )
    blank = jnp.zeros((1, half), F32)
    gg1 = in_order(gg1, blank)
    gs1 = in_order(gs1, blank)
    gg1, gs1 = lax.psum((gg1, gs1), ("blk", "tp"))
    gbo = lax.dynamic_slice_in_dim(gbo, me * half, half, axis=1)
    cot_sum = col_sum(cotangent.astype(F32))
    gb, gt, gmt, grad_pos, gbo, gg2, gs2, gbe, cot_sum = lax.psum(
        (gb, gt, gmt, grad_pos, gbo, gg2, gs2, gbe, cot_sum), "blk"
    )
    return (
        result,
        gin.reshape(clips * TOK, half),
        gg1.reshape(-1),
        gs1.reshape(-1),
        gw.astype(F32).reshape(2 * half, 3, half),
        gb.reshape(3, half),
        jnp.transpose(gt.reshape(27, 3, half), (1, 0, 2)),
        jnp.transpose(gmt.reshape(KC, 2, half), (1, 0, 2)),
        grad_pos,
        gwo.astype(F32),
        gbo.reshape(-1),
        gg2.reshape(-1),
        gs2.reshape(-1),
        gwe.astype(F32),
        gbe.reshape(-1),
        gwr.astype(F32),
        cot_sum.reshape(-1),
    )


def solution(mesh):
    return jax.shard_map(
        local,
        mesh=mesh,
        in_specs=(
            P("blk", "tp"),
            P(),
            P(),
            P(None, None, "tp"),
            P(None, "tp"),
            P(None, None, "tp"),
            P(None, None, "tp"),
            P("tp", None),
            P("tp", None),
            P("tp"),
            P(),
            P(),
            P(None, "tp"),
            P("tp"),
            P("tp", None),
            P("tp"),
            P("blk", "tp"),
            P("blk"),
        ),
        out_specs=(
            P("blk", "tp"),
            P("blk", "tp"),
            P(),
            P(),
            P(None, None, "tp"),
            P(None, "tp"),
            P(None, None, "tp"),
            P(None, None, "tp"),
            P("tp", None),
            P("tp", None),
            P("tp"),
            P(),
            P(),
            P(None, "tp"),
            P("tp"),
            P("tp", None),
            P("tp"),
        ),
        check_vma=False,
    )
```

```python
import functools

import jax
import jax.numpy as jnp
import numpy as np
from jax import lax
from jax.experimental import pallas as pl
from jax.experimental.pallas import tpu as pltpu
from jax.sharding import PartitionSpec as P

HEAD_DIM = 96
CT = 8
CS = 7
KC = 4
KT = 12
NT = 19
NHW = 13
TOK = 392
PAD = 448
MROW = 112
KROWS = 672
EPS = 1e-06
SCALE = HEAD_DIM ** (-0.5)
LOG2E = 1.4426950408889634
EXP_SCALE = SCALE * LOG2E
NEG = -1e30
VMEM = 60 << 20
F32 = jnp.float32
BF16 = jnp.bfloat16

NT_DIMS = (((1,), (1,)), ((), ()))
TN_DIMS = (((0,), (0,)), ((), ()))


def mm(a, b):
    return jnp.dot(a, b, preferred_element_type=F32)


def mm_nt(a, b):
    return lax.dot_general(a, b, NT_DIMS, preferred_element_type=F32)


def mm_tn(a, b):
    return lax.dot_general(a, b, TN_DIMS, preferred_element_type=F32)


def iota(shape, dim):
    return lax.broadcasted_iota(jnp.int32, shape, dim)


def pad_matrix():
    row = iota((PAD, TOK), 0)
    col = iota((PAD, TOK), 1)
    x = lax.bitwise_and(row, 7)
    line = lax.shift_right_logical(row, 3)
    return jnp.where((x < CS) & (col == line * CS + x), 1.0, 0.0).astype(BF16)


def query_onehot():
    row = iota((PAD, 128), 0)
    col = iota((PAD, 128), 1)
    x = lax.bitwise_and(row, 7)
    line = lax.shift_right_logical(row, 3)
    t = lax.div(line, CS)
    y = line - t * CS
    c = lax.bitwise_and(col, 31)
    hit = (c == t) | (c == 8 + y) | ((c == 15 + x) & (x < CS))
    return jnp.where(hit & (col < 64), 1.0, 0.0).astype(BF16)


def key_onehot(dtype=BF16):
    row = iota((KROWS, 32), 0)
    col = iota((KROWS, 32), 1)
    x = lax.bitwise_and(row, 7)
    line = lax.shift_right_logical(row, 3)
    t = lax.div(line, CS)
    y = line - t * CS
    hit = (col == t) | (col == 12 + y) | ((col == 19 + x) & (x < CS))
    return jnp.where(hit, 1.0, 0.0).astype(dtype)


def key_mask(place):
    row = iota((KROWS, 32), 0)
    col = iota((KROWS, 32), 1)
    x = lax.bitwise_and(row, 7)
    need = jnp.where(row < PAD, 0, jnp.where(row < PAD + MROW, 1, 2))
    bad = (x == CS) | (place < need)
    return jnp.where(bad & (col == 0), NEG, 0.0).astype(BF16)


def one_column():
    return jnp.where(iota((PAD, 32), 1) == 0, 1.0, 0.0).astype(BF16)


def table_onehot():
    out = np.zeros((NT + 2 * NHW, 32, 128), np.float32)
    for t2 in range(KT):
        for t in range(CT):
            out[t - t2 + CT - 1 if t2 < CT else t2 + CT - 1, t2, t] = 1
    for a2 in range(CS):
        for a in range(CS):
            out[NT + a - a2 + CS - 1, 12 + a2, 8 + a] = 1
            out[NT + NHW + a - a2 + CS - 1, 19 + a2, 15 + a] = 1
    out[:, :, 32:64] = out[:, :, :32]
    return out


def bias_tables(pos, hot, tab_o):
    col = iota((32, 128), 1)
    for h in range(4):
        table = 0.0
        for e in range(NT + 2 * NHW):
            table = table + pos[h, e] * hot[e]
        table = table * (HEAD_DIM**0.5)
        high = table.astype(BF16)
        low = (table - high.astype(F32)).astype(BF16)
        tab_o[h] = jnp.where(col < 32, high, low)


def row_stats(x):
    mean = jnp.mean(x, axis=-1, keepdims=True)
    cen = x - mean
    var = jnp.mean(cen * cen, axis=-1, keepdims=True)
    return cen, lax.rsqrt(var + EPS)


def col_sum(x):
    return jnp.sum(x, axis=0, keepdims=True)


def as_row(ref):
    return ref[...].reshape(1, ref.shape[0])


def remote(src, dst, ssem, rsem, **where):
    return pltpu.make_async_remote_copy(
        src_ref=src, dst_ref=dst, send_sem=ssem, recv_sem=rsem,
        device_id=where, device_id_type=pl.DeviceIdType.MESH,
    )


def half_lanes(which):
    return pl.ds(pl.multiple_of(which * 384, 128), 384)


def peer_of(bit):
    blk = lax.axis_index("blk")
    mine = lax.rem(lax.div(blk, 1 << bit), 2)
    return mine, blk + (1 - 2 * mine) * (1 << bit)


def meet(bits=(), ring=False):
    barrier = pltpu.get_barrier_semaphore()
    blk = lax.axis_index("blk")
    peers = lax.axis_size("blk")
    others = [{"tp": 1 - lax.axis_index("tp")}] + [{"blk": peer_of(b)[1]} for b in bits]
    if ring:
        others += [{"blk": lax.rem(blk + by, peers)} for by in (1, peers - 1)]
    for other in others:
        pl.semaphore_signal(barrier, device_id=other, device_id_type=pl.DeviceIdType.MESH)
    pl.semaphore_wait(barrier, len(others))


def blk_bits():
    return lax.axis_size("blk").bit_length() - 1


def shifts_to(sh, grid4, by_left, by_right):
    flat = grid4.reshape(CT * CS, 8, 128)
    sh[0] = pltpu.roll(flat, by_left, 1).reshape(CT, CS, 8, 128)
    sh[1] = grid4
    sh[2] = pltpu.roll(flat, by_right, 1).reshape(CT, CS, 8, 128)


def pool_step(c, xb, gain, shift, w, b, taps, mtaps, pool_s, proj_o, ext_s, pr, sh, ps):
    cen, r = row_stats(xb.astype(F32))
    normed = (cen * r * as_row(gain) + as_row(shift)).astype(BF16)
    npad = mm(pad_matrix(), normed).astype(BF16)
    valid = lax.bitwise_and(iota((PAD, 384), 0), 7) < CS
    for i in range(3):
        cols = slice(i * 384, i * 384 + 384)
        pr[:, cols] = jnp.where(valid, mm(npad, w[i]) + b[i : i + 1], 0.0)
    proj_o[0] = pr[...].astype(BF16)
    keep = iota((CT, 8, 128), 1) < CS

    def group(gi, with_memory):
        lanes = pl.ds(pl.multiple_of(gi * 128, 128), 128)
        part = lax.div(gi, 3)
        sub = pl.ds(pl.multiple_of(lax.rem(gi, 3) * 128, 128), 128)
        shifts_to(sh, pr[:, lanes].reshape(CT, CS, 8, 128), 1, 7)
        for y in range(CS):
            a0 = a1 = a2 = 0.0
            for bb in range(3):
                yy = y + bb - 1
                if not 0 <= yy < CS:
                    continue
                for e in range(3):
                    v = sh[e, :, yy]
                    k = 3 * bb + e
                    a0 = a0 + v[: CT - 1] * taps[part, k : k + 1, sub]
                    a1 = a1 + v * taps[part, k + 9 : k + 10, sub]
                    a2 = a2 + v[1:] * taps[part, k + 18 : k + 19, sub]
            zero = jnp.zeros((1, 8, 128), F32)
            total = a1 + jnp.concatenate([zero, a0], 0) + jnp.concatenate([a2, zero], 0)
            ps[:, y] = jnp.where(keep, total, 0.0)
        pool_s[c, :, lanes] = ps[...].reshape(PAD, 128).astype(BF16)
        if with_memory:
            mlanes = pl.ds(pl.multiple_of((gi - 3) * 128, 128), 128)
            for s in range(2):
                m = 0.0
                for u in range(KC):
                    m = m + ps[s * KC + u] * mtaps[part - 1, u : u + 1, sub]
                ext_s[c + 2, s * 56 : s * 56 + 56, mlanes] = m.reshape(56, 128).astype(BF16)

    @pl.loop(0, 3)
    def _(gi):
        group(gi, False)

    @pl.loop(3, 9)
    def _(gi):
        group(gi, True)


def whole(shape):
    zeros = (0,) * len(shape)
    return pl.BlockSpec(shape, lambda c: zeros, pipeline_mode=pl.Buffered(1))


def per_clip(*shape):
    rest = (0,) * len(shape)
    return pl.BlockSpec((1,) + shape, lambda c: (c,) + rest)


def params(**kw):
    return pltpu.CompilerParams(vmem_limit_bytes=VMEM, **kw)


def cost(gflops, mbytes):
    return pl.CostEstimate(
        flops=int(gflops * 1e9), bytes_accessed=int(mbytes * 1e6), transcendentals=0
    )


def head_keys(kv, mask, tab, h):
    k = kv[:, h * HEAD_DIM : (h + 1) * HEAD_DIM]
    bias = mm(key_onehot(), tab[h]).astype(BF16)
    return jnp.concatenate([k, mask, bias], axis=1)


def head_queries(q, ones, onehot):
    return jnp.concatenate([q, ones, onehot], axis=1)


CHUNK = 48


def chunks():
    return [slice(j * CHUNK, j * CHUNK + CHUNK) for j in range(KROWS // CHUNK)]


def fold(x, op):
    return op(x.reshape(x.shape[0] // 8, 8, x.shape[1]), axis=0)


def attend_step(place, own, m1, m2, tab, lse_o, kv, s_scr, p_scr, mix_t):
    kv[:PAD] = own[:, 384:]
    kv[PAD : PAD + MROW] = m1[...]
    kv[PAD + MROW :] = m2[...]
    mask = key_mask(place)
    ones = one_column()
    onehot = query_onehot()
    mix_t[:, PAD:] = jnp.zeros((384, 512 - PAD), F32)
    for h in range(4):
        feats = slice(h * HEAD_DIM, (h + 1) * HEAD_DIM)
        ka = head_keys(kv, mask, tab, h)
        qa = head_queries(own[:, feats], ones, onehot)
        s_scr[...] = mm_nt(ka, qa)
        top = jnp.max(fold(s_scr[...], jnp.max), axis=0, keepdims=True) * EXP_SCALE
        total = 0.0
        for rows in chunks():
            p = jnp.exp2(s_scr[rows] * EXP_SCALE - top)
            total = total + fold(p, jnp.sum)
            p_scr[rows] = p.astype(BF16)
        total = jnp.sum(total, axis=0, keepdims=True)
        v = kv[:, 384 + h * HEAD_DIM : 384 + (h + 1) * HEAD_DIM]
        mix_t[feats, :PAD] = mm_tn(v, p_scr[...]) * (1.0 / total)
        lse_o[0, h : h + 1] = top + jnp.log2(total)
    mix = jnp.transpose(mix_t[...])[:PAD]
    merged = (mix + own[:, :384].astype(F32)).astype(BF16)
    return mm_tn(pad_matrix(), merged).astype(BF16)


FFC = 512


def phi_pair(x):
    ax = jnp.abs(x) * 0.7071067811865476
    t = 1.0 / (1.0 + 0.3275911 * ax)
    e = jnp.exp(-ax * ax)
    poly = 1.061405429 * t - 1.453152027
    poly = poly * t + 1.421413741
    poly = poly * t - 0.284496736
    poly = poly * t + 0.254829592
    tail = 0.5 * poly * t * e
    return jnp.where(x >= 0, 1.0 - tail, tail), e * 0.3989422804014327


def feed_step(hid, cot, g2, s2, we, be, wr, nt_s, br_s, gn_s, gwr, gwe, gbe_o):
    cen, r = row_stats(hid)
    nt_s[...] = (cen * r * as_row(g2) + as_row(s2)).astype(BF16)
    br_s[...] = jnp.zeros_like(br_s)
    gn_s[...] = jnp.zeros_like(gn_s)

    @pl.loop(0, we.shape[1] // FFC)
    def _(j):
        cols = pl.ds(pl.multiple_of(j * FFC, FFC), FFC)
        ex = mm(nt_s[...], we[:, cols]) + be[cols].reshape(1, FFC)
        cdf, pdf = phi_pair(ex)
        act = (ex * cdf).astype(BF16)
        br_s[...] += mm(act, wr[cols, :])
        ga = mm_nt(cot[...], wr[cols, :])
        ge = (ga * (cdf + ex * pdf)).astype(BF16)
        gbe_o[:, cols] += col_sum(ge.astype(F32))
        gn_s[...] += mm_nt(ge, we[:, cols])
        gwr[cols, :] += mm_tn(act, cot[...])
        gwe[:, cols] += mm_tn(nt_s[...], ge)


def pool_turn(s):
    return lax.rem(s + 2, 4)


def own_turn(s):
    return lax.rem(s + 2 * lax.axis_index("tp"), 4)


def other_turn(s):
    return lax.rem(s + 2 + 2 * lax.axis_index("tp"), 4)


def front_kernel(
    place, pos, x_h, cot_h, wo_h, bo, gain, shift, w, b, taps, mtaps, hot,
    wo, g2, s2, we, be, wr, br,
    pool_o, proj_o, x_o, ext_o, lse_o, wop_o, tab_o, mo_o, mp_o, hid_o, cot_o, gn_o, res_o,
    bpeer_o, gwr_o, gwe_o, gbe_o, gbr_o,
    xs, cs, pool_s, ext_s, mo_s, mp_s, wop_s, bo_s, pr, sh, ps, kv, s_scr, p_scr, mix_t,
    nt_s, br_s, gn_s, gnb, gnr, gwr, gwe,
    x_snd, x_rcv, x_loc, c_snd, c_rcv, c_loc, w_snd, w_rcv, e_snd, e_rcv,
    m_snd, m_rcv, g_snd, g_rcv, o_sem,
):
    step = pl.program_id(0)
    me = lax.axis_index("tp")
    blk = lax.axis_index("blk")
    peers = lax.axis_size("blk")
    core, mate = peer_of(0)
    mine, theirs = half_lanes(me), half_lanes(1 - me)

    def x_copy(c):
        return remote(x_h.at[c], xs.at[c, :, mine], x_snd.at[c], x_rcv.at[c], tp=1 - me)

    def x_local(c):
        return pltpu.make_async_copy(x_h.at[c], xs.at[c, :, mine], x_loc.at[c])

    def cot_copy(c):
        return remote(cot_h.at[c], cs.at[c, :, mine], c_snd.at[c], c_rcv.at[c], tp=1 - me)

    def cot_local(c):
        return pltpu.make_async_copy(cot_h.at[c], cs.at[c, :, mine], c_loc.at[c])

    weight_rows = pl.ds(pl.multiple_of(core * 192, 64), 192)

    def weight_copy():
        return remote(
            wo_h.at[weight_rows], wop_s.at[weight_rows], w_snd.at[0], w_rcv.at[0], tp=1 - me
        )

    def bias_copy():
        return remote(bo_s.at[:, mine], bo_s.at[:, mine], w_snd.at[1], w_rcv.at[1], tp=1 - me)

    def weight_share():
        rows = wop_s.at[weight_rows]
        return remote(rows, rows, w_snd.at[2], w_rcv.at[2], blk=mate)

    def memory_copy(j):
        return remote(
            ext_s.at[4 + j], ext_s.at[j], e_snd.at[j], e_rcv.at[j],
            blk=lax.rem(blk + 1, peers),
        )

    def merged_copy(c):
        return remote(mo_s.at[c], mp_s.at[c], m_snd.at[c], m_rcv.at[c], tp=1 - me)

    def grad_copy(j):
        return remote(gnb.at[j], gnr.at[j], g_snd.at[j], g_rcv.at[j], tp=1 - me)

    outs = [
        pltpu.make_async_copy(pool_s, pool_o, o_sem.at[0]),
        pltpu.make_async_copy(xs, x_o, o_sem.at[1]),
        pltpu.make_async_copy(ext_s, ext_o, o_sem.at[2]),
        pltpu.make_async_copy(wop_s, wop_o, o_sem.at[3]),
        pltpu.make_async_copy(cs, cot_o, o_sem.at[4]),
        pltpu.make_async_copy(mo_s, mo_o, o_sem.at[5]),
        pltpu.make_async_copy(mp_s, mp_o, o_sem.at[6]),
    ]

    @pl.when(step == 0)
    def _():
        meet(ring=True)
        for c in (2, 3, 0, 1):
            x_copy(c).start()
            x_local(c).start()
        bo_s[:, mine] = jnp.broadcast_to(as_row(bo), (8, 384))
        gwr[...] = jnp.zeros_like(gwr)
        gwe[...] = jnp.zeros_like(gwe)
        gbe_o[...] = jnp.zeros_like(gbe_o)
        gbr_o[...] = jnp.zeros_like(gbr_o)
        bias_tables(pos, hot, tab_o)

    @pl.when((step == 0) & (blk == 0))
    def _():
        ext_s[:2] = jnp.zeros((2, MROW, 768), BF16)

    @pl.when(step < 4)
    def _():
        c = pool_turn(step)
        x_local(c).wait()
        x_copy(c).wait_recv()

        @pl.when(step == 2)
        def _():
            weight_copy().start()
            bias_copy().start()

        @pl.when(step == 3)
        def _():
            cot_copy(own_turn(0)).start()
            for t in range(4):
                cot_local(t).start()

        pool_step(c, xs[c], gain, shift, w, b, taps, mtaps, pool_s, proj_o, ext_s, pr, sh, ps)

        @pl.when((step < 2) & (blk < peers - 1))
        def _():
            memory_copy(step).start()

        @pl.when(step == 3)
        def _():
            outs[0].start()
            outs[1].start()

    @pl.when((step >= 4) & (step < 8))
    def _():
        c = own_turn(step)

        @pl.when((step == 4) & (blk > 0))
        def _():
            memory_copy(0).wait_recv()
            memory_copy(1).wait_recv()

        @pl.when(step < 7)
        def _():
            cot_copy(own_turn(step + 1)).start()

        mo_s[c] = attend_step(
            place[c], pool_s.at[c], ext_s.at[c + 1], ext_s.at[c], tab_o, lse_o,
            kv, s_scr, p_scr, mix_t,
        )
        merged_copy(c).start()

        @pl.when(step == 5)
        def _():
            weight_copy().wait_recv()
            weight_share().start()

    @pl.when(step >= 8)
    def _():
        c = other_turn(step)

        @pl.when(step == 8)
        def _():
            weight_share().wait_recv()
            bias_copy().wait_recv()
            outs[2].start()
            outs[3].start()

        cot_local(c).wait()
        cot_copy(c).wait_recv()
        merged_copy(c).wait_recv()

        @pl.when(step == 11)
        def _():
            for t in outs[4:]:
                t.start()

        hid = xs[c].astype(F32) + mm(mo_s[c], wo[...]) + mm(mp_s[c], wop_s[...])
        hid = hid + bo_s[0:1, :]
        hid_o[0] = hid
        feed_step(hid, cs.at[c], g2, s2, we, be, wr, nt_s, br_s, gn_s, gwr, gwe, gbe_o)
        res_o[0] = hid_o[0, :, mine] + br_s[:, mine] + as_row(br)
        bpeer_o[0] = br_s[:, theirs].astype(BF16)
        gbr_o[...] += col_sum(cs[c, :, mine].astype(F32))

        @pl.when(step < 10)
        def _():
            gnb[step - 8] = gn_s[...].astype(BF16)
            grad_copy(step - 8).start()

        @pl.when(step >= 10)
        def _():
            grad_copy(step - 10).wait_recv()
            gn_o[0] = gn_s[...] + gnr[step - 10].astype(F32)

    @pl.when(step == 11)
    def _():
        gwr_o[...] = gwr[...].astype(BF16)
        gwe_o[...] = gwe[...].astype(BF16)
        for c in range(4):
            x_copy(c).wait_send()
            cot_copy(c).wait_send()
            merged_copy(c).wait_send()
        for t in (weight_copy(), bias_copy(), weight_share(), grad_copy(0), grad_copy(1)):
            t.wait_send()
        for t in outs:
            t.wait()

    @pl.when((step == 11) & (blk < peers - 1))
    def _():
        memory_copy(0).wait_send()
        memory_copy(1).wait_send()


HBM = pl.BlockSpec(memory_space=pl.ANY)
IN_SMEM = pl.BlockSpec(memory_space=pltpu.SMEM)
DMA = pltpu.SemaphoreType.DMA


def whole_like(*arrays):
    return [whole(a.shape) for a in arrays]


def front_call(place, pos, x, cot, wo, bo, gain, shift, w, b, taps, mtaps, hot, g2, s2, we, be, wr, br):
    ff = we.shape[1]

    def at(turn, low, high, *shape):
        rest = (0,) * len(shape)
        return pl.BlockSpec(
            (1,) + shape, lambda s: (turn(jnp.clip(s, low, high)),) + rest
        )

    def own(*shape):
        rest = (0,) * len(shape)
        return pl.BlockSpec((1,) + shape, lambda s: (jnp.maximum(s - 10, 0),) + rest)

    return pl.pallas_call(
        front_kernel,
        grid=(12,),
        in_specs=[IN_SMEM, IN_SMEM, HBM, HBM, HBM]
        + whole_like(bo, gain, shift, w, b, taps, mtaps, hot, wo, g2, s2, we, be, wr, br),
        out_specs=[
            HBM,
            at(pool_turn, 0, 3, PAD, 1152),
            HBM,
            HBM,
            at(own_turn, 4, 7, 4, PAD),
            HBM,
            whole((4, 32, 128)),
            HBM,
            HBM,
            own(TOK, 768),
            HBM,
            own(TOK, 768),
            at(other_turn, 8, 11, TOK, 384),
            at(other_turn, 8, 11, TOK, 384),
            whole((ff, 768)),
            whole((768, ff)),
            whole((1, ff)),
            whole((1, 384)),
        ],
        out_shape=[
            jax.ShapeDtypeStruct((4, PAD, 1152), BF16),
            jax.ShapeDtypeStruct((4, PAD, 1152), BF16),
            jax.ShapeDtypeStruct((4, TOK, 768), BF16),
            jax.ShapeDtypeStruct((6, MROW, 768), BF16),
            jax.ShapeDtypeStruct((4, 4, PAD), F32),
            jax.ShapeDtypeStruct((384, 768), BF16),
            jax.ShapeDtypeStruct((4, 32, 128), BF16),
            jax.ShapeDtypeStruct((4, TOK, 384), BF16),
            jax.ShapeDtypeStruct((4, TOK, 384), BF16),
            jax.ShapeDtypeStruct((2, TOK, 768), F32),
            jax.ShapeDtypeStruct((4, TOK, 768), BF16),
            jax.ShapeDtypeStruct((2, TOK, 768), F32),
            jax.ShapeDtypeStruct((4, TOK, 384), F32),
            jax.ShapeDtypeStruct((4, TOK, 384), BF16),
            jax.ShapeDtypeStruct((ff, 768), BF16),
            jax.ShapeDtypeStruct((768, ff), BF16),
            jax.ShapeDtypeStruct((1, ff), F32),
            jax.ShapeDtypeStruct((1, 384), F32),
        ],
        scratch_shapes=[
            pltpu.VMEM((4, TOK, 768), BF16),
            pltpu.VMEM((4, TOK, 768), BF16),
            pltpu.VMEM((4, PAD, 1152), BF16),
            pltpu.VMEM((6, MROW, 768), BF16),
            pltpu.VMEM((4, TOK, 384), BF16),
            pltpu.VMEM((4, TOK, 384), BF16),
            pltpu.VMEM((384, 768), BF16),
            pltpu.VMEM((8, 768), F32),
            pltpu.VMEM((PAD, 1152), F32),
            pltpu.VMEM((3, CT, CS, 8, 128), F32),
            pltpu.VMEM((CT, CS, 8, 128), F32),
            pltpu.VMEM((KROWS, 768), BF16),
            pltpu.VMEM((KROWS, PAD), F32),
            pltpu.VMEM((KROWS, PAD), BF16),
            pltpu.VMEM((384, 512), F32),
            pltpu.VMEM((TOK, 768), BF16),
            pltpu.VMEM((TOK, 768), F32),
            pltpu.VMEM((TOK, 768), F32),
            pltpu.VMEM((2, TOK, 768), BF16),
            pltpu.VMEM((2, TOK, 768), BF16),
            pltpu.VMEM((ff, 768), F32),
            pltpu.VMEM((768, ff), F32),
        ]
        + [DMA((4,))] * 6
        + [DMA((3,))] * 2
        + [DMA((2,))] * 2
        + [DMA((4,))] * 2
        + [DMA((2,))] * 2
        + [DMA((7,))],
        compiler_params=params(collective_id=1, has_side_effects=True),
        cost_estimate=cost(36, 60),
        name="front",
    )(place, pos, x, cot, wo, bo, gain, shift, w, b, taps, mtaps, hot, wo, g2, s2, we, be, wr, br)


def halvings(rows, bits):
    out = []
    for bit in range(bits):
        rows = rows // 2 if bit < 4 else rows
        out.append((bit, rows))
    return out


def slots(rows, bits):
    at, places = 0, []
    for _, n in halvings(rows, bits):
        places.append(at)
        at += n
    return at, places


class Halving:
    def __init__(self, src, keep, rcv, ssem, rsem, lsem):
        self.src, self.keep, self.rcv = src, keep, rcv
        self.ssem, self.rsem, self.lsem = ssem, rsem, lsem
        self.bits = blk_bits()
        self.rows = src.shape[0]
        self.list = halvings(self.rows, self.bits)
        self.places = slots(self.rows, self.bits)[1]

    def offset(self, r):
        off = 0
        for bit, n in self.list[1 : r + 1]:
            if bit < 4:
                off = off + peer_of(bit)[0] * n
        return off

    def span(self, at, n):
        return pl.ds(pl.multiple_of(at, 16), n)

    def copy(self, r):
        bit, n = self.list[r]
        mine, peer = peer_of(bit)
        if r == 0:
            src = self.src.at[self.span((1 - mine) * n, n)]
        else:
            away = self.offset(r - 1) + ((1 - mine) * n if bit < 4 else 0)
            src = self.keep.at[self.span(away, n)]
        dst = self.rcv.at[pl.ds(self.places[r], n)]
        return remote(src, dst, self.ssem.at[r], self.rsem.at[r], blk=peer)

    def load(self):
        n = self.list[0][1]
        src = self.src.at[self.span(peer_of(0)[0] * n, n)]
        return pltpu.make_async_copy(src, self.keep, self.lsem)

    def start(self, r):
        self.copy(r).start()
        if r == 0:
            self.load().start()

    def finish(self, r):
        if r == 0:
            self.load().wait()
        self.copy(r).wait()
        n = self.list[r][1]
        rows = self.span(self.offset(r), n)
        got = self.rcv[self.places[r] : self.places[r] + n]
        self.keep[rows] = (self.keep[rows].astype(F32) + got.astype(F32)).astype(BF16)

    def rest(self):
        for r in range(4, self.bits):
            self.start(r)
            self.finish(r)

    def piece(self):
        return self.keep[self.span(self.offset(3), self.list[3][1])]


class Doubling:
    def __init__(self, piece, out, ssem, rsem, lsem):
        self.piece, self.out = piece, out
        self.ssem, self.rsem, self.lsem = ssem, rsem, lsem
        self.rows = out.shape[0]

    def held(self, bit):
        at = 0
        for b in range(bit + 1):
            at = at + peer_of(b)[0] * (self.rows >> (b + 1))
        n = self.rows >> (bit + 1)
        return pl.ds(pl.multiple_of(at, 16), n)

    def load(self):
        return pltpu.make_async_copy(self.piece, self.out.at[self.held(3)], self.lsem)

    def copy(self, bit):
        rows = self.out.at[self.held(bit)]
        return remote(rows, rows, self.ssem.at[bit], self.rsem.at[bit], blk=peer_of(bit)[1])

    def start(self, bit):
        self.copy(bit).start()

    def finish(self, bit):
        self.copy(bit).wait()


def unattend_kernel(
    place, pool, m1, m2, tab, hot, lse, gn_i, hid, cot, mo, mp, wo, wop, g2, gwr_h, gwe_h, bp_h,
    gp_o, gext_o, gh_o, gwo_o, sums_o, pos_o, gwr_o, gwe_o, br_o,
    kv, s_scr, d_scr, p_scr, ds_scr, dq_t, dkv, dl, gwo_s, gwo_p, gwo_c, gwo_m, gwo_x, gwo_y,
    gms, gmb, gmr, gext, ka_s, kr_s, kb_s, ke_s,
    m_snd, m_rcv, w_snd, w_rcv, b_snd, b_rcv, fr_snd, fr_rcv, fe_snd, fe_rcv, f_loc,
):
    step = pl.program_id(0)
    me = lax.axis_index("tp")
    core, mate = peer_of(0)
    first = Halving(gwr_h, ka_s, kr_s, fr_snd, fr_rcv, f_loc.at[0])
    second = Halving(gwe_h, kb_s, ke_s, fe_snd, fe_rcv, f_loc.at[1])

    def merged_copy(j):
        return remote(gmb.at[j], gmr.at[j], m_snd.at[j], m_rcv.at[j], tp=1 - me)

    def weight_mate():
        return remote(gwo_c, gwo_m, w_snd.at[0], w_rcv.at[0], blk=mate)

    def weight_peer():
        return remote(gwo_x, gwo_y, w_snd.at[1], w_rcv.at[1], tp=1 - me)

    def branch_copy():
        return remote(bp_h, br_o, b_snd.at[0], b_rcv.at[0], tp=1 - me)

    @pl.when(step == 0)
    def _():
        meet(bits=range(blk_bits()))
        first.start(0)
        second.start(0)
        dl[...] = jnp.zeros_like(dl)
        gwo_s[...] = jnp.zeros_like(gwo_s)
        gwo_p[...] = jnp.zeros_like(gwo_p)
        sums_o[...] = jnp.zeros_like(sums_o)
        gext[...] = jnp.zeros_like(gext)

    @pl.when(step == 1)
    def _():
        first.finish(0)
        first.start(1)
        second.finish(0)
        second.start(1)

    @pl.when(step < 2)
    def _():
        gn = gn_i[0]
        cen, r = row_stats(hid[0])
        xhat = cen * r
        sums_o[2:3, :768] += col_sum(gn * xhat)
        sums_o[3:4, :768] += col_sum(gn)
        g = gn * as_row(g2)
        mean_g = jnp.mean(g, axis=-1, keepdims=True)
        mean_gx = jnp.mean(g * xhat, axis=-1, keepdims=True)
        gh_o[0] = cot[0].astype(F32) + r * (g - mean_g - xhat * mean_gx)
        gu = gh_o[0].astype(BF16)
        gmb[step] = mm_nt(gu, wop[...]).astype(BF16)
        merged_copy(step).start()
        gms[step] = mm_nt(gu, wo[...]).astype(BF16)
        sums_o[4:5, :768] += col_sum(gu.astype(F32))
        gwo_s[...] += mm_tn(mo[0], gu)
        gwo_p[...] += mm_tn(mp[0], gu)

    @pl.when(step == 1)
    def _():
        gwo_c[...] = gwo_p[:, half_lanes(1 - core)].astype(BF16)
        weight_mate().start()

    def hook(s, h):
        if (s, h) == (2, 1):
            weight_mate().wait()
            gwo_x[...] = (gwo_p[:, half_lanes(core)] + gwo_m[...].astype(F32)).astype(BF16)
            weight_peer().start()
            branch_copy().start()
        if (s, h) == (3, 0):
            first.finish(1)
            first.start(2)
        if (s, h) == (3, 3):
            first.finish(2)
            first.start(3)
        if (s, h) == (4, 1):
            second.finish(1)
            second.start(2)
        if (s, h) == (4, 2):
            first.finish(3)
        if (s, h) == (5, 0):
            second.finish(2)
            second.start(3)

    hooks = ((2, 1), (3, 0), (3, 3), (4, 1), (4, 2), (5, 0))

    def backward(gm_dense):
        c = own_turn(step - 2)
        gmerged = mm(pad_matrix(), gm_dense)
        gmix = gmerged.astype(BF16)
        kv[:PAD] = pool[0, :, 384:]
        kv[PAD : PAD + MROW] = m1[0]
        kv[PAD + MROW :] = m2[0]
        mask = key_mask(place[c])
        ones = one_column()
        onehot = query_onehot()
        dq_t[:, PAD:] = jnp.zeros((384, 512 - PAD), F32)
        for h in range(4):
            for s, at in hooks:
                if at == h:
                    pl.when(step == s)(functools.partial(hook, s, h))
            feats = slice(h * HEAD_DIM, (h + 1) * HEAD_DIM)
            vfeats = slice(384 + h * HEAD_DIM, 384 + (h + 1) * HEAD_DIM)
            ka = head_keys(kv, mask, tab, h)
            qa = head_queries(pool[0, :, feats], ones, onehot)
            gm = gmix[:, feats]
            s_scr[...] = mm_nt(ka, qa)
            d_scr[...] = mm_nt(kv[:, vfeats], gm)
            low = lse[0, h : h + 1]
            inner = 0.0
            for rows in chunks():
                p = jnp.exp2(s_scr[rows] * EXP_SCALE - low)
                s_scr[rows] = p
                p_scr[rows] = p.astype(BF16)
                inner = inner + fold(p * d_scr[rows], jnp.sum)
            inner = jnp.sum(inner, axis=0, keepdims=True)
            for rows in chunks():
                ds_scr[rows] = (s_scr[rows] * (d_scr[rows] - inner)).astype(BF16)
            ds = ds_scr[...]
            dkv[:, vfeats] = mm(p_scr[...], gm)
            dka = mm(ds, qa)
            dkv[:, feats] = dka[:, :HEAD_DIM] * SCALE
            dl[h] += dka[:, 128:]
            dq_t[feats, :PAD] = mm_tn(kv[:, feats], ds) * SCALE
        gp_o[0, :, :384] = (jnp.transpose(dq_t[...])[:PAD] + gmerged).astype(BF16)
        gp_o[0, :, 384:] = dkv[:PAD].astype(BF16)
        gext[c + 1] += dkv[PAD : PAD + MROW]
        gext[c] += dkv[PAD + MROW :]

    @pl.when(step >= 4)
    def _():
        merged_copy(step - 4).wait_recv()
        gms[step - 4] = gmr[step - 4]

    @pl.when(step >= 2)
    def _():
        backward(gms[lax.rem(step, 2)])

    @pl.when(step == 5)
    def _():
        gext_o[...] = gext[...].astype(BF16)
        weight_peer().wait()
        for j in range(2):
            merged_copy(j).wait_send()
        cols = half_lanes(core)
        gwo_s[:, cols] += gwo_y[...].astype(F32)
        gwo_o[:384] = gwo_s[:, :384].astype(BF16)
        gwo_o[384:] = gwo_s[:, 384:].astype(BF16)
        lane = iota((NT + 2 * NHW, 128), 1)
        keep = iota((32, 128), 1) < 32
        pos = jnp.zeros((NT + 2 * NHW, 128), F32)
        for h in range(4):
            dtab = lax.dot_general(
                key_onehot(F32), dl[h], TN_DIMS,
                precision=lax.Precision.HIGHEST, preferred_element_type=F32,
            )
            hits = jnp.sum(hot[...] * jnp.where(keep, dtab, 0.0)[None], axis=1)
            pos = jnp.where(lane == h, jnp.sum(hits, axis=-1, keepdims=True), pos)
        pos = jnp.concatenate([pos, jnp.zeros((128 - pos.shape[0], 128), F32)], 0)
        pos_o[...] = jnp.transpose(pos)[:8]
        second.finish(3)
        first.rest()
        second.rest()
        gwr_o[...] = first.piece()
        gwe_o[...] = second.piece()
        branch_copy().wait()


def unattend_call(
    place, pool, ext, tab, hot, lse, gn, hid, cot, mo, mp, wo, wop, g2, gwr, gwe, bpeer
):
    ff = gwe.shape[1]
    bits = blk_bits()

    def at(*shape, by=0):
        rest = (0,) * len(shape)
        return pl.BlockSpec(
            (1,) + shape, lambda s: (own_turn(jnp.maximum(s - 2, 0)) + by,) + rest
        )

    def own(*shape):
        rest = (0,) * len(shape)
        return pl.BlockSpec((1,) + shape, lambda s: (jnp.minimum(s, 1),) + rest)

    def clip(*shape):
        rest = (0,) * len(shape)
        return pl.BlockSpec((1,) + shape, lambda s: (own_turn(jnp.minimum(s, 1)),) + rest)

    return pl.pallas_call(
        unattend_kernel,
        grid=(6,),
        in_specs=[
            IN_SMEM,
            at(PAD, 1152),
            at(MROW, 768, by=1),
            at(MROW, 768),
            whole((4, 32, 128)),
            whole(hot.shape),
            at(4, PAD),
            own(TOK, 768),
            own(TOK, 768),
            clip(TOK, 768),
            clip(TOK, 384),
            clip(TOK, 384),
            whole((384, 768)),
            whole((384, 768)),
            whole((768,)),
            HBM,
            HBM,
            HBM,
        ],
        out_specs=[
            at(PAD, 1152),
            whole((6, MROW, 768)),
            own(TOK, 768),
            whole((768, 384)),
            whole((8, 1152)),
            whole((8, 128)),
            whole((ff // 16, 768)),
            whole((48, ff)),
            HBM,
        ],
        out_shape=[
            jax.ShapeDtypeStruct((4, PAD, 1152), BF16),
            jax.ShapeDtypeStruct((6, MROW, 768), BF16),
            jax.ShapeDtypeStruct((2, TOK, 768), F32),
            jax.ShapeDtypeStruct((768, 384), BF16),
            jax.ShapeDtypeStruct((8, 1152), F32),
            jax.ShapeDtypeStruct((8, 128), F32),
            jax.ShapeDtypeStruct((ff // 16, 768), BF16),
            jax.ShapeDtypeStruct((48, ff), BF16),
            jax.ShapeDtypeStruct(bpeer.shape, BF16),
        ],
        scratch_shapes=[
            pltpu.VMEM((KROWS, 768), BF16),
            pltpu.VMEM((KROWS, PAD), F32),
            pltpu.VMEM((KROWS, PAD), F32),
            pltpu.VMEM((KROWS, PAD), BF16),
            pltpu.VMEM((KROWS, PAD), BF16),
            pltpu.VMEM((384, 512), F32),
            pltpu.VMEM((KROWS, 768), F32),
            pltpu.VMEM((4, KROWS, 128), F32),
            pltpu.VMEM((384, 768), F32),
            pltpu.VMEM((384, 768), F32),
        ]
        + [pltpu.VMEM((384, 384), BF16)] * 4
        + [pltpu.VMEM((2, TOK, 384), BF16)] * 3
        + [
            pltpu.VMEM((6, MROW, 768), F32),
            pltpu.VMEM((ff // 2, 768), BF16),
            pltpu.VMEM((slots(ff, bits)[0], 768), BF16),
            pltpu.VMEM((384, ff), BF16),
            pltpu.VMEM((slots(768, bits)[0], ff), BF16),
        ]
        + [DMA((2,))] * 4
        + [DMA((1,))] * 2
        + [DMA((bits,))] * 4
        + [DMA((2,))],
        compiler_params=params(collective_id=2, has_side_effects=True),
        cost_estimate=cost(18, 30),
        name="unattend",
    )(
        place, pool, ext, ext, tab, hot, lse, gn, hid, cot, mo, mp, wo, wop, g2, gwr, gwe, bpeer
    )


def unpool_kernel(
    gp, gext, proj, pool, x, gh, w, taps, mtaps, gain, shift, gwr_h, gwe_h,
    own_o, recv_o, sum_o, sump_o, gw_o, small_o, norm_o, gwr_o, gwe_o,
    gr, sh, ps, tg, gw, rows_s, wcat, gm_s, back, z_s, peer_s,
    b_snd, b_rcv, n_snd, n_rcv, t_snd, t_rcv, fr_snd, fr_rcv, fe_snd, fe_rcv, f_loc,
):
    c = pl.program_id(0)
    me = lax.axis_index("tp")
    blk = lax.axis_index("blk")
    peers = lax.axis_size("blk")
    mine, theirs = half_lanes(me), half_lanes(1 - me)
    first = Doubling(gwr_h, gwr_o, fr_snd, fr_rcv, f_loc.at[0])
    second = Doubling(gwe_h, gwe_o, fe_snd, fe_rcv, f_loc.at[1])

    def back_copy(j):
        return remote(
            gext.at[j], back.at[j], b_snd.at[j], b_rcv.at[j],
            blk=lax.rem(blk + peers - 1, peers),
        )

    def norm_copy(i):
        return remote(peer_s.at[i], recv_o.at[i], n_snd.at[i], n_rcv.at[i], tp=1 - me)

    def sum_copy(i):
        return remote(sum_o.at[i], sump_o.at[i], t_snd.at[i], t_rcv.at[i], tp=1 - me)

    @pl.when(c == 0)
    def _():
        meet(bits=range(4), ring=True)
        first.load().start()
        second.load().start()
        first.load().wait()
        first.start(3)
        second.load().wait()
        second.start(3)
        gw[...] = jnp.zeros_like(gw)
        small_o[...] = jnp.zeros_like(small_o)
        norm_o[...] = jnp.zeros_like(norm_o)
        rows_s[...] = jnp.zeros_like(rows_s)
        for i in range(3):
            wcat[:, i * 384 : i * 384 + 384] = w[i]

    @pl.when((c == 0) & (blk > 0))
    def _():
        back_copy(0).start()
        back_copy(1).start()

    gm_s[...] = gext[c + 2].astype(F32)

    @pl.when((c >= 2) & (blk < peers - 1))
    def _():
        back_copy(c - 2).wait_recv()
        gm_s[...] += back[c - 2].astype(F32)

    def hook(s, g):
        if (s, g) == (0, 6):
            first.finish(3)
            first.start(2)
        if (s, g) == (1, 2):
            second.finish(3)
            second.start(2)
        if (s, g) == (1, 4):
            first.finish(2)
            first.start(1)
        if (s, g) == (1, 8):
            second.finish(2)
            second.start(1)
        if (s, g) == (2, 8):
            first.finish(1)
            first.start(0)
        if (s, g) == (3, 8):
            second.finish(1)
            second.start(0)

    hooks = ((0, 6), (1, 2), (1, 4), (1, 8), (2, 8), (3, 8))

    def group(gi, with_memory):
        for s, g in hooks:
            if (g > 2) == with_memory:
                pl.when((c == s) & (gi == g))(functools.partial(hook, s, g))
        lanes = pl.ds(pl.multiple_of(gi * 128, 128), 128)
        part = lax.div(gi, 3)
        sub = pl.ds(pl.multiple_of(lax.rem(gi, 3) * 128, 128), 128)
        grad = gp[0, :, lanes].astype(F32).reshape(CT, CS, 8, 128)
        if with_memory:
            mlanes = pl.ds(pl.multiple_of((gi - 3) * 128, 128), 128)
            gm = gm_s[:, mlanes].reshape(2, CS, 8, 128)
            pooled = pool[0, :, lanes].astype(F32).reshape(CT, CS, 8, 128)
            parts = []
            for u in range(KC):
                hit = gm[0] * pooled[u] + gm[1] * pooled[KC + u]
                small_o[28 + u : 29 + u, mlanes] += col_sum(jnp.sum(hit, axis=0))
            for t in range(CT):
                u = t % KC
                parts.append(grad[t] + gm[t // KC] * mtaps[part - 1, u : u + 1, sub])
            grad = jnp.stack(parts, 0)
        shifts_to(sh, grad, 7, 1)
        ps[...] = proj[0, :, lanes].astype(F32).reshape(CT, CS, 8, 128)
        tg[...] = jnp.zeros_like(tg)
        for y in range(CS):
            a0 = a1 = a2 = 0.0
            pr = ps[:, y]
            for bb in range(3):
                yy = y + 1 - bb
                if not 0 <= yy < CS:
                    continue
                for e in range(3):
                    v = sh[e, :, yy]
                    k = 3 * bb + e
                    a0 = a0 + v[1:] * taps[part, k : k + 1, sub]
                    a1 = a1 + v * taps[part, k + 9 : k + 10, sub]
                    a2 = a2 + v[: CT - 1] * taps[part, k + 18 : k + 19, sub]
                    tg[k] += jnp.sum(v[1:] * pr[: CT - 1], axis=0)
                    tg[k + 9] += jnp.sum(v * pr, axis=0)
                    tg[k + 18] += jnp.sum(v[: CT - 1] * pr[1:], axis=0)
            zero = jnp.zeros((1, 8, 128), F32)
            total = a1 + jnp.concatenate([a0, zero], 0) + jnp.concatenate([zero, a2], 0)
            sh[3, :, y] = total
        gr[:, lanes] = sh[3].reshape(PAD, 128).astype(BF16)
        small_o[:27, lanes] += jnp.sum(tg[...], axis=1)

    @pl.loop(0, 3)
    def _(gi):
        group(gi, False)

    @pl.loop(3, 9)
    def _(gi):
        group(gi, True)

    dense = mm_tn(pad_matrix(), gr[...]).astype(BF16)
    gn = mm_nt(dense, wcat[...])
    cen, r = row_stats(x[0].astype(F32))
    xhat = cen * r
    g = gn * as_row(gain)
    z_s[...] = r * g + jnp.where(lax.div(c, 2) == me, gh[0], 0.0)
    peer_s[c] = z_s[:, theirs].astype(BF16)
    norm_copy(c).start()
    own_o[0] = z_s[:, mine]
    first_sum = jnp.sum(g, axis=-1, keepdims=True)
    second_sum = jnp.sum(g * xhat, axis=-1, keepdims=True)
    lane = iota((TOK, 128), 1)
    rows_s[:TOK] = jnp.where(lane == 0, first_sum, jnp.where(lane == 1, second_sum, 0.0))
    sum_o[c] = jnp.transpose(rows_s[...])[:8]
    sum_copy(c).start()
    small_o[27:28] += col_sum(dense.astype(F32))
    norm_o[0:1, :768] += col_sum(gn * xhat)
    norm_o[1:2, :768] += col_sum(gn)
    normed = (xhat * as_row(gain) + as_row(shift)).astype(BF16)
    gw[...] += mm_tn(normed, dense)

    @pl.when(c == 3)
    def _():
        for i in range(3):
            gw_o[i] = gw[:, i * 384 : i * 384 + 384].astype(BF16)
        for i in range(4):
            norm_copy(i).wait()
            sum_copy(i).wait()
        first.finish(0)
        second.finish(0)

    @pl.when((c == 3) & (blk > 0))
    def _():
        back_copy(0).wait_send()
        back_copy(1).wait_send()


def unpool_call(gp, gext, proj, pool, x, gh, w, taps, mtaps, gain, shift, gwr, gwe):
    ff = gwe.shape[1]
    half_clip = pl.BlockSpec((1, TOK, 768), lambda c: (lax.rem(c, 2), 0, 0))
    return pl.pallas_call(
        unpool_kernel,
        grid=(4,),
        in_specs=[
            per_clip(PAD, 1152),
            whole((6, MROW, 768)),
            per_clip(PAD, 1152),
            per_clip(PAD, 1152),
            per_clip(TOK, 768),
            half_clip,
        ]
        + whole_like(w, taps, mtaps, gain, shift)
        + [HBM, HBM],
        out_specs=[
            per_clip(TOK, 384),
            HBM,
            whole((4, 8, 512)),
            HBM,
            whole((3, 768, 384)),
            whole((32, 1152)),
            whole((8, 1152)),
            HBM,
            HBM,
        ],
        out_shape=[
            jax.ShapeDtypeStruct((4, TOK, 384), F32),
            jax.ShapeDtypeStruct((4, TOK, 384), BF16),
            jax.ShapeDtypeStruct((4, 8, 512), F32),
            jax.ShapeDtypeStruct((4, 8, 512), F32),
            jax.ShapeDtypeStruct((3, 768, 384), BF16),
            jax.ShapeDtypeStruct((32, 1152), F32),
            jax.ShapeDtypeStruct((8, 1152), F32),
            jax.ShapeDtypeStruct((ff, 768), BF16),
            jax.ShapeDtypeStruct((768, ff), BF16),
        ],
        scratch_shapes=[
            pltpu.VMEM((PAD, 1152), BF16),
            pltpu.VMEM((4, CT, CS, 8, 128), F32),
            pltpu.VMEM((CT, CS, 8, 128), F32),
            pltpu.VMEM((27, 8, 128), F32),
            pltpu.VMEM((768, 1152), F32),
            pltpu.VMEM((512, 128), F32),
            pltpu.VMEM((768, 1152), BF16),
            pltpu.VMEM((MROW, 768), F32),
            pltpu.VMEM((2, MROW, 768), BF16),
            pltpu.VMEM((TOK, 768), F32),
            pltpu.VMEM((4, TOK, 384), BF16),
        ]
        + [DMA((2,))] * 2
        + [DMA((4,))] * 8
        + [DMA((2,))],
        compiler_params=params(collective_id=3, has_side_effects=True),
        cost_estimate=cost(12, 25),
        name="unpool",
    )(gp, gext, proj, pool, x, gh, w, taps, mtaps, gain, shift, gwr, gwe)


def final_kernel(
    own, recv, sums, sums_p, x, gain, res, br, red, redl, redr, gwr, gwe, small,
    gin_o, out_o, gw_o, gwo_o, gwr_o, gwe_o, gt_o, gb_o, gmt_o, pos_o,
    gbo_o, gg1_o, gs1_o, gg2_o, gs2_o, gbe_o, gbr_o,
    xs, rows_s,
):
    me = lax.axis_index("tp")
    mine = half_lanes(me)
    rows_s[8:] = jnp.zeros((120, 512), F32)
    rows_s[:8] = (sums[0] + sums_p[0]) * (1.0 / 768)
    total = jnp.transpose(rows_s[...])[:TOK]
    cen, r = row_stats(x[0].astype(F32))
    xs[...] = cen * (r * r)
    z = own[0] + recv[0].astype(F32)
    gin_o[0] = z - r * total[:, 0:1] - xs[:, mine] * total[:, 1:2]
    out_o[0] = (res[0] + br[0].astype(F32)).astype(BF16)
    gw_o[...] = red[...].astype(F32)
    gwo_o[:, :384] = redl[0].astype(F32)
    gwo_o[:, 384:] = redr[0].astype(F32)
    gwr_o[...] = gwr[...].astype(F32)
    gwe_o[...] = gwe[...].astype(F32)

    @pl.when(pl.program_id(0) == 3)
    def _():
        for i in range(3):
            cols = slice(i * 384, i * 384 + 384)
            gt_o[i] = small[:27, cols]
            gb_o[i : i + 1] = small[27:28, cols]
            if i < 2:
                gmt_o[i] = small[28:32, cols]
        pos_o[...] = small[40:44, : NT + 2 * NHW]
        gbo_o[...] = small[60:61, mine].reshape(384)
        for row, ref in ((56, gg1_o), (57, gs1_o), (58, gg2_o), (59, gs2_o)):
            ref[...] = small[row : row + 1, :768].reshape(768)
        half = gbe_o.shape[0] // 2
        gbe_o[:half] = small[32:33, :half].reshape(half)
        gbe_o[half:] = small[33:34, :half].reshape(half)
        gbr_o[...] = small[34:35, :384].reshape(384)


def final_call(own, recv, sums, sums_p, x, gain, res, br, red, gwr, gwe, small):
    ff = gwe.shape[1]

    def flat(*shape):
        return jax.ShapeDtypeStruct(shape, F32)

    vectors = [(384,), (768,), (768,), (768,), (768,), (ff,), (384,)]
    tables = [(3, 27, 384), (3, 384), (2, KC, 384), (4, NT + 2 * NHW)]

    def rows(n, width):
        return pl.BlockSpec((n, width), lambda c: (c, 0))

    return pl.pallas_call(
        final_kernel,
        grid=(4,),
        in_specs=[
            per_clip(TOK, 384),
            per_clip(TOK, 384),
            per_clip(8, 512),
            per_clip(8, 512),
            per_clip(TOK, 768),
            whole((768,)),
            per_clip(TOK, 384),
            per_clip(TOK, 384),
            pl.BlockSpec((3, 192, 384), lambda c: (0, c, 0)),
            pl.BlockSpec((1, 96, 384), lambda c: (3, c, 0)),
            pl.BlockSpec((1, 96, 384), lambda c: (3, c + 4, 0)),
            rows(ff // 4, 768),
            rows(192, ff),
            whole((64, 1152)),
        ],
        out_specs=[
            per_clip(TOK, 384),
            per_clip(TOK, 384),
            pl.BlockSpec((3, 192, 384), lambda c: (0, c, 0)),
            rows(96, 768),
            rows(ff // 4, 768),
            rows(192, ff),
        ]
        + [whole(s) for s in tables + vectors],
        out_shape=[
            flat(4, TOK, 384),
            jax.ShapeDtypeStruct((4, TOK, 384), BF16),
            flat(3, 768, 384),
            flat(384, 768),
            flat(ff, 768),
            flat(768, ff),
        ]
        + [flat(*s) for s in tables + vectors],
        scratch_shapes=[pltpu.VMEM((TOK, 768), F32), pltpu.VMEM((128, 512), F32)],
        compiler_params=params(),
        cost_estimate=cost(0.1, 40),
        name="final",
    )(own, recv, sums, sums_p, x, gain, res, br, red, red, red, gwr, gwe, small)


STREAMS = ((768, 384, BF16),) * 4 + ((64, 1152, F32),)


def stages_of(stream, bits):
    rows, _, dtype = stream
    least = 8 if dtype == F32 else 16
    out = []
    for bit in range(bits):
        halve = bit < 4 and rows // 2 >= least
        rows = rows // 2 if halve else rows
        out.append((bit, rows, halve))
    return out


def reduce_kernel(bits, gw, gwo, s1, gbe, gbr, pos, na, nb, red_o, small_o, *scratch):
    n = len(STREAMS)
    last = n - 1
    acc, snd, rcv = (scratch[i * n : i * n + n] for i in range(3))
    fin, fin_s, nsnd, nrcv, ssem, rsem = scratch[3 * n :]
    tp = lax.axis_index("tp")
    meet(bits=range(bits))

    nsnd[...] = na[...] + nb[...]
    norm = remote(nsnd, nrcv, ssem.at[n, 0], rsem.at[n, 0], tp=1 - tp)
    norm.start()

    stages = [stages_of(s, bits) for s in STREAMS]
    start = [0] * n
    copies = [None] * n
    slot = [0] * n
    rounds = bits

    def source(i, rows):
        return gw[i, rows] if i < 3 else gwo[rows] if i == 3 else acc[i][rows]

    def span(i, at, rows):
        return pl.ds(pl.multiple_of(at, 8 if i == last else 16), rows)

    def send(i, r):
        bit, rows, halve = stages[i][r]
        mine, peer = peer_of(bit)
        if halve:
            away = span(i, start[i] + (1 - mine) * rows, rows)
            start[i] = start[i] + mine * rows
        else:
            away = span(i, start[i], rows)
        here = slice(slot[i], slot[i] + rows)
        value = source(i, away) if r == 0 else acc[i][away]
        snd[i][here] = value.astype(snd[i].dtype)
        copies[i] = remote(
            snd[i].at[here], rcv[i].at[here], ssem.at[i, r], rsem.at[i, r], blk=peer
        )
        copies[i].start()

    def take(i, r):
        rows = stages[i][r][1]
        keep = span(i, start[i], rows)
        here = slice(slot[i], slot[i] + rows)
        slot[i] += rows
        copies[i].wait()
        value = source(i, keep) if r == 0 else acc[i][keep]
        acc[i][keep] = value.astype(F32) + rcv[i][here].astype(F32)

    for i in range(last):
        send(i, 0)
    acc[last][:32] = s1[...]
    acc[last][32:56] = jnp.zeros((24, 1152), F32)
    half = gbe.shape[1] // 2
    acc[last][32:33, :half] = gbe[:, :half]
    acc[last][33:34, :half] = gbe[:, half:]
    acc[last][34:35, :384] = gbr[...]
    acc[last][40:48, :128] = pos[...]
    norm.wait()
    acc[last][56:] = nsnd[...] + nrcv[...]
    send(last, 0)
    for r in range(rounds):
        for i in range(n):
            take(i, r)
            if r + 1 < rounds:
                send(i, r + 1)

    back = [[r for r in range(rounds) if stages[i][r][2]][::-1] for i in range(n)]

    def whole_of(i):
        return fin_s if i == last else fin.at[i]

    def give(i, r):
        bit, rows, _ = stages[i][r]
        mine, peer = peer_of(bit)
        here = whole_of(i).at[span(i, start[i], rows)]
        start[i] = start[i] - mine * rows
        copies[i] = remote(
            here, here, ssem.at[i, rounds + r], rsem.at[i, rounds + r], blk=peer
        )
        copies[i].start()

    for i in range(n):
        mine = span(i, start[i], stages[i][-1][1])
        whole_of(i)[mine] = acc[i][mine].astype(STREAMS[i][2])
        give(i, back[i][0])
    for k in range(max(len(b) for b in back)):
        for i in range(n):
            if k < len(back[i]):
                copies[i].wait()
                if k + 1 < len(back[i]):
                    give(i, back[i][k + 1])
    red_o[...] = fin[...]
    small_o[...] = fin_s[...]


def reduce_call(gw, gwo, s1, gbe, gbr, pos, na, nb):
    bits = blk_bits()
    inside = pl.BlockSpec(memory_space=pltpu.VMEM)
    kinds = [(F32, 1), (None, 2), (None, 2)]
    scratch = [
        pltpu.VMEM((rows * times, cols), kind or dtype)
        for kind, times in kinds
        for rows, cols, dtype in STREAMS
    ]
    sems = (len(STREAMS) + 1, 2 * bits)
    return pl.pallas_call(
        functools.partial(reduce_kernel, bits),
        in_specs=[inside] * 8,
        out_specs=[inside] * 2,
        out_shape=[
            jax.ShapeDtypeStruct((4, 768, 384), BF16),
            jax.ShapeDtypeStruct((64, 1152), F32),
        ],
        scratch_shapes=scratch
        + [
            pltpu.VMEM((4, 768, 384), BF16),
            pltpu.VMEM((64, 1152), F32),
            pltpu.VMEM((8, 1152), F32),
            pltpu.VMEM((8, 1152), F32),
            DMA(sems),
            DMA(sems),
        ],
        compiler_params=params(collective_id=4, has_side_effects=True),
        cost_estimate=cost(0.1, 100),
        name="reduce",
    )(gw, gwo, s1, gbe, gbr, pos, na, nb)


def local(
    layer_input,
    first_gain,
    first_shift,
    project_weight,
    project_bias,
    pool_taps,
    memory_taps,
    position_bias,
    output_weight,
    output_bias,
    second_gain,
    second_shift,
    expand_weight,
    expand_bias,
    reduce_weight,
    reduce_bias,
    cotangent,
    clip_place,
):
    clips = layer_input.shape[0] // TOK
    half = layer_input.shape[1]

    def clipwise(a):
        return a.reshape(clips, TOK, a.shape[-1])

    w = jnp.transpose(project_weight, (1, 0, 2))
    hot = jnp.asarray(table_onehot())
    (
        pool, proj, x, ext, lse, wop, tab, mo, mp, hid, cot, gn, res, bpeer,
        gwr, gwe, gbe, gbr,
    ) = front_call(
        clip_place, position_bias, clipwise(layer_input), clipwise(cotangent),
        output_weight, output_bias, first_gain, first_shift, w, project_bias, pool_taps,
        memory_taps, hot, second_gain, second_shift, expand_weight, expand_bias,
        reduce_weight, reduce_bias,
    )
    gp, gext, gh, gwo, sums2, pos, gwr, gwe, br = unattend_call(
        clip_place, pool, ext, tab, hot, lse, gn, hid, cot, mo, mp, output_weight, wop,
        second_gain, gwr, gwe, bpeer,
    )
    own, recv, sums, sums_p, gw, small, norm, gwr, gwe = unpool_call(
        gp, gext, proj, pool, x, gh, w, pool_taps, memory_taps, first_gain, first_shift,
        gwr, gwe,
    )
    red, small = reduce_call(gw, gwo, small, gbe, gbr, pos, norm, sums2)
    (
        gin, result, gw, gwo, gwr, gwe, gt, gb, gmt, pos, gbo, gg1, gs1, gg2, gs2, gbe, gbr
    ) = final_call(own, recv, sums, sums_p, x, first_gain, res, br, red, gwr, gwe, small)
    return (
        result.reshape(clips * TOK, half),
        gin.reshape(clips * TOK, half),
        gg1,
        gs1,
        jnp.transpose(gw, (1, 0, 2)),
        gb,
        gt,
        gmt,
        pos,
        gwo,
        gbo,
        gg2,
        gs2,
        gwe,
        gbe,
        gwr,
        gbr,
    )


def solution(mesh):
    return jax.shard_map(
        local,
        mesh=mesh,
        in_specs=(
            P("blk", "tp"),
            P(),
            P(),
            P(None, None, "tp"),
            P(None, "tp"),
            P(None, None, "tp"),
            P(None, None, "tp"),
            P("tp", None),
            P("tp", None),
            P("tp"),
            P(),
            P(),
            P(None, "tp"),
            P("tp"),
            P("tp", None),
            P("tp"),
            P("blk", "tp"),
            P("blk"),
        ),
        out_specs=(
            P("blk", "tp"),
            P("blk", "tp"),
            P(),
            P(),
            P(None, None, "tp"),
            P(None, "tp"),
            P(None, None, "tp"),
            P(None, None, "tp"),
            P("tp", None),
            P("tp", None),
            P("tp"),
            P(),
            P(),
            P(None, "tp"),
            P("tp"),
            P("tp", None),
            P("tp"),
        ),
        check_vma=False,
    )
```

```python
import functools

import jax
import jax.numpy as jnp
import numpy as np
from jax import lax
from jax.experimental import pallas as pl
from jax.experimental.pallas import tpu as pltpu
from jax.sharding import PartitionSpec as P

HEAD_DIM = 96
CT = 8
CS = 7
KC = 4
KT = 12
NT = 19
NHW = 13
TOK = 392
PAD = 448
MROW = 112
KROWS = 672
EPS = 1e-06
SCALE = HEAD_DIM ** (-0.5)
LOG2E = 1.4426950408889634
EXP_SCALE = SCALE * LOG2E
NEG = -1e30
VMEM = 61 << 20
F32 = jnp.float32
BF16 = jnp.bfloat16

NT_DIMS = (((1,), (1,)), ((), ()))
TN_DIMS = (((0,), (0,)), ((), ()))


def mm(a, b):
    return jnp.dot(a, b, preferred_element_type=F32)


def mm_nt(a, b):
    return lax.dot_general(a, b, NT_DIMS, preferred_element_type=F32)


def mm_tn(a, b):
    return lax.dot_general(a, b, TN_DIMS, preferred_element_type=F32)


def iota(shape, dim):
    return lax.broadcasted_iota(jnp.int32, shape, dim)


def pad_matrix():
    row = iota((PAD, TOK), 0)
    col = iota((PAD, TOK), 1)
    x = lax.bitwise_and(row, 7)
    line = lax.shift_right_logical(row, 3)
    return jnp.where((x < CS) & (col == line * CS + x), 1.0, 0.0).astype(BF16)


def query_onehot():
    row = iota((PAD, 128), 0)
    col = iota((PAD, 128), 1)
    x = lax.bitwise_and(row, 7)
    line = lax.shift_right_logical(row, 3)
    t = lax.div(line, CS)
    y = line - t * CS
    c = lax.bitwise_and(col, 31)
    hit = (c == t) | (c == 8 + y) | ((c == 15 + x) & (x < CS))
    return jnp.where(hit & (col < 64), 1.0, 0.0).astype(BF16)


def key_onehot(dtype=BF16):
    row = iota((KROWS, 32), 0)
    col = iota((KROWS, 32), 1)
    x = lax.bitwise_and(row, 7)
    line = lax.shift_right_logical(row, 3)
    t = lax.div(line, CS)
    y = line - t * CS
    hit = (col == t) | (col == 12 + y) | ((col == 19 + x) & (x < CS))
    return jnp.where(hit, 1.0, 0.0).astype(dtype)


def key_mask(place):
    row = iota((KROWS, 32), 0)
    col = iota((KROWS, 32), 1)
    x = lax.bitwise_and(row, 7)
    need = jnp.where(row < PAD, 0, jnp.where(row < PAD + MROW, 1, 2))
    bad = (x == CS) | (place < need)
    return jnp.where(bad & (col == 0), NEG, 0.0).astype(BF16)


def one_column():
    return jnp.where(iota((PAD, 32), 1) == 0, 1.0, 0.0).astype(BF16)


def table_onehot():
    out = np.zeros((NT + 2 * NHW, 32, 128), np.float32)
    for t2 in range(KT):
        for t in range(CT):
            out[t - t2 + CT - 1 if t2 < CT else t2 + CT - 1, t2, t] = 1
    for a2 in range(CS):
        for a in range(CS):
            out[NT + a - a2 + CS - 1, 12 + a2, 8 + a] = 1
            out[NT + NHW + a - a2 + CS - 1, 19 + a2, 15 + a] = 1
    out[:, :, 32:64] = out[:, :, :32]
    return out


FREQ = 304
GRID = (9, 8, 8)


def frequencies():
    alone, paired, seen = [], [], set()
    for t in range(9):
        for y in range(8):
            for x in range(8):
                other = (-t % 9, -y % 8, -x % 8)
                if (t, y, x) not in seen:
                    (alone if other == (t, y, x) else paired).append((t, y, x))
                    seen.update(((t, y, x), other))
    return np.array(alone + paired), len(alone)


def waves(points):
    freq, _ = frequencies()
    angle = 2 * np.pi * (freq[:, None, :] * points[None, :, :] / np.array(GRID)).sum(-1)
    out = np.zeros((2 * FREQ, len(points)))
    out[: len(freq)] = np.cos(angle)
    out[FREQ : FREQ + len(freq)] = np.sin(angle)
    return out


def fourier_tables():
    freq, alone = frequencies()
    tokens = np.array([(t, y, x) for t in range(CT) for y in range(CS) for x in range(CS)])
    shifts = np.array([(a - 1, b - 1, e - 1) for a in range(3) for b in range(3) for e in range(3)])
    sign = np.ones((2 * FREQ, 1))
    sign[FREQ:] = -1
    weight = np.zeros((2 * FREQ, 1))
    for start in (0, FREQ):
        weight[start : start + alone] = 1
        weight[start + alone : start + len(freq)] = 2
    ahead = waves(tokens) * sign
    padded = np.zeros((2 * FREQ, PAD))
    padded[:, [r for r in range(PAD) if r % 8 < CS]] = ahead
    taps = np.zeros((2 * FREQ, 32))
    taps[:, :27] = waves(shifts)
    scale = 1.0 / np.prod(GRID)
    high, low = two_parts(taps * scale)
    return (
        jnp.asarray(ahead, BF16),
        jnp.asarray(padded, BF16),
        jnp.asarray((ahead * weight).T, BF16),
        jnp.asarray((padded * weight).T, BF16),
        jnp.asarray(np.concatenate([high, high, low, low], 1)),
        jnp.asarray((taps * sign * weight * scale).T, BF16),
    )


def two_parts(a):
    xp = np if isinstance(a, np.ndarray) else jnp
    high = a.astype(BF16)
    return high, (a - high.astype(xp.float32)).astype(BF16)


def tap_spectra(tapwaves, taps, h_s):
    for i in range(3):
        high, low = two_parts(jnp.concatenate([taps[i], jnp.zeros((5, 384), F32)], 0))
        parts = jnp.concatenate([high, low, high, low], 0)
        h_s[:, i * 384 : i * 384 + 384] = mm(tapwaves[...], parts)


def bias_tables(pos, hot, tab_o):
    col = iota((32, 128), 1)
    for h in range(4):
        table = 0.0
        for e in range(NT + 2 * NHW):
            table = table + pos[h, e] * hot[e]
        table = table * (HEAD_DIM**0.5)
        high = table.astype(BF16)
        low = (table - high.astype(F32)).astype(BF16)
        tab_o[h] = jnp.where(col < 32, high, low)


def row_stats(x):
    mean = jnp.mean(x, axis=-1, keepdims=True)
    cen = x - mean
    var = jnp.mean(cen * cen, axis=-1, keepdims=True)
    return cen, lax.rsqrt(var + EPS)


def col_sum(x):
    return jnp.sum(x, axis=0, keepdims=True)


def as_row(ref):
    return ref[...].reshape(1, ref.shape[0])


def remote(src, dst, ssem, rsem, **where):
    return pltpu.make_async_remote_copy(
        src_ref=src, dst_ref=dst, send_sem=ssem, recv_sem=rsem,
        device_id=where, device_id_type=pl.DeviceIdType.MESH,
    )


def half_lanes(which):
    return pl.ds(pl.multiple_of(which * 384, 128), 384)


def peer_of(bit):
    blk = lax.axis_index("blk")
    mine = lax.rem(lax.div(blk, 1 << bit), 2)
    return mine, blk + (1 - 2 * mine) * (1 << bit)


def meet(bits=(), ring=False):
    barrier = pltpu.get_barrier_semaphore()
    blk = lax.axis_index("blk")
    peers = lax.axis_size("blk")
    others = [{"tp": 1 - lax.axis_index("tp")}] + [{"blk": peer_of(b)[1]} for b in bits]
    if ring:
        others += [{"blk": lax.rem(blk + by, peers)} for by in (1, peers - 1)]
    for other in others:
        pl.semaphore_signal(barrier, device_id=other, device_id_type=pl.DeviceIdType.MESH)
    pl.semaphore_wait(barrier, len(others))


def blk_bits():
    return lax.axis_size("blk").bit_length() - 1


def pool_step(c, xb, gain, shift, w, b, mtaps, fd, gp, h_s, pool_s, proj_o, ext_s, z_s):
    cen, r = row_stats(xb.astype(F32))
    normed = (cen * r * as_row(gain) + as_row(shift)).astype(BF16)
    for i in range(3):
        cols = slice(i * 384, i * 384 + 384)
        project = (mm(normed, w[i]) + b[i : i + 1]).astype(BF16)
        proj_o[0, :, cols] = project
        spec = mm(fd[...], project)
        hr, hi = h_s[:FREQ, cols], h_s[FREQ:, cols]
        z_s[i, :FREQ] = (hr * spec[:FREQ] - hi * spec[FREQ:]).astype(BF16)
        z_s[i, FREQ:] = (hr * spec[FREQ:] + hi * spec[:FREQ]).astype(BF16)
        pooled = mm(gp[...], z_s[i])
        pool_s[c, :, cols] = pooled.astype(BF16)
        if i:
            frames = pooled.reshape(CT, 56, 384)
            mcols = slice((i - 1) * 384, i * 384)
            for s in range(2):
                m = 0.0
                for u in range(KC):
                    m = m + frames[s * KC + u] * mtaps[i - 1, u : u + 1]
                ext_s[c + 2, s * 56 : s * 56 + 56, mcols] = m.astype(BF16)


def whole(shape):
    zeros = (0,) * len(shape)
    return pl.BlockSpec(shape, lambda c: zeros, pipeline_mode=pl.Buffered(1))


def per_clip(*shape):
    rest = (0,) * len(shape)
    return pl.BlockSpec((1,) + shape, lambda c: (c,) + rest)


def params(**kw):
    return pltpu.CompilerParams(vmem_limit_bytes=VMEM, **kw)


def cost(gflops, mbytes):
    return pl.CostEstimate(
        flops=int(gflops * 1e9), bytes_accessed=int(mbytes * 1e6), transcendentals=0
    )


def head_keys(kv, mask, tab, h):
    k = kv[:, h * HEAD_DIM : (h + 1) * HEAD_DIM]
    bias = mm(key_onehot(), tab[h]).astype(BF16)
    return jnp.concatenate([k, mask, bias], axis=1)


def head_queries(q, ones, onehot):
    return jnp.concatenate([q, ones, onehot], axis=1)


CHUNK = 48


def chunks():
    return [slice(j * CHUNK, j * CHUNK + CHUNK) for j in range(KROWS // CHUNK)]


def fold(x, op):
    return op(x.reshape(x.shape[0] // 8, 8, x.shape[1]), axis=0)


def attend_step(place, own, m1, m2, tab, lse_o, kv, s_scr, p_scr, mix_t):
    kv[:PAD] = own[:, 384:]
    kv[PAD : PAD + MROW] = m1[...]
    kv[PAD + MROW :] = m2[...]
    mask = key_mask(place)
    ones = one_column()
    onehot = query_onehot()
    mix_t[:, PAD:] = jnp.zeros((384, 512 - PAD), F32)
    for h in range(4):
        feats = slice(h * HEAD_DIM, (h + 1) * HEAD_DIM)
        ka = head_keys(kv, mask, tab, h)
        qa = head_queries(own[:, feats], ones, onehot)
        s_scr[...] = mm_nt(ka, qa)
        top = jnp.max(fold(s_scr[...], jnp.max), axis=0, keepdims=True) * EXP_SCALE
        total = 0.0
        for rows in chunks():
            p = jnp.exp2(s_scr[rows] * EXP_SCALE - top)
            total = total + fold(p, jnp.sum)
            p_scr[rows] = p.astype(BF16)
        total = jnp.sum(total, axis=0, keepdims=True)
        v = kv[:, 384 + h * HEAD_DIM : 384 + (h + 1) * HEAD_DIM]
        mix_t[feats, :PAD] = mm_tn(v, p_scr[...]) * (1.0 / total)
        lse_o[0, h : h + 1] = top + jnp.log2(total)
    mix = jnp.transpose(mix_t[...])[:PAD]
    merged = (mix + own[:, :384].astype(F32)).astype(BF16)
    return mm_tn(pad_matrix(), merged).astype(BF16)


FFC = 512
GWC = 384


def phi_pair(x):
    ax = jnp.abs(x) * 0.7071067811865476
    t = 1.0 / (1.0 + 0.3275911 * ax)
    e = jnp.exp(-ax * ax)
    poly = 1.061405429 * t - 1.453152027
    poly = poly * t + 1.421413741
    poly = poly * t - 0.284496736
    poly = poly * t + 0.254829592
    tail = 0.5 * poly * t * e
    return jnp.where(x >= 0, 1.0 - tail, tail), e * 0.3989422804014327


def feed_step(start, hid, cot, g2, s2, we, be, wr, nt_s, br_s, gn_s, gwr, gwe, gbe_o):
    cen, r = row_stats(hid)
    nt_s[...] = (cen * r * as_row(g2) + as_row(s2)).astype(BF16)
    for j in range(we.shape[1] // FFC):
        cols = slice(j * FFC, j * FFC + FFC)
        ex = mm(nt_s[...], we[:, cols]) + be[cols].reshape(1, FFC)
        cdf, pdf = phi_pair(ex)
        act = (ex * cdf).astype(BF16)
        ga = mm_nt(cot[...], wr[cols, :])
        ge = (ga * (cdf + ex * pdf)).astype(BF16)
        gbe_o[:, cols] += col_sum(ge.astype(F32))
        br, gn = mm(act, wr[cols, :]), mm_nt(ge, we[:, cols])
        br_s[...] = br if j == 0 else br_s[...] + br
        gn_s[...] = gn if j == 0 else gn_s[...] + gn
        add_to(gwr.at[cols], mm_tn(act, cot[...]), start)
        add_to(gwe.at[:, cols], mm_tn(nt_s[...], ge), start)


def add_to(ref, value, start):
    ref[...] = value if start else ref[...] + value


def pool_turn(s):
    return lax.rem(s + 2, 4)


def own_turn(s):
    return lax.rem(s + 2 * lax.axis_index("tp"), 4)


def other_turn(s):
    return lax.rem(s + 2 + 2 * lax.axis_index("tp"), 4)


def front_kernel(
    place, pos, x_h, cot_h, wo_h, bo, gain, shift, w, b, taps, mtaps, hot, fd, gp, tw,
    wo, g2, s2, we, be, wr, br,
    pool_o, proj_o, x_o, ext_o, lse_o, wop_o, tab_o, mo_o, mp_o, hid_o, cot_o, gn_o, res_o,
    bpeer_o, gwr_o, gwe_o, gbe_o, gbr_o, gnb_o,
    xs, cs, pool_s, ext_s, mo_s, mp_s, wop_s, bo_s, h_s, z_s, kv, s_scr, p_scr, mix_t,
    nt_s, br_s, gn_s, gnb, gnr, gwr, gwe, gwb, geb,
    x_snd, x_rcv, x_loc, c_snd, c_rcv, c_loc, w_snd, w_rcv, e_snd, e_rcv,
    m_snd, m_rcv, g_snd, g_rcv, o_sem, gr_sem, ge_sem, v_snd, v_rcv,
):
    step = pl.program_id(0)
    me = lax.axis_index("tp")
    blk = lax.axis_index("blk")
    peers = lax.axis_size("blk")
    mine, theirs = half_lanes(me), half_lanes(1 - me)

    def x_copy(c):
        return remote(x_h.at[c], xs.at[c, :, mine], x_snd.at[c], x_rcv.at[c], tp=1 - me)

    def x_local(c):
        return pltpu.make_async_copy(x_h.at[c], xs.at[c, :, mine], x_loc.at[c])

    def cot_copy(c):
        return remote(cot_h.at[c], cs.at[c, :, mine], c_snd.at[c], c_rcv.at[c], tp=1 - me)

    def cot_local(c):
        return pltpu.make_async_copy(cot_h.at[c], cs.at[c, :, mine], c_loc.at[c])

    weights = Doubling(None, wop_s, 2, v_snd, v_rcv)

    def weight_copy():
        rows = weights.held(2)
        return remote(wo_h.at[rows], wop_s.at[rows], w_snd.at[0], w_rcv.at[0], tp=1 - me)

    def bias_copy():
        return remote(bo_s.at[:, mine], bo_s.at[:, mine], w_snd.at[1], w_rcv.at[1], tp=1 - me)

    def memory_copy(j):
        return remote(
            ext_s.at[4 + j], ext_s.at[j], e_snd.at[j], e_rcv.at[j],
            blk=lax.rem(blk + 1, peers),
        )

    def merged_copy(c):
        return remote(mo_s.at[c], mp_s.at[c], m_snd.at[c], m_rcv.at[c], tp=1 - me)

    def grad_copy():
        return remote(gnb.at[0], gnr, g_snd.at[0], g_rcv.at[0], tp=1 - me)

    outs = [
        pltpu.make_async_copy(pool_s, pool_o, o_sem.at[0]),
        pltpu.make_async_copy(xs, x_o, o_sem.at[1]),
        pltpu.make_async_copy(ext_s, ext_o, o_sem.at[2]),
        pltpu.make_async_copy(wop_s, wop_o, o_sem.at[3]),
        pltpu.make_async_copy(cs, cot_o, o_sem.at[4]),
        pltpu.make_async_copy(mo_s, mo_o, o_sem.at[5]),
        pltpu.make_async_copy(mp_s, mp_o, o_sem.at[6]),
    ]

    @pl.when(step == 0)
    def _():
        meet(bits=(0, 1, 2), ring=True)
        for c in (2, 3, 0, 1):
            x_copy(c).start()
            x_local(c).start()
        bo_s[:, mine] = jnp.broadcast_to(as_row(bo), (8, 384))
        gbe_o[...] = jnp.zeros_like(gbe_o)
        gbr_o[...] = jnp.zeros_like(gbr_o)
        bias_tables(pos, hot, tab_o)
        tap_spectra(tw, taps, h_s)

    @pl.when((step == 0) & (blk == 0))
    def _():
        ext_s[:2] = jnp.zeros((2, MROW, 768), BF16)

    @pl.when(step < 4)
    def _():
        c = pool_turn(step)
        x_local(c).wait()
        x_copy(c).wait_recv()

        @pl.when(step == 2)
        def _():
            weight_copy().start()
            bias_copy().start()

        @pl.when(step == 3)
        def _():
            cot_copy(own_turn(0)).start()
            for t in range(4):
                cot_local(t).start()

        pool_step(c, xs[c], gain, shift, w, b, mtaps, fd, gp, h_s, pool_s, proj_o, ext_s, z_s)

        @pl.when((step < 2) & (blk < peers - 1))
        def _():
            memory_copy(step).start()

        @pl.when(step == 3)
        def _():
            outs[0].start()
            outs[1].start()

    @pl.when((step >= 4) & (step < 8))
    def _():
        c = own_turn(step)

        @pl.when((step == 4) & (blk > 0))
        def _():
            memory_copy(0).wait_recv()
            memory_copy(1).wait_recv()

        @pl.when(step < 7)
        def _():
            cot_copy(own_turn(step + 1)).start()

        mo_s[c] = attend_step(
            place[c], pool_s.at[c], ext_s.at[c + 1], ext_s.at[c], tab_o, lse_o,
            kv, s_scr, p_scr, mix_t,
        )
        merged_copy(c).start()

        @pl.when(step == 4)
        def _():
            weight_copy().wait_recv()
            weights.start(2)

        for bit in (2, 1):

            @pl.when(step == 7 - bit)
            def _():
                weights.finish(bit)
                weights.start(bit - 1)

    @pl.when(step >= 8)
    def _():
        c = other_turn(step)

        @pl.when(step == 8)
        def _():
            weights.finish(0)
            bias_copy().wait_recv()
            outs[2].start()
            outs[3].start()

        cot_local(c).wait()
        cot_copy(c).wait_recv()
        merged_copy(c).wait_recv()

        @pl.when(step == 11)
        def _():
            for t in outs[4:]:
                t.start()

        hid = xs[c].astype(F32) + mm(mo_s[c], wo[...]) + mm(mp_s[c], wop_s[...])
        hid = hid + bo_s[0:1, :]
        hid_o[0] = hid
        rest = (hid, cs.at[c], g2, s2, we, be, wr, nt_s, br_s, gn_s, gwr, gwe, gbe_o)
        pl.when(step == 8)(lambda: feed_step(True, *rest))
        pl.when(step > 8)(lambda: feed_step(False, *rest))
        res_o[0] = hid_o[0, :, mine] + br_s[:, mine] + as_row(br)
        bpeer_o[0] = br_s[:, theirs].astype(BF16)
        gbr_o[...] += col_sum(cs[c, :, mine].astype(F32))

        @pl.when(step < 10)
        def _():
            gnb[step - 8] = gn_s[...].astype(BF16)

        @pl.when(step == 8)
        def _():
            grad_copy().start()

        @pl.when(step == 9)
        def _():
            gnb_o[...] = gnb[1]

        @pl.when(step >= 10)
        def _():
            gn_o[step - 10] = gn_s[...]

    def reduce_out(j):
        rows = slice(j * GWC, j * GWC + GWC)
        return pltpu.make_async_copy(gwb.at[j % 2], gwr_o.at[rows], gr_sem.at[j % 2])

    def expand_out(j):
        cols = slice(j * GWC, j * GWC + GWC)
        return pltpu.make_async_copy(geb.at[j % 2], gwe_o.at[:, cols], ge_sem.at[j % 2])

    @pl.when(step == 11)
    def _():
        parts = we.shape[1] // GWC
        for j in range(parts):
            if j >= 2:
                reduce_out(j - 2).wait()
                expand_out(j - 2).wait()
            cols = slice(j * GWC, j * GWC + GWC)
            gwb[j % 2] = gwr[cols].astype(BF16)
            reduce_out(j).start()
            geb[j % 2] = gwe[:, cols].astype(BF16)
            expand_out(j).start()
        for j in (parts - 2, parts - 1):
            reduce_out(j).wait()
            expand_out(j).wait()
        grad_copy().wait_recv()
        gn_o[0] += gnr[...].astype(F32)
        for c in range(4):
            x_copy(c).wait_send()
            cot_copy(c).wait_send()
            merged_copy(c).wait_send()
        for t in (weight_copy(), bias_copy(), grad_copy()):
            t.wait_send()
        for t in outs:
            t.wait()

    @pl.when((step == 11) & (blk < peers - 1))
    def _():
        memory_copy(0).wait_send()
        memory_copy(1).wait_send()


HBM = pl.BlockSpec(memory_space=pl.ANY)
IN_SMEM = pl.BlockSpec(memory_space=pltpu.SMEM)
DMA = pltpu.SemaphoreType.DMA


def whole_like(*arrays):
    return [whole(a.shape) for a in arrays]


def front_call(
    place, pos, x, cot, wo, bo, gain, shift, w, b, taps, mtaps, hot, fd, gp, tw,
    g2, s2, we, be, wr, br,
):
    ff = we.shape[1]

    def at(turn, low, high, *shape):
        rest = (0,) * len(shape)
        return pl.BlockSpec(
            (1,) + shape, lambda s: (turn(jnp.clip(s, low, high)),) + rest
        )

    def own(*shape):
        rest = (0,) * len(shape)
        return pl.BlockSpec((1,) + shape, lambda s: (jnp.clip(s - 10, 0, 1),) + rest)

    return pl.pallas_call(
        front_kernel,
        grid=(12,),
        in_specs=[IN_SMEM, IN_SMEM, HBM, HBM, HBM]
        + whole_like(bo, gain, shift, w, b, taps, mtaps, hot, fd, gp, tw, wo, g2, s2, we, be, wr, br),
        out_specs=[
            HBM,
            at(pool_turn, 0, 3, TOK, 1152),
            HBM,
            HBM,
            at(own_turn, 4, 7, 4, PAD),
            HBM,
            whole((4, 32, 128)),
            HBM,
            HBM,
            own(TOK, 768),
            HBM,
            whole((2, TOK, 768)),
            at(other_turn, 8, 11, TOK, 384),
            at(other_turn, 8, 11, TOK, 384),
            HBM,
            HBM,
            whole((1, ff)),
            whole((1, 384)),
            whole((TOK, 768)),
        ],
        out_shape=[
            jax.ShapeDtypeStruct((4, PAD, 1152), BF16),
            jax.ShapeDtypeStruct((4, TOK, 1152), BF16),
            jax.ShapeDtypeStruct((4, TOK, 768), BF16),
            jax.ShapeDtypeStruct((6, MROW, 768), BF16),
            jax.ShapeDtypeStruct((4, 4, PAD), F32),
            jax.ShapeDtypeStruct((384, 768), BF16),
            jax.ShapeDtypeStruct((4, 32, 128), BF16),
            jax.ShapeDtypeStruct((4, TOK, 384), BF16),
            jax.ShapeDtypeStruct((4, TOK, 384), BF16),
            jax.ShapeDtypeStruct((2, TOK, 768), F32),
            jax.ShapeDtypeStruct((4, TOK, 768), BF16),
            jax.ShapeDtypeStruct((2, TOK, 768), F32),
            jax.ShapeDtypeStruct((4, TOK, 384), F32),
            jax.ShapeDtypeStruct((4, TOK, 384), BF16),
            jax.ShapeDtypeStruct((ff, 768), BF16),
            jax.ShapeDtypeStruct((768, ff), BF16),
            jax.ShapeDtypeStruct((1, ff), F32),
            jax.ShapeDtypeStruct((1, 384), F32),
            jax.ShapeDtypeStruct((TOK, 768), BF16),
        ],
        scratch_shapes=[
            pltpu.VMEM((4, TOK, 768), BF16),
            pltpu.VMEM((4, TOK, 768), BF16),
            pltpu.VMEM((4, PAD, 1152), BF16),
            pltpu.VMEM((6, MROW, 768), BF16),
            pltpu.VMEM((4, TOK, 384), BF16),
            pltpu.VMEM((4, TOK, 384), BF16),
            pltpu.VMEM((384, 768), BF16),
            pltpu.VMEM((8, 768), F32),
            pltpu.VMEM((2 * FREQ, 1152), F32),
            pltpu.VMEM((3, 2 * FREQ, 384), BF16),
            pltpu.VMEM((KROWS, 768), BF16),
            pltpu.VMEM((KROWS, PAD), F32),
            pltpu.VMEM((KROWS, PAD), BF16),
            pltpu.VMEM((384, 512), F32),
            pltpu.VMEM((TOK, 768), BF16),
            pltpu.VMEM((TOK, 768), F32),
            pltpu.VMEM((TOK, 768), F32),
            pltpu.VMEM((2, TOK, 768), BF16),
            pltpu.VMEM((TOK, 768), BF16),
            pltpu.VMEM((ff, 768), F32),
            pltpu.VMEM((768, ff), F32),
            pltpu.VMEM((2, GWC, 768), BF16),
            pltpu.VMEM((2, 768, GWC), BF16),
        ]
        + [DMA((4,))] * 6
        + [DMA((3,))] * 2
        + [DMA((2,))] * 2
        + [DMA((4,))] * 2
        + [DMA((2,))] * 2
        + [DMA((7,))]
        + [DMA((2,))] * 2
        + [DMA((3,))] * 2,
        compiler_params=params(collective_id=1, has_side_effects=True),
        cost_estimate=cost(36, 60),
        name="front",
    )(
        place, pos, x, cot, wo, bo, gain, shift, w, b, taps, mtaps, hot, fd, gp, tw,
        wo, g2, s2, we, be, wr, br,
    )


def halvings(rows, bits, levels=4):
    out = []
    for bit in range(bits):
        rows = rows // 2 if bit < levels else rows
        out.append((bit, rows))
    return out


def slots(rows, bits, levels=4):
    at, places = 0, []
    for _, n in halvings(rows, bits, levels):
        places.append(at)
        at += n
    return at, places


class Halving:
    def __init__(self, src, keep, rcv, ssem, rsem, lsem=None, levels=4):
        self.src, self.keep, self.rcv = src, keep, rcv
        self.ssem, self.rsem, self.lsem = ssem, rsem, lsem
        self.bits, self.levels = blk_bits(), levels
        self.rows = src.shape[0]
        self.list = halvings(self.rows, self.bits, levels)
        self.places = slots(self.rows, self.bits, levels)[1]

    def offset(self, r):
        off = 0
        for bit, n in self.list[1 : r + 1]:
            if bit < self.levels:
                off = off + peer_of(bit)[0] * n
        return off

    def span(self, at, n):
        return pl.ds(pl.multiple_of(at, 8 if self.keep.dtype == F32 else 16), n)

    def copy(self, r):
        bit, n = self.list[r]
        mine, peer = peer_of(bit)
        if r == 0:
            src = self.src.at[self.span((1 - mine) * n, n)]
        else:
            away = self.offset(r - 1) + ((1 - mine) * n if bit < self.levels else 0)
            src = self.keep.at[self.span(away, n)]
        dst = self.rcv.at[pl.ds(self.places[r], n)]
        return remote(src, dst, self.ssem.at[r], self.rsem.at[r], blk=peer)

    def own_half(self):
        n = self.list[0][1]
        return self.span(peer_of(0)[0] * n, n)

    def load(self):
        return pltpu.make_async_copy(self.src.at[self.own_half()], self.keep, self.lsem)

    def start(self, r):
        self.copy(r).start()
        if r == 0 and self.lsem is not None:
            self.load().start()

    def finish(self, r):
        if r == 0:
            if self.lsem is not None:
                self.load().wait()
            else:
                self.keep[...] = self.src[self.own_half()]
        self.copy(r).wait()
        n = self.list[r][1]
        rows = self.span(self.offset(r), n)
        got = self.rcv[self.places[r] : self.places[r] + n]
        both = self.keep[rows].astype(F32) + got.astype(F32)
        self.keep[rows] = both.astype(self.keep.dtype)

    def rest(self):
        for r in range(4, self.bits):
            self.start(r)
            self.finish(r)

    def piece(self):
        return self.keep[self.span(self.offset(3), self.list[3][1])]


class Doubling:
    def __init__(self, piece, out, top, ssem, rsem, rows=None, at=0):
        self.piece, self.out, self.top, self.at = piece, out, top, at
        self.ssem, self.rsem = ssem, rsem
        self.rows = rows or out.shape[0]

    def held(self, bit):
        at = -self.at
        for b in range(bit + 1):
            at = at + peer_of(b)[0] * (self.rows >> (b + 1))
        n = self.rows >> (bit + 1)
        return pl.ds(pl.multiple_of(at, 8 if self.out.dtype == F32 else 16), n)

    def load(self):
        self.out[self.held(self.top)] = self.piece[...]

    def copy(self, bit):
        rows = self.out.at[self.held(bit)]
        return remote(rows, rows, self.ssem.at[bit], self.rsem.at[bit], blk=peer_of(bit)[1])

    def start(self, bit):
        self.copy(bit).start()

    def finish(self, bit):
        self.copy(bit).wait()


class Reduction:
    def __init__(self, halving, doubling):
        self.halving, self.doubling = halving, doubling
        self.count = 5 + doubling.top

    def start(self):
        self.halving.start(0)

    def advance(self, k):
        if k < 3:
            self.halving.finish(k)
            self.halving.start(k + 1)
        elif k == 3:
            self.halving.finish(3)
            self.halving.rest()
            self.doubling.out[self.doubling.held(self.doubling.top)] = self.halving.piece()
            self.doubling.start(self.doubling.top)
        else:
            bit = self.doubling.top - (k - 4)
            self.doubling.finish(bit)
            if bit:
                self.doubling.start(bit - 1)


class Gathering:
    def __init__(self, doubling):
        self.doubling = doubling
        self.count = 1 + doubling.top

    def start(self):
        self.doubling.load()
        self.doubling.start(self.doubling.top)

    def advance(self, k):
        bit = self.doubling.top - k
        self.doubling.finish(bit)
        if bit:
            self.doubling.start(bit - 1)


def attended(step):
    return jnp.where(step >= 3, step - 2, jnp.maximum(step - 1, 0))


def unattend_kernel(
    place, pool, m1, m2, tab, hot, lse, gn_i, hid, cot, mo, mp, wo, wop, g2, gwr_h, gwe_h, gnb,
    gp_o, gext_o, gh_o, gwo_o, sums_o, pos_o, gwr_o, gwe_o,
    kv, s_scr, d_scr, p_scr, ds_scr, dq_t, dkv, dl, gwo_s, gwo_p, gwo_c, gwo_m, gwo_x, gwo_y,
    gms, gmb, gmr, gext, ka_s, kr_s, kb_s, ke_s, gnr,
    m_snd, m_rcv, w_snd, w_rcv, b_snd, b_rcv, f_snd, f_rcv, f_loc,
):
    step = pl.program_id(0)
    me = lax.axis_index("tp")
    core, mate = peer_of(0)
    blocks = []
    for i in range(4):
        src, keep, rcv = (gwr_h, ka_s, kr_s) if i < 2 else (gwe_h, kb_s, ke_s)
        width = src.shape[1] // 2
        src = src.at[:, (i % 2) * width : (i % 2 + 1) * width]
        blocks.append(
            Halving(src, keep.at[i % 2], rcv.at[i % 2], f_snd.at[i], f_rcv.at[i], f_loc.at[i])
        )

    def merged_copy(j):
        return remote(gmb.at[j], gmr.at[j], m_snd.at[j], m_rcv.at[j], tp=1 - me)

    def weight_mate():
        return remote(gwo_c, gwo_m, w_snd.at[0], w_rcv.at[0], blk=mate)

    def weight_peer():
        return remote(gwo_x, gwo_y, w_snd.at[1], w_rcv.at[1], tp=1 - me)

    def grad_copy():
        return remote(gnb, gnr, b_snd.at[0], b_rcv.at[0], tp=1 - me)

    @pl.when(step == 0)
    def _():
        meet(bits=range(blk_bits()))
        grad_copy().start()
        for block in blocks:
            block.start(0)
        dl[...] = jnp.zeros_like(dl)
        gwo_s[...] = jnp.zeros_like(gwo_s)
        gwo_p[...] = jnp.zeros_like(gwo_p)
        sums_o[...] = jnp.zeros_like(sums_o)
        gext[...] = jnp.zeros_like(gext)

    def unnorm(j):
        gn = gn_i[0]
        if j:
            grad_copy().wait()
            gn = gn + gnr[...].astype(F32)
        cen, r = row_stats(hid[0])
        xhat = cen * r
        sums_o[2:3, :768] += col_sum(gn * xhat)
        sums_o[3:4, :768] += col_sum(gn)
        g = gn * as_row(g2)
        mean_g = jnp.mean(g, axis=-1, keepdims=True)
        mean_gx = jnp.mean(g * xhat, axis=-1, keepdims=True)
        gh_o[0] = cot[0].astype(F32) + r * (g - mean_g - xhat * mean_gx)
        gu = gh_o[0].astype(BF16)
        gmb[j] = mm_nt(gu, wop[...]).astype(BF16)
        merged_copy(j).start()
        gms[j] = mm_nt(gu, wo[...]).astype(BF16)
        sums_o[4:5, :768] += col_sum(gu.astype(F32))
        gwo_s[...] += mm_tn(mo[0], gu)
        gwo_p[...] += mm_tn(mp[0], gu)

    @pl.when(step == 0)
    def _():
        unnorm(0)

    @pl.when(step == 2)
    def _():
        unnorm(1)
        gwo_c[...] = gwo_p[:, half_lanes(1 - core)].astype(BF16)
        weight_mate().start()

    def hook(s, h):
        if (s, h) == (3, 0):
            weight_mate().wait()
            gwo_x[...] = (gwo_p[:, half_lanes(core)] + gwo_m[...].astype(F32)).astype(BF16)
            weight_peer().start()
        for i, r in plan.get((s, h), ()):
            blocks[i].finish(r)
            if r < 3:
                blocks[i].start(r + 1)

    plan = {
        (1, 0): [(0, 0), (1, 0), (2, 0), (3, 0)],
        (3, 0): [(0, 1)],
        (3, 2): [(1, 1)],
        (3, 3): [(0, 2)],
        (4, 0): [(2, 1)],
        (4, 1): [(1, 2)],
        (4, 2): [(0, 3)],
        (4, 3): [(3, 1), (2, 2)],
        (5, 1): [(1, 3)],
        (5, 2): [(3, 2), (2, 3)],
    }
    hooks = tuple(plan)

    def backward(gm_dense):
        c = own_turn(attended(step))
        gmerged = mm(pad_matrix(), gm_dense)
        gmix = gmerged.astype(BF16)
        kv[:PAD] = pool[0, :, 384:]
        kv[PAD : PAD + MROW] = m1[0]
        kv[PAD + MROW :] = m2[0]
        mask = key_mask(place[c])
        ones = one_column()
        onehot = query_onehot()
        dq_t[:, PAD:] = jnp.zeros((384, 512 - PAD), F32)
        for h in range(4):
            for s, at in hooks:
                if at == h:
                    pl.when(step == s)(functools.partial(hook, s, h))
            feats = slice(h * HEAD_DIM, (h + 1) * HEAD_DIM)
            vfeats = slice(384 + h * HEAD_DIM, 384 + (h + 1) * HEAD_DIM)
            ka = head_keys(kv, mask, tab, h)
            qa = head_queries(pool[0, :, feats], ones, onehot)
            gm = gmix[:, feats]
            s_scr[...] = mm_nt(ka, qa)
            d_scr[...] = mm_nt(kv[:, vfeats], gm)
            low = lse[0, h : h + 1]
            inner = 0.0
            for rows in chunks():
                p = jnp.exp2(s_scr[rows] * EXP_SCALE - low)
                s_scr[rows] = p
                p_scr[rows] = p.astype(BF16)
                inner = inner + fold(p * d_scr[rows], jnp.sum)
            inner = jnp.sum(inner, axis=0, keepdims=True)
            for rows in chunks():
                ds_scr[rows] = (s_scr[rows] * (d_scr[rows] - inner)).astype(BF16)
            ds = ds_scr[...]
            dkv[:, vfeats] = mm(p_scr[...], gm)
            dka = mm(ds, qa)
            dkv[:, feats] = dka[:, :HEAD_DIM] * SCALE
            dl[h] += dka[:, 128:]
            dq_t[feats, :PAD] = mm_tn(kv[:, feats], ds) * SCALE
        gp_o[0, :, :384] = (jnp.transpose(dq_t[...])[:PAD] + gmerged).astype(BF16)
        gp_o[0, :, 384:] = dkv[:PAD].astype(BF16)
        gext[c + 1] += dkv[PAD : PAD + MROW]
        gext[c] += dkv[PAD + MROW :]

    @pl.when(step >= 4)
    def _():
        merged_copy(step - 4).wait_recv()
        gms[step - 4] = gmr[step - 4]

    @pl.when((step != 0) & (step != 2))
    def _():
        backward(gms[lax.rem(attended(step), 2)])

    @pl.when(step == 5)
    def _():
        gext_o[...] = gext[...].astype(BF16)
        weight_peer().wait()
        for j in range(2):
            merged_copy(j).wait_send()
        cols = half_lanes(core)
        gwo_s[:, cols] += gwo_y[...].astype(F32)
        gwo_o[:384] = gwo_s[:, :384].astype(BF16)
        gwo_o[384:] = gwo_s[:, 384:].astype(BF16)
        lane = iota((NT + 2 * NHW, 128), 1)
        keep = iota((32, 128), 1) < 32
        pos = jnp.zeros((NT + 2 * NHW, 128), F32)
        for h in range(4):
            dtab = lax.dot_general(
                key_onehot(F32), dl[h], TN_DIMS,
                precision=lax.Precision.HIGHEST, preferred_element_type=F32,
            )
            hits = jnp.sum(hot[...] * jnp.where(keep, dtab, 0.0)[None], axis=1)
            pos = jnp.where(lane == h, jnp.sum(hits, axis=-1, keepdims=True), pos)
        pos = jnp.concatenate([pos, jnp.zeros((128 - pos.shape[0], 128), F32)], 0)
        pos_o[...] = jnp.transpose(pos)[:8]
        blocks[3].finish(3)
        for i, block in enumerate(blocks):
            block.rest()
            (gwr_o if i < 2 else gwe_o)[i % 2] = block.piece()


def unattend_call(
    place, pool, ext, tab, hot, lse, gn, hid, cot, mo, mp, wo, wop, g2, gwr, gwe, gnb
):
    ff = gwe.shape[1]
    bits = blk_bits()

    def at(*shape, by=0):
        rest = (0,) * len(shape)
        return pl.BlockSpec(
            (1,) + shape, lambda s: (own_turn(attended(s)) + by,) + rest
        )

    def own(*shape):
        rest = (0,) * len(shape)
        return pl.BlockSpec((1,) + shape, lambda s: (jnp.minimum(s, 1),) + rest)

    def clip(*shape):
        rest = (0,) * len(shape)
        return pl.BlockSpec((1,) + shape, lambda s: (own_turn(jnp.minimum(s, 1)),) + rest)

    return pl.pallas_call(
        unattend_kernel,
        grid=(6,),
        in_specs=[
            IN_SMEM,
            at(PAD, 1152),
            at(MROW, 768, by=1),
            at(MROW, 768),
            whole((4, 32, 128)),
            whole(hot.shape),
            at(4, PAD),
            own(TOK, 768),
            own(TOK, 768),
            clip(TOK, 768),
            clip(TOK, 384),
            clip(TOK, 384),
            whole((384, 768)),
            whole((384, 768)),
            whole((768,)),
            HBM,
            HBM,
            whole((TOK, 768)),
        ],
        out_specs=[
            at(PAD, 1152),
            whole((6, MROW, 768)),
            own(TOK, 768),
            whole((768, 384)),
            whole((8, 1152)),
            whole((8, 128)),
            whole((2, ff // 16, 384)),
            whole((2, 48, ff // 2)),
        ],
        out_shape=[
            jax.ShapeDtypeStruct((4, PAD, 1152), BF16),
            jax.ShapeDtypeStruct((6, MROW, 768), BF16),
            jax.ShapeDtypeStruct((2, TOK, 768), F32),
            jax.ShapeDtypeStruct((768, 384), BF16),
            jax.ShapeDtypeStruct((8, 1152), F32),
            jax.ShapeDtypeStruct((8, 128), F32),
            jax.ShapeDtypeStruct((2, ff // 16, 384), BF16),
            jax.ShapeDtypeStruct((2, 48, ff // 2), BF16),
        ],
        scratch_shapes=[
            pltpu.VMEM((KROWS, 768), BF16),
            pltpu.VMEM((KROWS, PAD), F32),
            pltpu.VMEM((KROWS, PAD), F32),
            pltpu.VMEM((KROWS, PAD), BF16),
            pltpu.VMEM((KROWS, PAD), BF16),
            pltpu.VMEM((384, 512), F32),
            pltpu.VMEM((KROWS, 768), F32),
            pltpu.VMEM((4, KROWS, 128), F32),
            pltpu.VMEM((384, 768), F32),
            pltpu.VMEM((384, 768), F32),
        ]
        + [pltpu.VMEM((384, 384), BF16)] * 4
        + [pltpu.VMEM((2, TOK, 384), BF16)] * 3
        + [
            pltpu.VMEM((6, MROW, 768), F32),
            pltpu.VMEM((2, ff // 2, 384), BF16),
            pltpu.VMEM((2, slots(ff, bits)[0], 384), BF16),
            pltpu.VMEM((2, 384, ff // 2), BF16),
            pltpu.VMEM((2, slots(768, bits)[0], ff // 2), BF16),
            pltpu.VMEM((TOK, 768), BF16),
        ]
        + [DMA((2,))] * 4
        + [DMA((1,))] * 2
        + [DMA((4, bits))] * 2
        + [DMA((4,))],
        compiler_params=params(collective_id=2, has_side_effects=True),
        cost_estimate=cost(18, 30),
        name="unattend",
    )(
        place, pool, ext, ext, tab, hot, lse, gn, hid, cot, mo, mp, wo, wop, g2, gwr, gwe, gnb
    )


SMALL_ROWS = 64


def back_kernel(
    gp, gext, proj, pool, x, gh, w, taps, mtaps, gain, shift, fd, fp, gd, tw, ta,
    gwr_p, gwe_p, gwo, bp, gbe, gbr, pos, sums2,
    own_o, recv_o, sum_o, sump_o, br_o, red_o, small_o, gwr_o, gwe_o,
    h_s, c_s, zf_s, gwb, normed_t, dense_s, rows_s, wcat, gm_s, back, z_s, peer_s, br_s,
    gwr_s, gwe_s, small_s, nsnd, nrcv,
    kq, kk, kv, ko, ks, rq, rk, rv, ro, rs, fin, fin_s,
    b_snd, b_rcv, n_snd, n_rcv, t_snd, t_rcv, f_snd, f_rcv,
    x_snd, x_rcv, s_snd, s_rcv, d_snd, d_rcv, o_sem,
):
    step = pl.program_id(0)
    me = lax.axis_index("tp")
    blk = lax.axis_index("blk")
    peers = lax.axis_size("blk")
    mine, theirs = half_lanes(me), half_lanes(1 - me)

    blocks = []
    for i in range(4):
        piece, out = (gwr_p, gwr_s) if i < 2 else (gwe_p, gwe_s)
        width = out.shape[1] // 2
        out = out.at[:, (i % 2) * width : (i % 2 + 1) * width]
        blocks.append(Gathering(Doubling(piece.at[i % 2], out, 3, f_snd.at[i], f_rcv.at[i])))

    def late(i, src, keep, rcv, out, levels=4):
        return Reduction(
            Halving(src, keep, rcv, s_snd.at[i], s_rcv.at[i], levels=levels),
            Doubling(None, out, levels - 1, d_snd.at[i], d_rcv.at[i]),
        )

    parts = [
        late(0, gwb.at[0], kq, rq, fin.at[0]),
        late(1, gwb.at[1], kk, rk, fin.at[1]),
        late(2, gwb.at[2], kv, rv, fin.at[2]),
    ]
    output = late(3, gwo, ko, ro, fin.at[3])
    small = late(4, small_s, ks, rs, fin_s, levels=3)

    def back_copy(j):
        return remote(
            gext.at[j], back.at[j], b_snd.at[j], b_rcv.at[j],
            blk=lax.rem(blk + peers - 1, peers),
        )

    def norm_copy(i):
        return remote(peer_s.at[i], recv_o.at[i], n_snd.at[i], n_rcv.at[i], tp=1 - me)

    def sum_copy():
        return remote(sum_o, sump_o, t_snd.at[0], t_rcv.at[0], tp=1 - me)

    def branch_copy():
        return remote(bp, br_s, x_snd.at[0], x_rcv.at[0], tp=1 - me)

    def last_copy():
        return remote(nsnd, nrcv, x_snd.at[1], x_rcv.at[1], tp=1 - me)

    outs = [
        pltpu.make_async_copy(gwr_s, gwr_o, o_sem.at[0]),
        pltpu.make_async_copy(gwe_s, gwe_o, o_sem.at[1]),
        pltpu.make_async_copy(br_s, br_o, o_sem.at[2]),
    ]

    @pl.when(step == 0)
    def _():
        meet(bits=range(blk_bits()), ring=True)
        for block in blocks:
            block.start()
        output.start()
        branch_copy().start()

    @pl.when((step == 0) & (blk > 0))
    def _():
        back_copy(0).start()
        back_copy(1).start()

    @pl.when(step == 0)
    def _():
        tap_spectra(tw, taps, h_s)
        rows_s[...] = jnp.zeros_like(rows_s)
        small_s[...] = jnp.zeros_like(small_s)
        for i in range(3):
            wcat[:, i * 384 : i * 384 + 384] = w[i]
        for c in range(4):
            gm_s[c] = gext[c + 2].astype(F32)
            cen, r = row_stats(x[c].astype(F32))
            normed = cen * r * as_row(gain) + as_row(shift)
            normed_t[c] = jnp.transpose(normed).astype(BF16)

    @pl.when((step == 1) & (blk < peers - 1))
    def _():
        for j in range(2):
            back_copy(j).wait_recv()
            gm_s[2 + j] += back[j].astype(F32)

    f0, f1, f2, f3 = blocks
    pq, pk, pv = parts
    plan = {
        (0, 1): [(output, 0)],
        (0, 2): [(f0, 0)],
        (0, 3): [(f1, 0), (output, 1)],
        (1, 0): [(f0, 1)],
        (1, 1): [(f2, 0), (output, 2), (pq, 0)],
        (1, 2): [(f1, 1), (f3, 0)],
        (1, 3): [(output, 3), (f2, 1)],
        (2, 0): [(f0, 2)],
        (2, 1): [(output, 4), (f3, 1), (pk, 0)],
        (2, 2): [(pq, 1), (f1, 2)],
        (2, 3): [(pq, 2), (output, 5)],
        (3, 0): [(f0, 3)],
        (3, 1): [(pq, 3), (pv, 0), (f2, 2)],
        (3, 2): [(pk, 1), (f1, 3)],
        (3, 3): [(pq, 4), (f2, 3)],
    }

    def hook(s, c):
        for stream, k in plan.get((s, c), ()):
            stream.advance(k)

    def part_step(i, with_memory):
        lanes = pl.ds(pl.multiple_of(i * 384, 128), 384)
        hr, hi = h_s[:FREQ, lanes], h_s[FREQ:, lanes]
        total = 0.0
        for c in range(4):
            for s in (1, 2) if with_memory else (0,):
                pl.when(step == s)(functools.partial(hook, s, c))
            grad = gp[c]
            if with_memory:
                mlanes = pl.ds(pl.multiple_of((i - 1) * 384, 128), 384)
                gm = gm_s[c, :, mlanes].reshape(2, 56, 384)
                frames = grad.astype(F32).reshape(CT, 56, 384)
                pooled = pool[c].astype(F32).reshape(CT, 56, 384)
                sums = []
                for u in range(KC):
                    hit = gm[0] * pooled[u] + gm[1] * pooled[KC + u]
                    small_s[28 + u : 29 + u, mlanes] += col_sum(hit)
                for t in range(CT):
                    u = t % KC
                    sums.append(frames[t] + gm[t // KC] * mtaps[i - 1, u : u + 1])
                grad = jnp.stack(sums, 0).reshape(PAD, 384).astype(BF16)
            gs = mm(fp[...], grad)
            ps = mm(fd[...], proj[c])
            zf_s[:FREQ] = (hr * gs[:FREQ] + hi * gs[FREQ:]).astype(BF16)
            zf_s[FREQ:] = (hr * gs[FREQ:] - hi * gs[:FREQ]).astype(BF16)
            real = gs[:FREQ] * ps[:FREQ] + gs[FREQ:] * ps[FREQ:]
            imag = gs[:FREQ] * ps[FREQ:] - gs[FREQ:] * ps[:FREQ]
            c_s[:FREQ] = real if c == 0 else c_s[:FREQ] + real
            c_s[FREQ:] = imag if c == 0 else c_s[FREQ:] + imag
            dense = mm(gd[...], zf_s[...]).astype(BF16)
            dense_s[c, :, lanes] = dense
            small_s[27:28, lanes] += col_sum(dense.astype(F32))
            total = total + mm(normed_t[c], dense)
        gwb[i] = total.astype(BF16)
        high, low = two_parts(c_s[...])
        small_s[:27, lanes] = (mm(ta[...], high) + mm(ta[...], low))[:27]

    @pl.when(step == 0)
    def _():
        part_step(0, False)
        parts[0].start()

    @pl.when((step == 1) | (step == 2))
    def _():
        part_step(step, True)

    for i in (1, 2):
        pl.when(step == i)(parts[i].start)

    @pl.when(step == 3)
    def _():
        small_s[56:] = sums2[...]
        for c in range(4):
            hook(3, c)
            gn = mm_nt(dense_s[c], wcat[...])
            cen, r = row_stats(x[c].astype(F32))
            xhat = cen * r
            g = gn * as_row(gain)
            z_s[...] = r * g + jnp.where(c // 2 == me, gh[c % 2], 0.0)
            peer_s[c] = z_s[:, theirs].astype(BF16)
            norm_copy(c).start()
            own_o[c] = z_s[:, mine].astype(BF16)
            first_sum = jnp.sum(g, axis=-1, keepdims=True)
            second_sum = jnp.sum(g * xhat, axis=-1, keepdims=True)
            lane = iota((TOK, 128), 1)
            pair = jnp.where(lane == 0, first_sum, jnp.where(lane == 1, second_sum, 0.0))
            rows_s[:TOK] = pair
            sum_o[c] = jnp.transpose(rows_s[...])[:8]
            small_s[56:57, :768] += col_sum(gn * xhat)
            small_s[57:58, :768] += col_sum(gn)
        sum_copy().start()
        half = gbe.shape[1] // 2
        small_s[32:33, :half] = gbe[:, :half]
        small_s[33:34, :half] = gbe[:, half:]
        small_s[34:35, :384] = gbr[...]
        small_s[40:48, :128] = pos[...]
        small.start()

        done = {}
        for jobs in plan.values():
            for stream, k in jobs:
                done[id(stream)] = k + 1
        streams = [f3, output, pq, pk, pv, small, f0, f1, f2]
        left = [list(range(done.get(id(t), 0), t.count)) for t in streams]
        while any(left):
            for stream, todo in zip(streams, left):
                if todo:
                    stream.advance(todo.pop(0))
        for t in outs[:2]:
            t.start()
        nsnd[...] = fin_s[56:]
        last_copy().start()
        branch_copy().wait()
        outs[2].start()
        red_o[...] = fin[...]
        small_o[...] = fin_s[...]
        for i in range(4):
            norm_copy(i).wait()
        sum_copy().wait()
        last_copy().wait()
        small_o[56:] = nsnd[...] + nrcv[...]
        for t in outs:
            t.wait()

    @pl.when((step == 3) & (blk > 0))
    def _():
        back_copy(0).wait_send()
        back_copy(1).wait_send()


def back_call(
    gp, gext, proj, pool, x, gh, w, taps, mtaps, gain, shift, fd, fp, gd, tw, ta,
    gwr, gwe, gwo, bp, gbe, gbr, pos, sums2,
):
    ff = 2 * gwe.shape[2]
    bits = blk_bits()

    def third(rows):
        return pl.BlockSpec((4, rows, 384), lambda s: (0, 0, jnp.minimum(s, 2)))

    def stream(rows, cols, dtype, levels=4):
        keep = pltpu.VMEM((rows // 2, cols), dtype)
        return keep, pltpu.VMEM((slots(rows, bits, levels)[0], cols), dtype)

    kept, got = zip(*[stream(768, 384, BF16)] * 4 + [stream(SMALL_ROWS, 1152, F32, 3)])
    return pl.pallas_call(
        back_kernel,
        grid=(4,),
        in_specs=[third(PAD), whole((6, MROW, 768)), third(TOK), third(PAD)]
        + whole_like(x, gh, w, taps, mtaps, gain, shift, fd, fp, gd, tw, ta)
        + whole_like(gwr, gwe, gwo, bp, gbe, gbr, pos, sums2),
        out_specs=[
            whole((4, TOK, 384)),
            HBM,
            whole((4, 8, 512)),
            HBM,
            HBM,
            whole((4, 768, 384)),
            whole((SMALL_ROWS, 1152)),
            HBM,
            HBM,
        ],
        out_shape=[
            jax.ShapeDtypeStruct((4, TOK, 384), BF16),
            jax.ShapeDtypeStruct((4, TOK, 384), BF16),
            jax.ShapeDtypeStruct((4, 8, 512), F32),
            jax.ShapeDtypeStruct((4, 8, 512), F32),
            jax.ShapeDtypeStruct((4, TOK, 384), BF16),
            jax.ShapeDtypeStruct((4, 768, 384), BF16),
            jax.ShapeDtypeStruct((SMALL_ROWS, 1152), F32),
            jax.ShapeDtypeStruct((ff, 768), BF16),
            jax.ShapeDtypeStruct((768, ff), BF16),
        ],
        scratch_shapes=[
            pltpu.VMEM((2 * FREQ, 1152), F32),
            pltpu.VMEM((2 * FREQ, 384), F32),
            pltpu.VMEM((2 * FREQ, 384), BF16),
            pltpu.VMEM((3, 768, 384), BF16),
            pltpu.VMEM((4, 768, TOK), BF16),
            pltpu.VMEM((4, TOK, 1152), BF16),
            pltpu.VMEM((512, 128), F32),
            pltpu.VMEM((768, 1152), BF16),
            pltpu.VMEM((4, MROW, 768), F32),
            pltpu.VMEM((2, MROW, 768), BF16),
            pltpu.VMEM((TOK, 768), F32),
            pltpu.VMEM((4, TOK, 384), BF16),
            pltpu.VMEM((4, TOK, 384), BF16),
            pltpu.VMEM((ff, 768), BF16),
            pltpu.VMEM((768, ff), BF16),
            pltpu.VMEM((SMALL_ROWS, 1152), F32),
            pltpu.VMEM((8, 1152), F32),
            pltpu.VMEM((8, 1152), F32),
            *kept,
            *got,
            pltpu.VMEM((4, 768, 384), BF16),
            pltpu.VMEM((SMALL_ROWS, 1152), F32),
        ]
        + [DMA((2,))] * 2
        + [DMA((4,))] * 2
        + [DMA((1,))] * 2
        + [DMA((4, 4))] * 2
        + [DMA((2,))] * 2
        + [DMA((5, bits))] * 2
        + [DMA((5, 4))] * 2
        + [DMA((3,))],
        compiler_params=params(collective_id=3, has_side_effects=True),
        cost_estimate=cost(12, 25),
        name="back",
    )(
        gp, gext, proj, pool, x, gh, w, taps, mtaps, gain, shift, fd, fp, gd, tw, ta,
        gwr, gwe, gwo, bp, gbe, gbr, pos, sums2,
    )


def final_kernel(
    own, recv, sums, sums_p, x, gain, res, br, red, redl, redr, gwr, gwe, small,
    gin_o, out_o, gw_o, gwo_o, gwr_o, gwe_o, gt_o, gb_o, gmt_o, pos_o,
    gbo_o, gg1_o, gs1_o, gg2_o, gs2_o, gbe_o, gbr_o,
    xs, rows_s,
):
    me = lax.axis_index("tp")
    mine = half_lanes(me)
    rows_s[8:] = jnp.zeros((120, 512), F32)
    rows_s[:8] = (sums[0] + sums_p[0]) * (1.0 / 768)
    total = jnp.transpose(rows_s[...])[:TOK]
    cen, r = row_stats(x[0].astype(F32))
    xs[...] = cen * (r * r)
    z = own[0].astype(F32) + recv[0].astype(F32)
    gin_o[0] = z - r * total[:, 0:1] - xs[:, mine] * total[:, 1:2]
    out_o[0] = (res[0] + br[0].astype(F32)).astype(BF16)
    gw_o[...] = red[...].astype(F32)
    gwo_o[:, :384] = redl[0].astype(F32)
    gwo_o[:, 384:] = redr[0].astype(F32)
    gwr_o[...] = gwr[...].astype(F32)
    gwe_o[...] = gwe[...].astype(F32)

    @pl.when(pl.program_id(0) == 3)
    def _():
        for i in range(3):
            cols = slice(i * 384, i * 384 + 384)
            gt_o[i] = small[:27, cols]
            gb_o[i : i + 1] = small[27:28, cols]
            if i < 2:
                gmt_o[i] = small[28:32, cols]
        pos_o[...] = small[40:44, : NT + 2 * NHW]
        gbo_o[...] = small[60:61, mine].reshape(384)
        for row, ref in ((56, gg1_o), (57, gs1_o), (58, gg2_o), (59, gs2_o)):
            ref[...] = small[row : row + 1, :768].reshape(768)
        half = gbe_o.shape[0] // 2
        gbe_o[:half] = small[32:33, :half].reshape(half)
        gbe_o[half:] = small[33:34, :half].reshape(half)
        gbr_o[...] = small[34:35, :384].reshape(384)


def final_call(own, recv, sums, sums_p, x, gain, res, br, red, gwr, gwe, small):
    ff = gwe.shape[1]

    def flat(*shape):
        return jax.ShapeDtypeStruct(shape, F32)

    vectors = [(384,), (768,), (768,), (768,), (768,), (ff,), (384,)]
    tables = [(3, 27, 384), (3, 384), (2, KC, 384), (4, NT + 2 * NHW)]

    def rows(n, width):
        return pl.BlockSpec((n, width), lambda c: (c, 0))

    return pl.pallas_call(
        final_kernel,
        grid=(4,),
        in_specs=[
            per_clip(TOK, 384),
            per_clip(TOK, 384),
            per_clip(8, 512),
            per_clip(8, 512),
            per_clip(TOK, 768),
            whole((768,)),
            per_clip(TOK, 384),
            per_clip(TOK, 384),
            pl.BlockSpec((3, 192, 384), lambda c: (0, c, 0)),
            pl.BlockSpec((1, 96, 384), lambda c: (3, c, 0)),
            pl.BlockSpec((1, 96, 384), lambda c: (3, c + 4, 0)),
            rows(ff // 4, 768),
            rows(192, ff),
            whole((64, 1152)),
        ],
        out_specs=[
            per_clip(TOK, 384),
            per_clip(TOK, 384),
            pl.BlockSpec((3, 192, 384), lambda c: (0, c, 0)),
            rows(96, 768),
            rows(ff // 4, 768),
            rows(192, ff),
        ]
        + [whole(s) for s in tables + vectors],
        out_shape=[
            flat(4, TOK, 384),
            jax.ShapeDtypeStruct((4, TOK, 384), BF16),
            flat(3, 768, 384),
            flat(384, 768),
            flat(ff, 768),
            flat(768, ff),
        ]
        + [flat(*s) for s in tables + vectors],
        scratch_shapes=[pltpu.VMEM((TOK, 768), F32), pltpu.VMEM((128, 512), F32)],
        compiler_params=params(),
        cost_estimate=cost(0.1, 40),
        name="final",
    )(own, recv, sums, sums_p, x, gain, res, br, red, red, red, gwr, gwe, small)


def local(
    layer_input,
    first_gain,
    first_shift,
    project_weight,
    project_bias,
    pool_taps,
    memory_taps,
    position_bias,
    output_weight,
    output_bias,
    second_gain,
    second_shift,
    expand_weight,
    expand_bias,
    reduce_weight,
    reduce_bias,
    cotangent,
    clip_place,
):
    clips = layer_input.shape[0] // TOK
    half = layer_input.shape[1]

    def clipwise(a):
        return a.reshape(clips, TOK, a.shape[-1])

    w = jnp.transpose(project_weight, (1, 0, 2))
    hot = jnp.asarray(table_onehot())
    fd, fp, gd, gpad, tw, ta = fourier_tables()
    (
        pool, proj, x, ext, lse, wop, tab, mo, mp, hid, cot, gn, res, bpeer,
        gwr, gwe, gbe, gbr, gnb,
    ) = front_call(
        clip_place, position_bias, clipwise(layer_input), clipwise(cotangent),
        output_weight, output_bias, first_gain, first_shift, w, project_bias, pool_taps,
        memory_taps, hot, fd, gpad, tw, second_gain, second_shift, expand_weight, expand_bias,
        reduce_weight, reduce_bias,
    )
    gp, gext, gh, gwo, sums2, pos, gwr, gwe = unattend_call(
        clip_place, pool, ext, tab, hot, lse, gn, hid, cot, mo, mp, output_weight, wop,
        second_gain, gwr, gwe, gnb,
    )
    own, recv, sums, sums_p, br, red, small, gwr, gwe = back_call(
        gp, gext, proj, pool, x, gh, w, pool_taps, memory_taps, first_gain, first_shift,
        fd, fp, gd, tw, ta, gwr, gwe, gwo, bpeer, gbe, gbr, pos, sums2,
    )
    (
        gin, result, gw, gwo, gwr, gwe, gt, gb, gmt, pos, gbo, gg1, gs1, gg2, gs2, gbe, gbr
    ) = final_call(own, recv, sums, sums_p, x, first_gain, res, br, red, gwr, gwe, small)
    return (
        result.reshape(clips * TOK, half),
        gin.reshape(clips * TOK, half),
        gg1,
        gs1,
        jnp.transpose(gw, (1, 0, 2)),
        gb,
        gt,
        gmt,
        pos,
        gwo,
        gbo,
        gg2,
        gs2,
        gwe,
        gbe,
        gwr,
        gbr,
    )


def solution(mesh):
    return jax.shard_map(
        local,
        mesh=mesh,
        in_specs=(
            P("blk", "tp"),
            P(),
            P(),
            P(None, None, "tp"),
            P(None, "tp"),
            P(None, None, "tp"),
            P(None, None, "tp"),
            P("tp", None),
            P("tp", None),
            P("tp"),
            P(),
            P(),
            P(None, "tp"),
            P("tp"),
            P("tp", None),
            P("tp"),
            P("blk", "tp"),
            P("blk"),
        ),
        out_specs=(
            P("blk", "tp"),
            P("blk", "tp"),
            P(),
            P(),
            P(None, None, "tp"),
            P(None, "tp"),
            P(None, None, "tp"),
            P(None, None, "tp"),
            P("tp", None),
            P("tp", None),
            P("tp"),
            P(),
            P(),
            P(None, "tp"),
            P("tp"),
            P("tp", None),
            P("tp"),
        ),
        check_vma=False,
    )
```

```python
import functools

import jax
import jax.numpy as jnp
import numpy as np
from jax import lax
from jax.experimental import pallas as pl
from jax.experimental.pallas import tpu as pltpu
from jax.sharding import PartitionSpec as P

HEAD_DIM = 96
CT = 8
CS = 7
KC = 4
KT = 12
NT = 19
NHW = 13
TOK = 392
PAD = 448
MROW = 112
KROWS = 672
EPS = 1e-06
SCALE = HEAD_DIM ** (-0.5)
LOG2E = 1.4426950408889634
EXP_SCALE = SCALE * LOG2E
NEG = -1e30
VMEM = 61 << 20
F32 = jnp.float32
BF16 = jnp.bfloat16

NT_DIMS = (((1,), (1,)), ((), ()))
TN_DIMS = (((0,), (0,)), ((), ()))


def mm(a, b):
    return jnp.dot(a, b, preferred_element_type=F32)


def mm_nt(a, b):
    return lax.dot_general(a, b, NT_DIMS, preferred_element_type=F32)


def mm_tn(a, b):
    return lax.dot_general(a, b, TN_DIMS, preferred_element_type=F32)


def iota(shape, dim):
    return lax.broadcasted_iota(jnp.int32, shape, dim)


def pad_matrix():
    row = iota((PAD, TOK), 0)
    col = iota((PAD, TOK), 1)
    x = lax.bitwise_and(row, 7)
    line = lax.shift_right_logical(row, 3)
    return jnp.where((x < CS) & (col == line * CS + x), 1.0, 0.0).astype(BF16)


def query_onehot():
    row = iota((PAD, 128), 0)
    col = iota((PAD, 128), 1)
    x = lax.bitwise_and(row, 7)
    line = lax.shift_right_logical(row, 3)
    t = lax.div(line, CS)
    y = line - t * CS
    c = lax.bitwise_and(col, 31)
    hit = (c == t) | (c == 8 + y) | ((c == 15 + x) & (x < CS))
    return jnp.where(hit & (col < 64), 1.0, 0.0).astype(BF16)


def key_onehot(dtype=BF16):
    row = iota((KROWS, 32), 0)
    col = iota((KROWS, 32), 1)
    x = lax.bitwise_and(row, 7)
    line = lax.shift_right_logical(row, 3)
    t = lax.div(line, CS)
    y = line - t * CS
    hit = (col == t) | (col == 12 + y) | ((col == 19 + x) & (x < CS))
    return jnp.where(hit, 1.0, 0.0).astype(dtype)


def key_mask(place):
    row = iota((KROWS, 32), 0)
    col = iota((KROWS, 32), 1)
    x = lax.bitwise_and(row, 7)
    need = jnp.where(row < PAD, 0, jnp.where(row < PAD + MROW, 1, 2))
    bad = (x == CS) | (place < need)
    return jnp.where(bad & (col == 0), NEG, 0.0).astype(BF16)


def one_column():
    return jnp.where(iota((PAD, 32), 1) == 0, 1.0, 0.0).astype(BF16)


def table_onehot():
    out = np.zeros((NT + 2 * NHW, 32, 128), np.float32)
    for t2 in range(KT):
        for t in range(CT):
            out[t - t2 + CT - 1 if t2 < CT else t2 + CT - 1, t2, t] = 1
    for a2 in range(CS):
        for a in range(CS):
            out[NT + a - a2 + CS - 1, 12 + a2, 8 + a] = 1
            out[NT + NHW + a - a2 + CS - 1, 19 + a2, 15 + a] = 1
    out[:, :, 32:64] = out[:, :, :32]
    return out


FREQ = 304
GRID = (9, 8, 8)


def frequencies():
    alone, paired, seen = [], [], set()
    for t in range(9):
        for y in range(8):
            for x in range(8):
                other = (-t % 9, -y % 8, -x % 8)
                if (t, y, x) not in seen:
                    (alone if other == (t, y, x) else paired).append((t, y, x))
                    seen.update(((t, y, x), other))
    return np.array(alone + paired), len(alone)


def waves(points):
    freq, _ = frequencies()
    angle = 2 * np.pi * (freq[:, None, :] * points[None, :, :] / np.array(GRID)).sum(-1)
    out = np.zeros((2 * FREQ, len(points)))
    out[: len(freq)] = np.cos(angle)
    out[FREQ : FREQ + len(freq)] = np.sin(angle)
    return out


def fourier_tables():
    freq, alone = frequencies()
    tokens = np.array([(t, y, x) for t in range(CT) for y in range(CS) for x in range(CS)])
    shifts = np.array([(a - 1, b - 1, e - 1) for a in range(3) for b in range(3) for e in range(3)])
    sign = np.ones((2 * FREQ, 1))
    sign[FREQ:] = -1
    weight = np.zeros((2 * FREQ, 1))
    for start in (0, FREQ):
        weight[start : start + alone] = 1
        weight[start + alone : start + len(freq)] = 2
    ahead = waves(tokens) * sign
    padded = np.zeros((2 * FREQ, PAD))
    padded[:, [r for r in range(PAD) if r % 8 < CS]] = ahead
    taps = np.zeros((2 * FREQ, 32))
    taps[:, :27] = waves(shifts)
    scale = 1.0 / np.prod(GRID)
    high, low = two_parts(taps * scale)
    return (
        jnp.asarray(ahead, BF16),
        jnp.asarray(padded, BF16),
        jnp.asarray((ahead * weight).T, BF16),
        jnp.asarray((padded * weight).T, BF16),
        jnp.asarray(np.concatenate([high, high, low, low], 1)),
        jnp.asarray((taps * sign * weight * scale).T, BF16),
    )


def two_parts(a):
    xp = np if isinstance(a, np.ndarray) else jnp
    high = a.astype(BF16)
    return high, (a - high.astype(xp.float32)).astype(BF16)


def tap_spectra(tapwaves, taps, h_s):
    for i in range(3):
        high, low = two_parts(jnp.concatenate([taps[i], jnp.zeros((5, 384), F32)], 0))
        parts = jnp.concatenate([high, low, high, low], 0)
        h_s[:, i * 384 : i * 384 + 384] = mm(tapwaves[...], parts)


def bias_tables(pos, hot, tab_o):
    col = iota((32, 128), 1)
    for h in range(4):
        table = 0.0
        for e in range(NT + 2 * NHW):
            table = table + pos[h, e] * hot[e]
        table = table * (HEAD_DIM**0.5)
        high = table.astype(BF16)
        low = (table - high.astype(F32)).astype(BF16)
        tab_o[h] = jnp.where(col < 32, high, low)


def row_stats(x):
    mean = jnp.mean(x, axis=-1, keepdims=True)
    cen = x - mean
    var = jnp.mean(cen * cen, axis=-1, keepdims=True)
    return cen, lax.rsqrt(var + EPS)


def col_sum(x):
    return jnp.sum(x, axis=0, keepdims=True)


def as_row(ref):
    return ref[...].reshape(1, ref.shape[0])


def remote(src, dst, ssem, rsem, **where):
    return pltpu.make_async_remote_copy(
        src_ref=src, dst_ref=dst, send_sem=ssem, recv_sem=rsem,
        device_id=where, device_id_type=pl.DeviceIdType.MESH,
    )


def half_lanes(which):
    return pl.ds(pl.multiple_of(which * 384, 128), 384)


def peer_of(bit):
    blk = lax.axis_index("blk")
    mine = lax.rem(lax.div(blk, 1 << bit), 2)
    return mine, blk + (1 - 2 * mine) * (1 << bit)


def meet(bits=(), ring=False):
    barrier = pltpu.get_barrier_semaphore()
    blk = lax.axis_index("blk")
    peers = lax.axis_size("blk")
    others = [{"tp": 1 - lax.axis_index("tp")}] + [{"blk": peer_of(b)[1]} for b in bits]
    if ring:
        others += [{"blk": lax.rem(blk + by, peers)} for by in (1, peers - 1)]
    for other in others:
        pl.semaphore_signal(barrier, device_id=other, device_id_type=pl.DeviceIdType.MESH)
    pl.semaphore_wait(barrier, len(others))


def blk_bits():
    return lax.axis_size("blk").bit_length() - 1


def pool_step(c, xb, gain, shift, w, b, mtaps, fd, gp, h_s, pool_s, proj_o, ext_s, z_s):
    cen, r = row_stats(xb.astype(F32))
    normed = (cen * r * as_row(gain) + as_row(shift)).astype(BF16)
    for i in range(3):
        cols = slice(i * 384, i * 384 + 384)
        project = (mm(normed, w[i]) + b[i : i + 1]).astype(BF16)
        proj_o[0, :, cols] = project
        spec = mm(fd[...], project)
        hr, hi = h_s[:FREQ, cols], h_s[FREQ:, cols]
        z_s[i, :FREQ] = (hr * spec[:FREQ] - hi * spec[FREQ:]).astype(BF16)
        z_s[i, FREQ:] = (hr * spec[FREQ:] + hi * spec[:FREQ]).astype(BF16)
        pooled = mm(gp[...], z_s[i])
        pool_s[c, :, cols] = pooled.astype(BF16)
        if i:
            frames = pooled.reshape(CT, 56, 384)
            mcols = slice((i - 1) * 384, i * 384)
            for s in range(2):
                m = 0.0
                for u in range(KC):
                    m = m + frames[s * KC + u] * mtaps[i - 1, u : u + 1]
                ext_s[c + 2, s * 56 : s * 56 + 56, mcols] = m.astype(BF16)


def whole(shape):
    zeros = (0,) * len(shape)
    return pl.BlockSpec(shape, lambda c: zeros, pipeline_mode=pl.Buffered(1))


def per_clip(*shape):
    rest = (0,) * len(shape)
    return pl.BlockSpec((1,) + shape, lambda c: (c,) + rest)


def params(**kw):
    return pltpu.CompilerParams(vmem_limit_bytes=VMEM, **kw)


def cost(gflops, mbytes):
    return pl.CostEstimate(
        flops=int(gflops * 1e9), bytes_accessed=int(mbytes * 1e6), transcendentals=0
    )


def head_keys(kv, mask, tab, h):
    k = kv[:, h * HEAD_DIM : (h + 1) * HEAD_DIM]
    bias = mm(key_onehot(), tab[h]).astype(BF16)
    return jnp.concatenate([k, mask, bias], axis=1)


def head_queries(q, ones, onehot):
    return jnp.concatenate([q, ones, onehot], axis=1)


CHUNK = 48


def chunks():
    return [slice(j * CHUNK, j * CHUNK + CHUNK) for j in range(KROWS // CHUNK)]


def fold(x, op):
    return op(x.reshape(x.shape[0] // 8, 8, x.shape[1]), axis=0)


def attend_step(place, own, m1, m2, tab, lse_o, kv, s_scr, p_scr, mix_t):
    kv[:PAD] = own[:, 384:]
    kv[PAD : PAD + MROW] = m1[...]
    kv[PAD + MROW :] = m2[...]
    mask = key_mask(place)
    ones = one_column()
    onehot = query_onehot()
    mix_t[:, PAD:] = jnp.zeros((384, 512 - PAD), F32)
    for h in range(4):
        feats = slice(h * HEAD_DIM, (h + 1) * HEAD_DIM)
        ka = head_keys(kv, mask, tab, h)
        qa = head_queries(own[:, feats], ones, onehot)
        s_scr[...] = mm_nt(ka, qa)
        top = jnp.max(fold(s_scr[...], jnp.max), axis=0, keepdims=True) * EXP_SCALE
        total = 0.0
        for rows in chunks():
            p = jnp.exp2(s_scr[rows] * EXP_SCALE - top)
            total = total + fold(p, jnp.sum)
            p_scr[rows] = p.astype(BF16)
        total = jnp.sum(total, axis=0, keepdims=True)
        v = kv[:, 384 + h * HEAD_DIM : 384 + (h + 1) * HEAD_DIM]
        mix_t[feats, :PAD] = mm_tn(v, p_scr[...]) * (1.0 / total)
        lse_o[0, h : h + 1] = top + jnp.log2(total)
    mix = jnp.transpose(mix_t[...])[:PAD]
    merged = (mix + own[:, :384].astype(F32)).astype(BF16)
    return mm_tn(pad_matrix(), merged).astype(BF16)


FFC = 512
GWC = 384


def phi_pair(x):
    ax = jnp.abs(x) * 0.7071067811865476
    t = 1.0 / (1.0 + 0.3275911 * ax)
    e = jnp.exp(-ax * ax)
    poly = 1.061405429 * t - 1.453152027
    poly = poly * t + 1.421413741
    poly = poly * t - 0.284496736
    poly = poly * t + 0.254829592
    tail = 0.5 * poly * t * e
    return jnp.where(x >= 0, 1.0 - tail, tail), e * 0.3989422804014327


def feed_step(hid, cot, g2, s2, we, be, wr, nt_s, br_s, gn_s, gwr, gwe, gbe_o):
    cen, r = row_stats(hid)
    nt_s[...] = (cen * r * as_row(g2) + as_row(s2)).astype(BF16)
    br_s[...] = jnp.zeros_like(br_s)
    gn_s[...] = jnp.zeros_like(gn_s)

    @pl.loop(0, we.shape[1] // FFC)
    def _(j):
        cols = pl.ds(pl.multiple_of(j * FFC, FFC), FFC)
        ex = mm(nt_s[...], we[:, cols]) + be[cols].reshape(1, FFC)
        cdf, pdf = phi_pair(ex)
        act = (ex * cdf).astype(BF16)
        br_s[...] += mm(act, wr[cols, :])
        ga = mm_nt(cot[...], wr[cols, :])
        ge = (ga * (cdf + ex * pdf)).astype(BF16)
        gbe_o[:, cols] += col_sum(ge.astype(F32))
        gn_s[...] += mm_nt(ge, we[:, cols])
        gwr[cols, :] += mm_tn(act, cot[...])
        gwe[:, cols] += mm_tn(nt_s[...], ge)


def pool_turn(s):
    return lax.rem(s + 2, 4)


def own_turn(s):
    return lax.rem(s + 2 * lax.axis_index("tp"), 4)


def other_turn(s):
    return lax.rem(s + 2 + 2 * lax.axis_index("tp"), 4)


def front_kernel(
    place, pos, x_h, cot_h, wo_h, bo, gain, shift, w, b, taps, mtaps, hot, fd, gp, tw,
    wo, g2, s2, we, be, wr, br,
    pool_o, proj_o, x_o, ext_o, lse_o, wop_o, tab_o, mo_o, mp_o, hid_o, cot_o, gn_o, res_o,
    bpeer_o, gwr_o, gwe_o, gbe_o, gbr_o, gnb_o,
    xs, cs, pool_s, ext_s, mo_s, mp_s, wop_s, bo_s, h_s, z_s, kv, s_scr, p_scr, mix_t,
    nt_s, br_s, gn_s, gnb, gnr, gwr, gwe, gwb, geb,
    x_snd, x_rcv, x_loc, c_snd, c_rcv, c_loc, w_snd, w_rcv, e_snd, e_rcv,
    m_snd, m_rcv, g_snd, g_rcv, o_sem, gr_sem, ge_sem, v_snd, v_rcv,
):
    step = pl.program_id(0)
    me = lax.axis_index("tp")
    blk = lax.axis_index("blk")
    peers = lax.axis_size("blk")
    mine, theirs = half_lanes(me), half_lanes(1 - me)

    def x_copy(c):
        return remote(x_h.at[c], xs.at[c, :, mine], x_snd.at[c], x_rcv.at[c], tp=1 - me)

    def x_local(c):
        return pltpu.make_async_copy(x_h.at[c], xs.at[c, :, mine], x_loc.at[c])

    def cot_copy(c):
        return remote(cot_h.at[c], cs.at[c, :, mine], c_snd.at[c], c_rcv.at[c], tp=1 - me)

    def cot_local(c):
        return pltpu.make_async_copy(cot_h.at[c], cs.at[c, :, mine], c_loc.at[c])

    weights = Doubling(None, wop_s, 2, v_snd, v_rcv)

    def weight_copy():
        rows = weights.held(2)
        return remote(wo_h.at[rows], wop_s.at[rows], w_snd.at[0], w_rcv.at[0], tp=1 - me)

    def bias_copy():
        return remote(bo_s.at[:, mine], bo_s.at[:, mine], w_snd.at[1], w_rcv.at[1], tp=1 - me)

    def memory_copy(j):
        return remote(
            ext_s.at[4 + j], ext_s.at[j], e_snd.at[j], e_rcv.at[j],
            blk=lax.rem(blk + 1, peers),
        )

    def merged_copy(c):
        return remote(mo_s.at[c], mp_s.at[c], m_snd.at[c], m_rcv.at[c], tp=1 - me)

    def grad_copy():
        return remote(gnb.at[0], gnr, g_snd.at[0], g_rcv.at[0], tp=1 - me)

    outs = [
        pltpu.make_async_copy(pool_s, pool_o, o_sem.at[0]),
        pltpu.make_async_copy(xs, x_o, o_sem.at[1]),
        pltpu.make_async_copy(ext_s, ext_o, o_sem.at[2]),
        pltpu.make_async_copy(wop_s, wop_o, o_sem.at[3]),
        pltpu.make_async_copy(cs, cot_o, o_sem.at[4]),
        pltpu.make_async_copy(mo_s, mo_o, o_sem.at[5]),
        pltpu.make_async_copy(mp_s, mp_o, o_sem.at[6]),
    ]

    @pl.when(step == 0)
    def _():
        meet(bits=(0, 1, 2), ring=True)
        for c in (2, 3, 0, 1):
            x_copy(c).start()
            x_local(c).start()
        bo_s[:, mine] = jnp.broadcast_to(as_row(bo), (8, 384))
        gwr[...] = jnp.zeros_like(gwr)
        gwe[...] = jnp.zeros_like(gwe)
        gbe_o[...] = jnp.zeros_like(gbe_o)
        gbr_o[...] = jnp.zeros_like(gbr_o)
        bias_tables(pos, hot, tab_o)
        tap_spectra(tw, taps, h_s)

    @pl.when((step == 0) & (blk == 0))
    def _():
        ext_s[:2] = jnp.zeros((2, MROW, 768), BF16)

    @pl.when(step < 4)
    def _():
        c = pool_turn(step)
        x_local(c).wait()
        x_copy(c).wait_recv()

        @pl.when(step == 2)
        def _():
            weight_copy().start()
            bias_copy().start()

        @pl.when(step == 3)
        def _():
            cot_copy(own_turn(0)).start()
            for t in range(4):
                cot_local(t).start()

        pool_step(c, xs[c], gain, shift, w, b, mtaps, fd, gp, h_s, pool_s, proj_o, ext_s, z_s)

        @pl.when((step < 2) & (blk < peers - 1))
        def _():
            memory_copy(step).start()

        @pl.when(step == 3)
        def _():
            outs[0].start()
            outs[1].start()

    @pl.when((step >= 4) & (step < 8))
    def _():
        c = own_turn(step)

        @pl.when((step == 4) & (blk > 0))
        def _():
            memory_copy(0).wait_recv()
            memory_copy(1).wait_recv()

        @pl.when(step < 7)
        def _():
            cot_copy(own_turn(step + 1)).start()

        mo_s[c] = attend_step(
            place[c], pool_s.at[c], ext_s.at[c + 1], ext_s.at[c], tab_o, lse_o,
            kv, s_scr, p_scr, mix_t,
        )
        merged_copy(c).start()

        @pl.when(step == 4)
        def _():
            weight_copy().wait_recv()
            weights.start(2)

        for bit in (2, 1):

            @pl.when(step == 7 - bit)
            def _():
                weights.finish(bit)
                weights.start(bit - 1)

    @pl.when(step >= 8)
    def _():
        c = other_turn(step)

        @pl.when(step == 8)
        def _():
            weights.finish(0)
            bias_copy().wait_recv()
            outs[2].start()
            outs[3].start()

        cot_local(c).wait()
        cot_copy(c).wait_recv()
        merged_copy(c).wait_recv()

        @pl.when(step == 11)
        def _():
            for t in outs[4:]:
                t.start()

        hid = xs[c].astype(F32) + mm(mo_s[c], wo[...]) + mm(mp_s[c], wop_s[...])
        hid = hid + bo_s[0:1, :]
        hid_o[0] = hid
        feed_step(hid, cs.at[c], g2, s2, we, be, wr, nt_s, br_s, gn_s, gwr, gwe, gbe_o)
        res_o[0] = hid_o[0, :, mine] + br_s[:, mine] + as_row(br)
        bpeer_o[0] = br_s[:, theirs].astype(BF16)
        gbr_o[...] += col_sum(cs[c, :, mine].astype(F32))

        @pl.when(step < 10)
        def _():
            gnb[step - 8] = gn_s[...].astype(BF16)

        @pl.when(step == 8)
        def _():
            grad_copy().start()

        @pl.when(step == 9)
        def _():
            gnb_o[...] = gnb[1]

        @pl.when(step >= 10)
        def _():
            gn_o[step - 10] = gn_s[...]

    def reduce_out(j):
        rows = slice(j * GWC, j * GWC + GWC)
        return pltpu.make_async_copy(gwb.at[j % 2], gwr_o.at[rows], gr_sem.at[j % 2])

    def expand_out(j):
        cols = slice(j * GWC, j * GWC + GWC)
        return pltpu.make_async_copy(geb.at[j % 2], gwe_o.at[:, cols], ge_sem.at[j % 2])

    @pl.when(step == 11)
    def _():
        parts = we.shape[1] // GWC
        for j in range(parts):
            if j >= 2:
                reduce_out(j - 2).wait()
                expand_out(j - 2).wait()
            cols = slice(j * GWC, j * GWC + GWC)
            gwb[j % 2] = gwr[cols].astype(BF16)
            reduce_out(j).start()
            geb[j % 2] = gwe[:, cols].astype(BF16)
            expand_out(j).start()
        for j in (parts - 2, parts - 1):
            reduce_out(j).wait()
            expand_out(j).wait()
        grad_copy().wait_recv()
        gn_o[0] += gnr[...].astype(F32)
        for c in range(4):
            x_copy(c).wait_send()
            cot_copy(c).wait_send()
            merged_copy(c).wait_send()
        for t in (weight_copy(), bias_copy(), grad_copy()):
            t.wait_send()
        for t in outs:
            t.wait()

    @pl.when((step == 11) & (blk < peers - 1))
    def _():
        memory_copy(0).wait_send()
        memory_copy(1).wait_send()


HBM = pl.BlockSpec(memory_space=pl.ANY)
IN_SMEM = pl.BlockSpec(memory_space=pltpu.SMEM)
DMA = pltpu.SemaphoreType.DMA


def whole_like(*arrays):
    return [whole(a.shape) for a in arrays]


def front_call(
    place, pos, x, cot, wo, bo, gain, shift, w, b, taps, mtaps, hot, fd, gp, tw,
    g2, s2, we, be, wr, br,
):
    ff = we.shape[1]

    def at(turn, low, high, *shape):
        rest = (0,) * len(shape)
        return pl.BlockSpec(
            (1,) + shape, lambda s: (turn(jnp.clip(s, low, high)),) + rest
        )

    def own(*shape):
        rest = (0,) * len(shape)
        return pl.BlockSpec((1,) + shape, lambda s: (jnp.clip(s - 10, 0, 1),) + rest)

    return pl.pallas_call(
        front_kernel,
        grid=(12,),
        in_specs=[IN_SMEM, IN_SMEM, HBM, HBM, HBM]
        + whole_like(bo, gain, shift, w, b, taps, mtaps, hot, fd, gp, tw, wo, g2, s2, we, be, wr, br),
        out_specs=[
            HBM,
            at(pool_turn, 0, 3, TOK, 1152),
            HBM,
            HBM,
            at(own_turn, 4, 7, 4, PAD),
            HBM,
            whole((4, 32, 128)),
            HBM,
            HBM,
            own(TOK, 768),
            HBM,
            whole((2, TOK, 768)),
            at(other_turn, 8, 11, TOK, 384),
            at(other_turn, 8, 11, TOK, 384),
            HBM,
            HBM,
            whole((1, ff)),
            whole((1, 384)),
            whole((TOK, 768)),
        ],
        out_shape=[
            jax.ShapeDtypeStruct((4, PAD, 1152), BF16),
            jax.ShapeDtypeStruct((4, TOK, 1152), BF16),
            jax.ShapeDtypeStruct((4, TOK, 768), BF16),
            jax.ShapeDtypeStruct((6, MROW, 768), BF16),
            jax.ShapeDtypeStruct((4, 4, PAD), F32),
            jax.ShapeDtypeStruct((384, 768), BF16),
            jax.ShapeDtypeStruct((4, 32, 128), BF16),
            jax.ShapeDtypeStruct((4, TOK, 384), BF16),
            jax.ShapeDtypeStruct((4, TOK, 384), BF16),
            jax.ShapeDtypeStruct((2, TOK, 768), F32),
            jax.ShapeDtypeStruct((4, TOK, 768), BF16),
            jax.ShapeDtypeStruct((2, TOK, 768), F32),
            jax.ShapeDtypeStruct((4, TOK, 384), F32),
            jax.ShapeDtypeStruct((4, TOK, 384), BF16),
            jax.ShapeDtypeStruct((ff, 768), BF16),
            jax.ShapeDtypeStruct((768, ff), BF16),
            jax.ShapeDtypeStruct((1, ff), F32),
            jax.ShapeDtypeStruct((1, 384), F32),
            jax.ShapeDtypeStruct((TOK, 768), BF16),
        ],
        scratch_shapes=[
            pltpu.VMEM((4, TOK, 768), BF16),
            pltpu.VMEM((4, TOK, 768), BF16),
            pltpu.VMEM((4, PAD, 1152), BF16),
            pltpu.VMEM((6, MROW, 768), BF16),
            pltpu.VMEM((4, TOK, 384), BF16),
            pltpu.VMEM((4, TOK, 384), BF16),
            pltpu.VMEM((384, 768), BF16),
            pltpu.VMEM((8, 768), F32),
            pltpu.VMEM((2 * FREQ, 1152), F32),
            pltpu.VMEM((3, 2 * FREQ, 384), BF16),
            pltpu.VMEM((KROWS, 768), BF16),
            pltpu.VMEM((KROWS, PAD), F32),
            pltpu.VMEM((KROWS, PAD), BF16),
            pltpu.VMEM((384, 512), F32),
            pltpu.VMEM((TOK, 768), BF16),
            pltpu.VMEM((TOK, 768), F32),
            pltpu.VMEM((TOK, 768), F32),
            pltpu.VMEM((2, TOK, 768), BF16),
            pltpu.VMEM((TOK, 768), BF16),
            pltpu.VMEM((ff, 768), F32),
            pltpu.VMEM((768, ff), F32),
            pltpu.VMEM((2, GWC, 768), BF16),
            pltpu.VMEM((2, 768, GWC), BF16),
        ]
        + [DMA((4,))] * 6
        + [DMA((3,))] * 2
        + [DMA((2,))] * 2
        + [DMA((4,))] * 2
        + [DMA((2,))] * 2
        + [DMA((7,))]
        + [DMA((2,))] * 2
        + [DMA((3,))] * 2,
        compiler_params=params(collective_id=1, has_side_effects=True),
        cost_estimate=cost(36, 60),
        name="front",
    )(
        place, pos, x, cot, wo, bo, gain, shift, w, b, taps, mtaps, hot, fd, gp, tw,
        wo, g2, s2, we, be, wr, br,
    )


def halvings(rows, bits, levels=4):
    out = []
    for bit in range(bits):
        rows = rows // 2 if bit < levels else rows
        out.append((bit, rows))
    return out


def slots(rows, bits, levels=4):
    at, places = 0, []
    for _, n in halvings(rows, bits, levels):
        places.append(at)
        at += n
    return at, places


class Halving:
    def __init__(self, src, keep, rcv, ssem, rsem, lsem=None, levels=4):
        self.src, self.keep, self.rcv = src, keep, rcv
        self.ssem, self.rsem, self.lsem = ssem, rsem, lsem
        self.bits, self.levels = blk_bits(), levels
        self.rows = src.shape[0]
        self.list = halvings(self.rows, self.bits, levels)
        self.places = slots(self.rows, self.bits, levels)[1]

    def offset(self, r):
        off = 0
        for bit, n in self.list[1 : r + 1]:
            if bit < self.levels:
                off = off + peer_of(bit)[0] * n
        return off

    def span(self, at, n):
        return pl.ds(pl.multiple_of(at, 8 if self.keep.dtype == F32 else 16), n)

    def copy(self, r):
        bit, n = self.list[r]
        mine, peer = peer_of(bit)
        if r == 0:
            src = self.src.at[self.span((1 - mine) * n, n)]
        else:
            away = self.offset(r - 1) + ((1 - mine) * n if bit < self.levels else 0)
            src = self.keep.at[self.span(away, n)]
        dst = self.rcv.at[pl.ds(self.places[r], n)]
        return remote(src, dst, self.ssem.at[r], self.rsem.at[r], blk=peer)

    def own_half(self):
        n = self.list[0][1]
        return self.span(peer_of(0)[0] * n, n)

    def load(self):
        return pltpu.make_async_copy(self.src.at[self.own_half()], self.keep, self.lsem)

    def start(self, r):
        self.copy(r).start()
        if r == 0 and self.lsem is not None:
            self.load().start()

    def finish(self, r):
        if r == 0:
            if self.lsem is not None:
                self.load().wait()
            else:
                self.keep[...] = self.src[self.own_half()]
        self.copy(r).wait()
        n = self.list[r][1]
        rows = self.span(self.offset(r), n)
        got = self.rcv[self.places[r] : self.places[r] + n]
        both = self.keep[rows].astype(F32) + got.astype(F32)
        self.keep[rows] = both.astype(self.keep.dtype)

    def rest(self):
        for r in range(4, self.bits):
            self.start(r)
            self.finish(r)

    def piece(self):
        return self.keep[self.span(self.offset(3), self.list[3][1])]


class Doubling:
    def __init__(self, piece, out, top, ssem, rsem, rows=None, at=0):
        self.piece, self.out, self.top, self.at = piece, out, top, at
        self.ssem, self.rsem = ssem, rsem
        self.rows = rows or out.shape[0]

    def held(self, bit):
        at = -self.at
        for b in range(bit + 1):
            at = at + peer_of(b)[0] * (self.rows >> (b + 1))
        n = self.rows >> (bit + 1)
        return pl.ds(pl.multiple_of(at, 8 if self.out.dtype == F32 else 16), n)

    def load(self):
        self.out[self.held(self.top)] = self.piece[...]

    def copy(self, bit):
        rows = self.out.at[self.held(bit)]
        return remote(rows, rows, self.ssem.at[bit], self.rsem.at[bit], blk=peer_of(bit)[1])

    def start(self, bit):
        self.copy(bit).start()

    def finish(self, bit):
        self.copy(bit).wait()


class Reduction:
    def __init__(self, halving, doubling):
        self.halving, self.doubling = halving, doubling
        self.count = 5 + doubling.top

    def start(self):
        self.halving.start(0)

    def advance(self, k):
        if k < 3:
            self.halving.finish(k)
            self.halving.start(k + 1)
        elif k == 3:
            self.halving.finish(3)
            self.halving.rest()
            self.doubling.out[self.doubling.held(self.doubling.top)] = self.halving.piece()
            self.doubling.start(self.doubling.top)
        else:
            bit = self.doubling.top - (k - 4)
            self.doubling.finish(bit)
            if bit:
                self.doubling.start(bit - 1)


class Gathering:
    def __init__(self, doubling):
        self.doubling = doubling
        self.count = 1 + doubling.top

    def start(self):
        self.doubling.load()
        self.doubling.start(self.doubling.top)

    def advance(self, k):
        bit = self.doubling.top - k
        self.doubling.finish(bit)
        if bit:
            self.doubling.start(bit - 1)


def attended(step):
    return jnp.where(step >= 3, step - 2, jnp.maximum(step - 1, 0))


def unattend_kernel(
    place, pool, m1, m2, tab, hot, lse, gn_i, hid, cot, mo, mp, wo, wop, g2, gwr_h, gwe_h, gnb,
    gp_o, gext_o, gh_o, gwo_o, sums_o, pos_o, gwr_o, gwe_o,
    kv, s_scr, d_scr, p_scr, ds_scr, dq_t, dkv, dl, gwo_s, gwo_p, gwo_c, gwo_m, gwo_x, gwo_y,
    gms, gmb, gmr, gext, ka_s, kr_s, kb_s, ke_s, gnr,
    m_snd, m_rcv, w_snd, w_rcv, b_snd, b_rcv, f_snd, f_rcv, f_loc,
):
    step = pl.program_id(0)
    me = lax.axis_index("tp")
    core, mate = peer_of(0)
    blocks = []
    for i in range(4):
        src, keep, rcv = (gwr_h, ka_s, kr_s) if i < 2 else (gwe_h, kb_s, ke_s)
        width = src.shape[1] // 2
        src = src.at[:, (i % 2) * width : (i % 2 + 1) * width]
        blocks.append(
            Halving(src, keep.at[i % 2], rcv.at[i % 2], f_snd.at[i], f_rcv.at[i], f_loc.at[i])
        )

    def merged_copy(j):
        return remote(gmb.at[j], gmr.at[j], m_snd.at[j], m_rcv.at[j], tp=1 - me)

    def weight_mate():
        return remote(gwo_c, gwo_m, w_snd.at[0], w_rcv.at[0], blk=mate)

    def weight_peer():
        return remote(gwo_x, gwo_y, w_snd.at[1], w_rcv.at[1], tp=1 - me)

    def grad_copy():
        return remote(gnb, gnr, b_snd.at[0], b_rcv.at[0], tp=1 - me)

    @pl.when(step == 0)
    def _():
        meet(bits=range(blk_bits()))
        grad_copy().start()
        for block in blocks:
            block.start(0)
        dl[...] = jnp.zeros_like(dl)
        gwo_s[...] = jnp.zeros_like(gwo_s)
        gwo_p[...] = jnp.zeros_like(gwo_p)
        sums_o[...] = jnp.zeros_like(sums_o)
        gext[...] = jnp.zeros_like(gext)

    def unnorm(j):
        gn = gn_i[0]
        if j:
            grad_copy().wait()
            gn = gn + gnr[...].astype(F32)
        cen, r = row_stats(hid[0])
        xhat = cen * r
        sums_o[2:3, :768] += col_sum(gn * xhat)
        sums_o[3:4, :768] += col_sum(gn)
        g = gn * as_row(g2)
        mean_g = jnp.mean(g, axis=-1, keepdims=True)
        mean_gx = jnp.mean(g * xhat, axis=-1, keepdims=True)
        gh_o[0] = cot[0].astype(F32) + r * (g - mean_g - xhat * mean_gx)
        gu = gh_o[0].astype(BF16)
        gmb[j] = mm_nt(gu, wop[...]).astype(BF16)
        merged_copy(j).start()
        gms[j] = mm_nt(gu, wo[...]).astype(BF16)
        sums_o[4:5, :768] += col_sum(gu.astype(F32))
        gwo_s[...] += mm_tn(mo[0], gu)
        gwo_p[...] += mm_tn(mp[0], gu)

    @pl.when(step == 0)
    def _():
        unnorm(0)

    @pl.when(step == 2)
    def _():
        unnorm(1)
        gwo_c[...] = gwo_p[:, half_lanes(1 - core)].astype(BF16)
        weight_mate().start()

    def hook(s, h):
        if (s, h) == (3, 0):
            weight_mate().wait()
            gwo_x[...] = (gwo_p[:, half_lanes(core)] + gwo_m[...].astype(F32)).astype(BF16)
            weight_peer().start()
        for i, r in plan.get((s, h), ()):
            blocks[i].finish(r)
            if r < 3:
                blocks[i].start(r + 1)

    plan = {
        (1, 0): [(0, 0), (1, 0), (2, 0), (3, 0)],
        (3, 0): [(0, 1)],
        (3, 2): [(1, 1)],
        (3, 3): [(0, 2)],
        (4, 0): [(2, 1)],
        (4, 1): [(1, 2)],
        (4, 2): [(0, 3)],
        (4, 3): [(3, 1), (2, 2)],
        (5, 1): [(1, 3)],
        (5, 2): [(3, 2), (2, 3)],
    }
    hooks = tuple(plan)

    def backward(gm_dense):
        c = own_turn(attended(step))
        gmerged = mm(pad_matrix(), gm_dense)
        gmix = gmerged.astype(BF16)
        kv[:PAD] = pool[0, :, 384:]
        kv[PAD : PAD + MROW] = m1[0]
        kv[PAD + MROW :] = m2[0]
        mask = key_mask(place[c])
        ones = one_column()
        onehot = query_onehot()
        dq_t[:, PAD:] = jnp.zeros((384, 512 - PAD), F32)
        for h in range(4):
            for s, at in hooks:
                if at == h:
                    pl.when(step == s)(functools.partial(hook, s, h))
            feats = slice(h * HEAD_DIM, (h + 1) * HEAD_DIM)
            vfeats = slice(384 + h * HEAD_DIM, 384 + (h + 1) * HEAD_DIM)
            ka = head_keys(kv, mask, tab, h)
            qa = head_queries(pool[0, :, feats], ones, onehot)
            gm = gmix[:, feats]
            s_scr[...] = mm_nt(ka, qa)
            d_scr[...] = mm_nt(kv[:, vfeats], gm)
            low = lse[0, h : h + 1]
            inner = 0.0
            for rows in chunks():
                p = jnp.exp2(s_scr[rows] * EXP_SCALE - low)
                s_scr[rows] = p
                p_scr[rows] = p.astype(BF16)
                inner = inner + fold(p * d_scr[rows], jnp.sum)
            inner = jnp.sum(inner, axis=0, keepdims=True)
            for rows in chunks():
                ds_scr[rows] = (s_scr[rows] * (d_scr[rows] - inner)).astype(BF16)
            ds = ds_scr[...]
            dkv[:, vfeats] = mm(p_scr[...], gm)
            dka = mm(ds, qa)
            dkv[:, feats] = dka[:, :HEAD_DIM] * SCALE
            dl[h] += dka[:, 128:]
            dq_t[feats, :PAD] = mm_tn(kv[:, feats], ds) * SCALE
        gp_o[0, :, :384] = (jnp.transpose(dq_t[...])[:PAD] + gmerged).astype(BF16)
        gp_o[0, :, 384:] = dkv[:PAD].astype(BF16)
        gext[c + 1] += dkv[PAD : PAD + MROW]
        gext[c] += dkv[PAD + MROW :]

    @pl.when(step >= 4)
    def _():
        merged_copy(step - 4).wait_recv()
        gms[step - 4] = gmr[step - 4]

    @pl.when((step != 0) & (step != 2))
    def _():
        backward(gms[lax.rem(attended(step), 2)])

    @pl.when(step == 5)
    def _():
        gext_o[...] = gext[...].astype(BF16)
        weight_peer().wait()
        for j in range(2):
            merged_copy(j).wait_send()
        cols = half_lanes(core)
        gwo_s[:, cols] += gwo_y[...].astype(F32)
        gwo_o[:384] = gwo_s[:, :384].astype(BF16)
        gwo_o[384:] = gwo_s[:, 384:].astype(BF16)
        lane = iota((NT + 2 * NHW, 128), 1)
        keep = iota((32, 128), 1) < 32
        pos = jnp.zeros((NT + 2 * NHW, 128), F32)
        for h in range(4):
            dtab = lax.dot_general(
                key_onehot(F32), dl[h], TN_DIMS,
                precision=lax.Precision.HIGHEST, preferred_element_type=F32,
            )
            hits = jnp.sum(hot[...] * jnp.where(keep, dtab, 0.0)[None], axis=1)
            pos = jnp.where(lane == h, jnp.sum(hits, axis=-1, keepdims=True), pos)
        pos = jnp.concatenate([pos, jnp.zeros((128 - pos.shape[0], 128), F32)], 0)
        pos_o[...] = jnp.transpose(pos)[:8]
        blocks[3].finish(3)
        for i, block in enumerate(blocks):
            block.rest()
            (gwr_o if i < 2 else gwe_o)[i % 2] = block.piece()


def unattend_call(
    place, pool, ext, tab, hot, lse, gn, hid, cot, mo, mp, wo, wop, g2, gwr, gwe, gnb
):
    ff = gwe.shape[1]
    bits = blk_bits()

    def at(*shape, by=0):
        rest = (0,) * len(shape)
        return pl.BlockSpec(
            (1,) + shape, lambda s: (own_turn(attended(s)) + by,) + rest
        )

    def own(*shape):
        rest = (0,) * len(shape)
        return pl.BlockSpec((1,) + shape, lambda s: (jnp.minimum(s, 1),) + rest)

    def clip(*shape):
        rest = (0,) * len(shape)
        return pl.BlockSpec((1,) + shape, lambda s: (own_turn(jnp.minimum(s, 1)),) + rest)

    return pl.pallas_call(
        unattend_kernel,
        grid=(6,),
        in_specs=[
            IN_SMEM,
            at(PAD, 1152),
            at(MROW, 768, by=1),
            at(MROW, 768),
            whole((4, 32, 128)),
            whole(hot.shape),
            at(4, PAD),
            own(TOK, 768),
            own(TOK, 768),
            clip(TOK, 768),
            clip(TOK, 384),
            clip(TOK, 384),
            whole((384, 768)),
            whole((384, 768)),
            whole((768,)),
            HBM,
            HBM,
            whole((TOK, 768)),
        ],
        out_specs=[
            at(PAD, 1152),
            whole((6, MROW, 768)),
            own(TOK, 768),
            whole((768, 384)),
            whole((8, 1152)),
            whole((8, 128)),
            whole((2, ff // 16, 384)),
            whole((2, 48, ff // 2)),
        ],
        out_shape=[
            jax.ShapeDtypeStruct((4, PAD, 1152), BF16),
            jax.ShapeDtypeStruct((6, MROW, 768), BF16),
            jax.ShapeDtypeStruct((2, TOK, 768), F32),
            jax.ShapeDtypeStruct((768, 384), BF16),
            jax.ShapeDtypeStruct((8, 1152), F32),
            jax.ShapeDtypeStruct((8, 128), F32),
            jax.ShapeDtypeStruct((2, ff // 16, 384), BF16),
            jax.ShapeDtypeStruct((2, 48, ff // 2), BF16),
        ],
        scratch_shapes=[
            pltpu.VMEM((KROWS, 768), BF16),
            pltpu.VMEM((KROWS, PAD), F32),
            pltpu.VMEM((KROWS, PAD), F32),
            pltpu.VMEM((KROWS, PAD), BF16),
            pltpu.VMEM((KROWS, PAD), BF16),
            pltpu.VMEM((384, 512), F32),
            pltpu.VMEM((KROWS, 768), F32),
            pltpu.VMEM((4, KROWS, 128), F32),
            pltpu.VMEM((384, 768), F32),
            pltpu.VMEM((384, 768), F32),
        ]
        + [pltpu.VMEM((384, 384), BF16)] * 4
        + [pltpu.VMEM((2, TOK, 384), BF16)] * 3
        + [
            pltpu.VMEM((6, MROW, 768), F32),
            pltpu.VMEM((2, ff // 2, 384), BF16),
            pltpu.VMEM((2, slots(ff, bits)[0], 384), BF16),
            pltpu.VMEM((2, 384, ff // 2), BF16),
            pltpu.VMEM((2, slots(768, bits)[0], ff // 2), BF16),
            pltpu.VMEM((TOK, 768), BF16),
        ]
        + [DMA((2,))] * 4
        + [DMA((1,))] * 2
        + [DMA((4, bits))] * 2
        + [DMA((4,))],
        compiler_params=params(collective_id=2, has_side_effects=True),
        cost_estimate=cost(18, 30),
        name="unattend",
    )(
        place, pool, ext, ext, tab, hot, lse, gn, hid, cot, mo, mp, wo, wop, g2, gwr, gwe, gnb
    )


SMALL_ROWS = 64


def back_kernel(
    gp, gext, proj, pool, x, gh, w, taps, mtaps, gain, shift, fd, fp, gd, tw, ta,
    gwr_p, gwe_p, gwo, bp, gbe, gbr, pos, sums2,
    own_o, recv_o, sum_o, sump_o, br_o, red_o, small_o, gwr_o, gwe_o,
    h_s, c_s, zf_s, gw_a, gwb, normed_t, dense_s, rows_s, wcat, gm_s, back, z_s, peer_s, br_s,
    gwr_s, gwe_s, small_s, nsnd, nrcv,
    kq, kk, kv, ko, ks, rq, rk, rv, ro, rs, fin, fin_s,
    b_snd, b_rcv, n_snd, n_rcv, t_snd, t_rcv, f_snd, f_rcv,
    x_snd, x_rcv, s_snd, s_rcv, d_snd, d_rcv, o_sem,
):
    step = pl.program_id(0)
    me = lax.axis_index("tp")
    blk = lax.axis_index("blk")
    peers = lax.axis_size("blk")
    mine, theirs = half_lanes(me), half_lanes(1 - me)

    blocks = []
    for i in range(4):
        piece, out = (gwr_p, gwr_s) if i < 2 else (gwe_p, gwe_s)
        width = out.shape[1] // 2
        out = out.at[:, (i % 2) * width : (i % 2 + 1) * width]
        blocks.append(Gathering(Doubling(piece.at[i % 2], out, 3, f_snd.at[i], f_rcv.at[i])))

    def late(i, src, keep, rcv, out, levels=4):
        return Reduction(
            Halving(src, keep, rcv, s_snd.at[i], s_rcv.at[i], levels=levels),
            Doubling(None, out, levels - 1, d_snd.at[i], d_rcv.at[i]),
        )

    parts = [
        late(0, gwb.at[0], kq, rq, fin.at[0]),
        late(1, gwb.at[1], kk, rk, fin.at[1]),
        late(2, gwb.at[2], kv, rv, fin.at[2]),
    ]
    output = late(3, gwo, ko, ro, fin.at[3])
    small = late(4, small_s, ks, rs, fin_s, levels=3)

    def back_copy(j):
        return remote(
            gext.at[j], back.at[j], b_snd.at[j], b_rcv.at[j],
            blk=lax.rem(blk + peers - 1, peers),
        )

    def norm_copy(i):
        return remote(peer_s.at[i], recv_o.at[i], n_snd.at[i], n_rcv.at[i], tp=1 - me)

    def sum_copy():
        return remote(sum_o, sump_o, t_snd.at[0], t_rcv.at[0], tp=1 - me)

    def branch_copy():
        return remote(bp, br_s, x_snd.at[0], x_rcv.at[0], tp=1 - me)

    def last_copy():
        return remote(nsnd, nrcv, x_snd.at[1], x_rcv.at[1], tp=1 - me)

    outs = [
        pltpu.make_async_copy(gwr_s, gwr_o, o_sem.at[0]),
        pltpu.make_async_copy(gwe_s, gwe_o, o_sem.at[1]),
        pltpu.make_async_copy(br_s, br_o, o_sem.at[2]),
    ]

    @pl.when(step == 0)
    def _():
        meet(bits=range(blk_bits()), ring=True)
        for block in blocks:
            block.start()
        output.start()
        branch_copy().start()

    @pl.when((step == 0) & (blk > 0))
    def _():
        back_copy(0).start()
        back_copy(1).start()

    @pl.when(step == 0)
    def _():
        tap_spectra(tw, taps, h_s)
        rows_s[...] = jnp.zeros_like(rows_s)
        small_s[...] = jnp.zeros_like(small_s)
        for i in range(3):
            wcat[:, i * 384 : i * 384 + 384] = w[i]

        @pl.loop(0, 4)
        def _(c):
            gm_s[c] = gext[c + 2].astype(F32)
            cen, r = row_stats(x[c].astype(F32))
            normed = cen * r * as_row(gain) + as_row(shift)
            normed_t[c] = jnp.transpose(normed).astype(BF16)

    @pl.when((step == 1) & (blk < peers - 1))
    def _():
        for j in range(2):
            back_copy(j).wait_recv()
            gm_s[2 + j] += back[j].astype(F32)

    f0, f1, f2, f3 = blocks
    pq, pk, pv = parts
    plan = {
        (0, 3): [(output, 0)],
        (1, 1): [(f0, 0)],
        (1, 2): [(output, 1), (f1, 0)],
        (1, 3): [(f2, 0), (pq, 0)],
        (2, 0): [(f3, 0)],
        (2, 1): [(f0, 1), (output, 2)],
        (2, 2): [(f1, 1)],
        (2, 3): [(f2, 1), (pq, 1), (pk, 0)],
        (3, 0): [(output, 3), (f3, 1)],
        (3, 1): [(f0, 2)],
        (3, 2): [(f1, 2), (pq, 2), (pk, 1)],
        (3, 3): [(f2, 2), (pv, 0), (output, 4)],
    }

    def hook(s, c):
        for stream, k in plan.get((s, c), ()):
            stream.advance(k)

    def hooks_at(c, steps):
        for s, at in plan:
            if s in steps:
                pl.when((step == s) & (c == at))(functools.partial(hook, s, at))

    @pl.when(step < 3)
    def _():
        lanes = pl.ds(pl.multiple_of(step * 384, 128), 384)
        kind = jnp.maximum(step - 1, 0)
        mlanes = pl.ds(pl.multiple_of(kind * 384, 128), 384)
        has = jnp.where(step > 0, 1.0, 0.0)
        hr, hi = h_s[:FREQ, lanes], h_s[FREQ:, lanes]
        c_s[...] = jnp.zeros_like(c_s)
        gw_a[...] = jnp.zeros_like(gw_a)

        @pl.loop(0, 4)
        def _(c):
            hooks_at(c, (0, 1, 2))
            gm = (gm_s[c, :, mlanes] * has).reshape(2, 56, 384)
            frames = gp[c].astype(F32).reshape(CT, 56, 384)
            pooled = pool[c].astype(F32).reshape(CT, 56, 384)
            sums = []
            for u in range(KC):
                hit = gm[0] * pooled[u] + gm[1] * pooled[KC + u]
                small_s[28 + u : 29 + u, mlanes] += col_sum(hit)
            for t in range(CT):
                u = t % KC
                sums.append(frames[t] + gm[t // KC] * mtaps[kind, u : u + 1])
            grad = jnp.stack(sums, 0).reshape(PAD, 384).astype(BF16)
            gs = mm(fp[...], grad)
            ps = mm(fd[...], proj[c])
            zf_s[:FREQ] = (hr * gs[:FREQ] + hi * gs[FREQ:]).astype(BF16)
            zf_s[FREQ:] = (hr * gs[FREQ:] - hi * gs[:FREQ]).astype(BF16)
            c_s[:FREQ] += gs[:FREQ] * ps[:FREQ] + gs[FREQ:] * ps[FREQ:]
            c_s[FREQ:] += gs[:FREQ] * ps[FREQ:] - gs[FREQ:] * ps[:FREQ]
            dense = mm(gd[...], zf_s[...]).astype(BF16)
            dense_s[c, :, lanes] = dense
            small_s[27:28, lanes] += col_sum(dense.astype(F32))
            gw_a[...] += mm(normed_t[c], dense)

        gwb[step] = gw_a[...].astype(BF16)
        high, low = two_parts(c_s[...])
        small_s[:27, lanes] = (mm(ta[...], high) + mm(ta[...], low))[:27]

    for i in range(3):
        pl.when(step == i)(parts[i].start)

    @pl.when(step == 3)
    def _():
        small_s[56:] = sums2[...]

        @pl.loop(0, 4)
        def _(c):
            hooks_at(c, (3,))
            gn = mm_nt(dense_s[c], wcat[...])
            cen, r = row_stats(x[c].astype(F32))
            xhat = cen * r
            g = gn * as_row(gain)
            z_s[...] = r * g + jnp.where(lax.div(c, 2) == me, gh[lax.rem(c, 2)], 0.0)
            peer_s[c] = z_s[:, theirs].astype(BF16)
            norm_copy(c).start()
            own_o[c] = z_s[:, mine].astype(BF16)
            first_sum = jnp.sum(g, axis=-1, keepdims=True)
            second_sum = jnp.sum(g * xhat, axis=-1, keepdims=True)
            lane = iota((TOK, 128), 1)
            pair = jnp.where(lane == 0, first_sum, jnp.where(lane == 1, second_sum, 0.0))
            rows_s[:TOK] = pair
            sum_o[c] = jnp.transpose(rows_s[...])[:8]
            small_s[56:57, :768] += col_sum(gn * xhat)
            small_s[57:58, :768] += col_sum(gn)

        sum_copy().start()
        half = gbe.shape[1] // 2
        small_s[32:33, :half] = gbe[:, :half]
        small_s[33:34, :half] = gbe[:, half:]
        small_s[34:35, :384] = gbr[...]
        small_s[40:48, :128] = pos[...]
        small.start()

        done = {}
        for jobs in plan.values():
            for stream, k in jobs:
                done[id(stream)] = k + 1
        streams = [f3, output, pq, pk, pv, small, f0, f1, f2]
        left = [list(range(done.get(id(t), 0), t.count)) for t in streams]
        while any(left):
            for stream, todo in zip(streams, left):
                if todo:
                    stream.advance(todo.pop(0))
        for t in outs[:2]:
            t.start()
        nsnd[...] = fin_s[56:]
        last_copy().start()
        branch_copy().wait()
        outs[2].start()
        red_o[...] = fin[...]
        small_o[...] = fin_s[...]
        for i in range(4):
            norm_copy(i).wait()
        sum_copy().wait()
        last_copy().wait()
        small_o[56:] = nsnd[...] + nrcv[...]
        for t in outs:
            t.wait()

    @pl.when((step == 3) & (blk > 0))
    def _():
        back_copy(0).wait_send()
        back_copy(1).wait_send()


def back_call(
    gp, gext, proj, pool, x, gh, w, taps, mtaps, gain, shift, fd, fp, gd, tw, ta,
    gwr, gwe, gwo, bp, gbe, gbr, pos, sums2,
):
    ff = 2 * gwe.shape[2]
    bits = blk_bits()

    def third(rows):
        return pl.BlockSpec((4, rows, 384), lambda s: (0, 0, jnp.minimum(s, 2)))

    def stream(rows, cols, dtype, levels=4):
        keep = pltpu.VMEM((rows // 2, cols), dtype)
        return keep, pltpu.VMEM((slots(rows, bits, levels)[0], cols), dtype)

    kept, got = zip(*[stream(768, 384, BF16)] * 4 + [stream(SMALL_ROWS, 1152, F32, 3)])
    return pl.pallas_call(
        back_kernel,
        grid=(4,),
        in_specs=[third(PAD), whole((6, MROW, 768)), third(TOK), third(PAD)]
        + whole_like(x, gh, w, taps, mtaps, gain, shift, fd, fp, gd, tw, ta)
        + whole_like(gwr, gwe, gwo, bp, gbe, gbr, pos, sums2),
        out_specs=[
            whole((4, TOK, 384)),
            HBM,
            whole((4, 8, 512)),
            HBM,
            HBM,
            whole((4, 768, 384)),
            whole((SMALL_ROWS, 1152)),
            HBM,
            HBM,
        ],
        out_shape=[
            jax.ShapeDtypeStruct((4, TOK, 384), BF16),
            jax.ShapeDtypeStruct((4, TOK, 384), BF16),
            jax.ShapeDtypeStruct((4, 8, 512), F32),
            jax.ShapeDtypeStruct((4, 8, 512), F32),
            jax.ShapeDtypeStruct((4, TOK, 384), BF16),
            jax.ShapeDtypeStruct((4, 768, 384), BF16),
            jax.ShapeDtypeStruct((SMALL_ROWS, 1152), F32),
            jax.ShapeDtypeStruct((ff, 768), BF16),
            jax.ShapeDtypeStruct((768, ff), BF16),
        ],
        scratch_shapes=[
            pltpu.VMEM((2 * FREQ, 1152), F32),
            pltpu.VMEM((2 * FREQ, 384), F32),
            pltpu.VMEM((2 * FREQ, 384), BF16),
            pltpu.VMEM((768, 384), F32),
            pltpu.VMEM((3, 768, 384), BF16),
            pltpu.VMEM((4, 768, TOK), BF16),
            pltpu.VMEM((4, TOK, 1152), BF16),
            pltpu.VMEM((512, 128), F32),
            pltpu.VMEM((768, 1152), BF16),
            pltpu.VMEM((4, MROW, 768), F32),
            pltpu.VMEM((2, MROW, 768), BF16),
            pltpu.VMEM((TOK, 768), F32),
            pltpu.VMEM((4, TOK, 384), BF16),
            pltpu.VMEM((4, TOK, 384), BF16),
            pltpu.VMEM((ff, 768), BF16),
            pltpu.VMEM((768, ff), BF16),
            pltpu.VMEM((SMALL_ROWS, 1152), F32),
            pltpu.VMEM((8, 1152), F32),
            pltpu.VMEM((8, 1152), F32),
            *kept,
            *got,
            pltpu.VMEM((4, 768, 384), BF16),
            pltpu.VMEM((SMALL_ROWS, 1152), F32),
        ]
        + [DMA((2,))] * 2
        + [DMA((4,))] * 2
        + [DMA((1,))] * 2
        + [DMA((4, 4))] * 2
        + [DMA((2,))] * 2
        + [DMA((5, bits))] * 2
        + [DMA((5, 4))] * 2
        + [DMA((3,))],
        compiler_params=params(collective_id=3, has_side_effects=True),
        cost_estimate=cost(12, 25),
        name="back",
    )(
        gp, gext, proj, pool, x, gh, w, taps, mtaps, gain, shift, fd, fp, gd, tw, ta,
        gwr, gwe, gwo, bp, gbe, gbr, pos, sums2,
    )


def final_kernel(
    own, recv, sums, sums_p, x, gain, res, br, red, redl, redr, gwr, gwe, small,
    gin_o, out_o, gw_o, gwo_o, gwr_o, gwe_o, gt_o, gb_o, gmt_o, pos_o,
    gbo_o, gg1_o, gs1_o, gg2_o, gs2_o, gbe_o, gbr_o,
    xs, rows_s,
):
    me = lax.axis_index("tp")
    mine = half_lanes(me)
    rows_s[8:] = jnp.zeros((120, 512), F32)
    rows_s[:8] = (sums[0] + sums_p[0]) * (1.0 / 768)
    total = jnp.transpose(rows_s[...])[:TOK]
    cen, r = row_stats(x[0].astype(F32))
    xs[...] = cen * (r * r)
    z = own[0].astype(F32) + recv[0].astype(F32)
    gin_o[0] = z - r * total[:, 0:1] - xs[:, mine] * total[:, 1:2]
    out_o[0] = (res[0] + br[0].astype(F32)).astype(BF16)
    gw_o[...] = red[...].astype(F32)
    gwo_o[:, :384] = redl[0].astype(F32)
    gwo_o[:, 384:] = redr[0].astype(F32)
    gwr_o[...] = gwr[...].astype(F32)
    gwe_o[...] = gwe[...].astype(F32)

    @pl.when(pl.program_id(0) == 3)
    def _():
        for i in range(3):
            cols = slice(i * 384, i * 384 + 384)
            gt_o[i] = small[:27, cols]
            gb_o[i : i + 1] = small[27:28, cols]
            if i < 2:
                gmt_o[i] = small[28:32, cols]
        pos_o[...] = small[40:44, : NT + 2 * NHW]
        gbo_o[...] = small[60:61, mine].reshape(384)
        for row, ref in ((56, gg1_o), (57, gs1_o), (58, gg2_o), (59, gs2_o)):
            ref[...] = small[row : row + 1, :768].reshape(768)
        half = gbe_o.shape[0] // 2
        gbe_o[:half] = small[32:33, :half].reshape(half)
        gbe_o[half:] = small[33:34, :half].reshape(half)
        gbr_o[...] = small[34:35, :384].reshape(384)


def final_call(own, recv, sums, sums_p, x, gain, res, br, red, gwr, gwe, small):
    ff = gwe.shape[1]

    def flat(*shape):
        return jax.ShapeDtypeStruct(shape, F32)

    vectors = [(384,), (768,), (768,), (768,), (768,), (ff,), (384,)]
    tables = [(3, 27, 384), (3, 384), (2, KC, 384), (4, NT + 2 * NHW)]

    def rows(n, width):
        return pl.BlockSpec((n, width), lambda c: (c, 0))

    return pl.pallas_call(
        final_kernel,
        grid=(4,),
        in_specs=[
            per_clip(TOK, 384),
            per_clip(TOK, 384),
            per_clip(8, 512),
            per_clip(8, 512),
            per_clip(TOK, 768),
            whole((768,)),
            per_clip(TOK, 384),
            per_clip(TOK, 384),
            pl.BlockSpec((3, 192, 384), lambda c: (0, c, 0)),
            pl.BlockSpec((1, 96, 384), lambda c: (3, c, 0)),
            pl.BlockSpec((1, 96, 384), lambda c: (3, c + 4, 0)),
            rows(ff // 4, 768),
            rows(192, ff),
            whole((64, 1152)),
        ],
        out_specs=[
            per_clip(TOK, 384),
            per_clip(TOK, 384),
            pl.BlockSpec((3, 192, 384), lambda c: (0, c, 0)),
            rows(96, 768),
            rows(ff // 4, 768),
            rows(192, ff),
        ]
        + [whole(s) for s in tables + vectors],
        out_shape=[
            flat(4, TOK, 384),
            jax.ShapeDtypeStruct((4, TOK, 384), BF16),
            flat(3, 768, 384),
            flat(384, 768),
            flat(ff, 768),
            flat(768, ff),
        ]
        + [flat(*s) for s in tables + vectors],
        scratch_shapes=[pltpu.VMEM((TOK, 768), F32), pltpu.VMEM((128, 512), F32)],
        compiler_params=params(),
        cost_estimate=cost(0.1, 40),
        name="final",
    )(own, recv, sums, sums_p, x, gain, res, br, red, red, red, gwr, gwe, small)


def local(
    layer_input,
    first_gain,
    first_shift,
    project_weight,
    project_bias,
    pool_taps,
    memory_taps,
    position_bias,
    output_weight,
    output_bias,
    second_gain,
    second_shift,
    expand_weight,
    expand_bias,
    reduce_weight,
    reduce_bias,
    cotangent,
    clip_place,
):
    clips = layer_input.shape[0] // TOK
    half = layer_input.shape[1]

    def clipwise(a):
        return a.reshape(clips, TOK, a.shape[-1])

    w = jnp.transpose(project_weight, (1, 0, 2))
    hot = jnp.asarray(table_onehot())
    fd, fp, gd, gpad, tw, ta = fourier_tables()
    (
        pool, proj, x, ext, lse, wop, tab, mo, mp, hid, cot, gn, res, bpeer,
        gwr, gwe, gbe, gbr, gnb,
    ) = front_call(
        clip_place, position_bias, clipwise(layer_input), clipwise(cotangent),
        output_weight, output_bias, first_gain, first_shift, w, project_bias, pool_taps,
        memory_taps, hot, fd, gpad, tw, second_gain, second_shift, expand_weight, expand_bias,
        reduce_weight, reduce_bias,
    )
    gp, gext, gh, gwo, sums2, pos, gwr, gwe = unattend_call(
        clip_place, pool, ext, tab, hot, lse, gn, hid, cot, mo, mp, output_weight, wop,
        second_gain, gwr, gwe, gnb,
    )
    own, recv, sums, sums_p, br, red, small, gwr, gwe = back_call(
        gp, gext, proj, pool, x, gh, w, pool_taps, memory_taps, first_gain, first_shift,
        fd, fp, gd, tw, ta, gwr, gwe, gwo, bpeer, gbe, gbr, pos, sums2,
    )
    (
        gin, result, gw, gwo, gwr, gwe, gt, gb, gmt, pos, gbo, gg1, gs1, gg2, gs2, gbe, gbr
    ) = final_call(own, recv, sums, sums_p, x, first_gain, res, br, red, gwr, gwe, small)
    return (
        result.reshape(clips * TOK, half),
        gin.reshape(clips * TOK, half),
        gg1,
        gs1,
        jnp.transpose(gw, (1, 0, 2)),
        gb,
        gt,
        gmt,
        pos,
        gwo,
        gbo,
        gg2,
        gs2,
        gwe,
        gbe,
        gwr,
        gbr,
    )


def solution(mesh):
    return jax.shard_map(
        local,
        mesh=mesh,
        in_specs=(
            P("blk", "tp"),
            P(),
            P(),
            P(None, None, "tp"),
            P(None, "tp"),
            P(None, None, "tp"),
            P(None, None, "tp"),
            P("tp", None),
            P("tp", None),
            P("tp"),
            P(),
            P(),
            P(None, "tp"),
            P("tp"),
            P("tp", None),
            P("tp"),
            P("blk", "tp"),
            P("blk"),
        ),
        out_specs=(
            P("blk", "tp"),
            P("blk", "tp"),
            P(),
            P(),
            P(None, None, "tp"),
            P(None, "tp"),
            P(None, None, "tp"),
            P(None, None, "tp"),
            P("tp", None),
            P("tp", None),
            P("tp"),
            P(),
            P(),
            P(None, "tp"),
            P("tp"),
            P("tp", None),
            P("tp"),
        ),
        check_vma=False,
    )
```
